256 devices in a mesh: pts: 4 (over x_hi, core), ctr: 64 (over z, x_lo, y).
Axes of the slice: x: 4 (x_hi: 2, x_lo: 2; x = x_hi * 2 + x_lo), y: 4, z: 8, core: 2. Of those that a mesh axis runs over, the one named last changes fastest.
Arguments:
- points: bfloat16 [32768, 128], P('pts'), may hold values from -16 to 16, as said below
- centers: bfloat16 [131072, 128], P('ctr'), may hold values from -16 to 16, as said below
- panel_inverse: bfloat16 [512, 512], P('pts'), as said below
- direction: float32 [32, 131072], P(None, 'ctr'), as said below
- residual: float32 [32, 131072], P(None, 'ctr'), as said below
Outputs:
- panel_rows: bfloat16 [131072, 512], P('ctr', 'pts')
- operator_image: float32 [32, 131072], P(None, 'ctr')
- new_residual: float32 [32, 131072], P(None, 'ctr')
The draws below stay inside these ranges and needn't reach their ends.
Inputs may be any that keep to these rules, and one draw needn't show every extreme that they name: `points`: rows of 128 real features. `centers`: rows of 128 real features. panel_inverse is lower triangular with a positive diagonal. `direction`: finite real values. `residual`: finite real values.
All inputs are finite; a program needn't handle non-finite values.
Results may differ from the reference program's by a relative error of at most 0.001.
The reference program's roundings to bfloat16 on the way count: a program that leaves them out, or rounds other values in their place, can miss the bound.
Values may be sent and summed in bfloat16 or wider, within the bound.
No kernel may reach another device: no remote copies, remote signals or barrier semaphores. Data moves between devices by JAX's collectives and lax.ppermute only.
A program may use at most 128 MiB of HBM per device.

```python
import math
import jax
import jax.numpy as jnp
from jax import lax

D = 128
PANEL = 512
R = 32
M = 131072
NPOINTS = 32768


cluster_members = 64


def cluster_layout(key):
    group_count = M // cluster_members
    key_one, key_two = jax.random.split(jax.random.fold_in(key, 59))
    center_groups = (jax.random.permutation(key_one, M) // cluster_members).astype(jnp.int32)
    point_groups = jax.random.randint(key_two, (NPOINTS,), 0, group_count, dtype=jnp.int32)
    return (center_groups, point_groups)


def rising_values(key, salt_value, scale_value, coherent):
    key_one = jax.random.fold_in(jax.random.fold_in(key, salt_value), 0)
    key_two = jax.random.fold_in(jax.random.fold_in(key, salt_value), 1)
    key_four = jax.random.fold_in(jax.random.fold_in(key, salt_value), 3)
    position = jnp.arange(M, dtype=jnp.float32) / M
    rise_factor = jnp.exp(jnp.log(3.0) * position)[None, :]
    row_spread = jnp.exp(jax.random.uniform(key_four, (R, 1), jnp.float32) * jnp.log(10.0))
    base_draw = jnp.clip(jax.random.normal(key_one, (R, M), jnp.float32), -4.0, 4.0)
    spread = jnp.exp(jax.random.uniform(key_two, (1, M), jnp.float32) * jnp.log(10.0))
    values = base_draw * spread
    return scale_value * (values + coherent) * rise_factor * row_spread


def scattered_rows(key, salt_value, groups, row_count):
    group_count = M // cluster_members
    key_mean = jax.random.fold_in(key, 71)
    key_one = jax.random.fold_in(key, salt_value)
    means = 3.5 * jnp.clip(jax.random.normal(key_mean, (group_count, D), jnp.float32), -4.0, 4.0)
    jitter = 0.6 * jnp.clip(jax.random.normal(key_one, (row_count, D), jnp.float32), -4.0, 4.0)
    scattered = means[groups] + jitter
    return jnp.clip(scattered, -16.0, 16.0).astype(jnp.bfloat16)


def draw_points(key, part):
    center_groups, point_groups = cluster_layout(key)
    return scattered_rows(key, 83, point_groups, NPOINTS)


def draw_centers(key, part):
    center_groups, point_groups = cluster_layout(key)
    return scattered_rows(key, 97, center_groups, M)


def draw_direction(key, part):
    center_groups, point_groups = cluster_layout(key)
    group_count = M // cluster_members
    key_group = jax.random.fold_in(key, 13)
    group_part = 4.0 * jnp.clip(jax.random.normal(key_group, (R, group_count), jnp.float32), -3.0, 3.0)
    coherent = group_part[:, center_groups]
    return rising_values(key, 11, 2.0, coherent)


def draw_residual(key, part):
    return rising_values(key, 23, 0.1, jnp.zeros((R, M), jnp.float32))


def draw_panel_inverse(key, part):
    key_one, key_two = jax.random.split(jax.random.fold_in(key, 37))
    scale = 1.0 / (3.0 * jnp.sqrt(PANEL / 2.0))
    lower = jnp.clip(jax.random.normal(key_one, (PANEL, PANEL), jnp.float32), -4.0, 4.0)
    diagonal = jnp.exp(jax.random.uniform(key_two, (PANEL,), jnp.float32) * jnp.log(3.0))
    matrix = jnp.tril(lower, -1) + jnp.diag(diagonal)
    return (matrix * scale).astype(jnp.bfloat16)


def setup_inputs(seed: int = 0) -> dict:
    key_of = jax.random.split(jax.random.key(seed), 6)
    points = draw_points(jax.random.fold_in(key_of[5], 71), 0)
    centers = draw_centers(jax.random.fold_in(key_of[5], 71), 0)
    panel_inverse = draw_panel_inverse(jax.random.fold_in(key_of[5], 71), 0)
    direction = draw_direction(jax.random.fold_in(key_of[5], 71), 0)
    residual = draw_residual(jax.random.fold_in(key_of[5], 71), 0)
    return dict(points=points, centers=centers, panel_inverse=panel_inverse, direction=direction, residual=residual)


RIDGE_TERM = 0.002

def similarity(left, right):
    inner_terms = jnp.dot(left, right.T, preferred_element_type=jnp.float32)
    left_sq = lax.optimization_barrier(jnp.sum(jnp.square(left.astype(jnp.float32)), axis=1))
    right_sq = lax.optimization_barrier(jnp.sum(jnp.square(right.astype(jnp.float32)), axis=1))
    feature_count = left.shape[1]
    return jnp.exp(-(left_sq[:, None] + right_sq[None, :] - 2.0 * inner_terms) / (2.0 * feature_count))

def reference(points, centers, panel_inverse, direction, residual):
    head_rows = centers[:PANEL]
    head_vals = direction[:, :PANEL].astype(jnp.bfloat16)
    z1_full = jnp.dot(head_vals, panel_inverse.T, preferred_element_type=jnp.float32).astype(jnp.bfloat16)
    q_sum = jnp.dot(z1_full, panel_inverse, preferred_element_type=jnp.float32)
    q_bf16 = q_sum.astype(jnp.bfloat16)
    k_panel = similarity(centers, head_rows).astype(jnp.bfloat16)
    panel_rows = jnp.dot(k_panel, panel_inverse.T, preferred_element_type=jnp.float32).astype(jnp.bfloat16)
    correction = jnp.dot(q_bf16, k_panel.T, preferred_element_type=jnp.float32)
    columns = jnp.arange(M, dtype=jnp.int32)
    padded = jnp.concatenate([z1_full.astype(jnp.float32), jnp.zeros((R, M - PANEL), jnp.float32)], axis=1)
    z_vector = jnp.where(columns[None, :] < PANEL, padded, direction - correction)
    z_bf16 = z_vector.astype(jnp.bfloat16)
    block_rows = min(512, NPOINTS)
    w_scale = 1.0 / (2.0 * math.sqrt(M))
    image_scale = 1.0 / (2.0 * math.sqrt(NPOINTS))

    def accumulate(total, point_rows):
        kernel_rows = similarity(point_rows, centers).astype(jnp.bfloat16)
        w_full = jnp.dot(z_bf16, kernel_rows.T, preferred_element_type=jnp.float32) * w_scale
        w_bf16 = w_full.astype(jnp.bfloat16)
        return (total + jnp.dot(w_bf16, kernel_rows, preferred_element_type=jnp.float32), None)
    center_terms, unused = lax.scan(accumulate, jnp.zeros((R, M), jnp.float32), points.reshape(NPOINTS // block_rows, block_rows, D))
    operator_image = center_terms * image_scale + RIDGE_TERM * z_vector
    curvature = lax.optimization_barrier(jnp.sum(z_vector * operator_image, axis=1))
    r_squares = lax.optimization_barrier(jnp.sum(residual * residual, axis=1))
    new_residual = residual - (r_squares / curvature)[:, None] * operator_image
    return (panel_rows, operator_image, new_residual)
```

```python
import functools
import math

import jax
import jax.numpy as jnp
from jax import lax
from jax.experimental import pallas as pl
from jax.experimental.pallas import tpu as pltpu
from jax.sharding import Mesh
from jax.sharding import PartitionSpec as P

CTR = ("ctr_0", "ctr_1", "ctr_2")
NEAR = ("ctr_1", "ctr_2")
FAR = "ctr_0"
RIDGE_TERM = 0.002

bf16, f32 = jnp.bfloat16, jnp.float32
LAST = (((1,), (1,)), ((), ()))
VMEM = pl.BlockSpec(memory_space=pltpu.VMEM)
SMEM = pl.BlockSpec(memory_space=pltpu.SMEM)
LIMIT = 12 << 20


def widened(x, side):
    xf = x.astype(f32)
    n = jnp.sum(xf * xf, axis=1, keepdims=True)
    high = n.astype(bf16).astype(f32)
    rest = n - high
    mid = rest.astype(bf16).astype(f32)
    low = rest - mid
    lane = lax.broadcasted_iota(jnp.int32, x.shape, 1)
    if side == 0:
        extra = jnp.where(lane < 6, 1.0, 0.0)
        extra = jnp.where(lane == 0, high, extra)
        extra = jnp.where(lane == 1, mid, extra)
        extra = jnp.where(lane == 2, low, extra)
        return jnp.concatenate([x, extra.astype(bf16)], axis=1)
    extra = jnp.where(lane < 3, -1.0, 0.0)
    extra = jnp.where(lane == 3, -high, extra)
    extra = jnp.where(lane == 4, -mid, extra)
    extra = jnp.where(lane == 5, -low, extra)
    return jnp.concatenate([(xf * 2.0).astype(bf16), extra.astype(bf16)], axis=1)


def similar(a, b, features):
    t = lax.dot_general(a, b, LAST, preferred_element_type=f32)
    return jnp.exp2(t * (math.log2(math.e) / (2 * features))).astype(bf16)


def block_kernel(tile, cols, left_ref, right_ref, out_ref, wide):
    features = left_ref.shape[1]
    wide[...] = widened(right_ref[...], 1)

    def step(i, carry):
        rows = pl.ds(pl.multiple_of(i * tile, tile), tile)
        left = widened(left_ref[rows], 0)
        for j in range(wide.shape[0] // cols):
            out_ref[rows, j * cols : (j + 1) * cols] = similar(
                left, wide[j * cols : (j + 1) * cols], features
            )
        return carry

    lax.fori_loop(0, left_ref.shape[0] // tile, step, 0)


def kernel_block(left, right, name, tile=1024, cols=256):
    rows, features = left.shape
    columns = right.shape[0]
    return pl.pallas_call(
        functools.partial(block_kernel, tile, cols),
        out_shape=jax.ShapeDtypeStruct((rows, columns), bf16),
        in_specs=[VMEM, VMEM],
        out_specs=VMEM,
        scratch_shapes=[pltpu.VMEM((columns, 2 * features), bf16)],
        compiler_params=pltpu.CompilerParams(vmem_limit_bytes=LIMIT),
        cost_estimate=pl.CostEstimate(
            flops=4 * rows * columns * features,
            bytes_accessed=2 * rows * columns,
            transcendentals=rows * columns,
        ),
        name=name,
    )(left, right)


def panel_kernel(flag_ref, centers_ref, head_ref, pinv_ref, dir_ref, z_ref, zz_ref, kp_ref):
    panel = pinv_ref.shape[0]
    outputs = dir_ref.shape[0]
    features = centers_ref.shape[1]
    vals = jnp.concatenate(
        [head_ref[pl.ds(panel + b * outputs, outputs)] for b in range(panel // features)], axis=1
    )
    z1 = lax.dot_general(vals, pinv_ref[...], LAST, preferred_element_type=f32).astype(bf16)
    q = jnp.dot(z1, pinv_ref[...], preferred_element_type=f32).astype(bf16)
    heads = widened(head_ref[:panel], 1)
    tile = panel
    for i in range(centers_ref.shape[0] // tile):
        rows = slice(i * tile, (i + 1) * tile)
        kp = similar(widened(centers_ref[rows], 0), heads, features)
        kp_ref[rows] = kp
        z = dir_ref[:, rows] - lax.dot_general(q, kp, LAST, preferred_element_type=f32)
        if i == 0:
            z = jnp.where(flag_ref[0] == 0, z1.astype(f32), z)
        z_ref[:, rows] = z
        high = z.astype(bf16)
        zz_ref[:outputs, rows] = high
        zz_ref[outputs:, rows] = (z - high.astype(f32)).astype(bf16)


def panel_step(flag, centers, head, pinv, direction):
    outputs, m_dev = direction.shape
    panel = pinv.shape[0]
    return pl.pallas_call(
        panel_kernel,
        out_shape=(
            jax.ShapeDtypeStruct((outputs, m_dev), f32),
            jax.ShapeDtypeStruct((2 * outputs, m_dev), bf16),
            jax.ShapeDtypeStruct((m_dev, panel), bf16),
        ),
        in_specs=[SMEM, VMEM, VMEM, VMEM, VMEM],
        out_specs=(VMEM, VMEM, VMEM),
        compiler_params=pltpu.CompilerParams(vmem_limit_bytes=LIMIT),
        cost_estimate=pl.CostEstimate(
            flops=6 * m_dev * panel * 128, bytes_accessed=4 << 20, transcendentals=m_dev * panel
        ),
        name="panel",
    )(flag, centers, head, pinv, direction)


def values_kernel(tile, zz_ref, *refs):
    blocks, (high_ref, both_ref) = refs[:-2], refs[-2:]
    outputs = high_ref.shape[1]
    done = 0
    for k_ref in blocks:
        for i in range(k_ref.shape[1] // tile):
            u = jnp.dot(zz_ref[...], k_ref[:, i * tile : (i + 1) * tile], preferred_element_type=f32)
            for b in range(tile // 128):
                part = u[:, b * 128 : (b + 1) * 128]
                high_ref[done] = part[:outputs]
                both_ref[done] = part[:outputs] + part[outputs:]
                done += 1


def values(zz, blocks, tile=512):
    outputs = zz.shape[0] // 2
    count = sum(k.shape[1] for k in blocks) // 128
    shape = jax.ShapeDtypeStruct((count, outputs, 128), f32)
    return pl.pallas_call(
        functools.partial(values_kernel, tile),
        out_shape=(shape, shape),
        in_specs=[VMEM] * (1 + len(blocks)),
        out_specs=(VMEM, VMEM),
        compiler_params=pltpu.CompilerParams(vmem_limit_bytes=LIMIT),
        cost_estimate=pl.CostEstimate(
            flops=2 * 256 * zz.shape[1] * count * 128,
            bytes_accessed=2 * zz.shape[1] * count * 128,
            transcendentals=0,
        ),
        name="values",
    )(zz, *blocks)


def image_kernel(tile, core_ref, w_ref, *refs):
    blocks, (keep_ref, send_ref, total) = refs[:-3], refs[-3:]
    per = tile // 128
    total[...] = jnp.zeros_like(total)
    done = 0
    for k_ref in blocks:

        def step(i, carry, k_ref=k_ref, done=done):
            w = jnp.concatenate([w_ref[done + i * per + b] for b in range(per)], axis=1)
            rows = pl.ds(pl.multiple_of(i * tile, tile), tile)
            total[...] += jnp.dot(w, k_ref[rows], preferred_element_type=f32)
            return carry

        lax.fori_loop(0, k_ref.shape[0] // tile, step, 0)
        done += k_ref.shape[0] // 128
    half = keep_ref.shape[0]
    mine = pl.multiple_of(core_ref[0] * half, half)
    keep_ref[...] = total[pl.ds(mine, half)]
    send_ref[...] = total[pl.ds(half - mine, half)]


def image(core, w, blocks, tile=1024):
    outputs = w.shape[1]
    m_dev = blocks[0].shape[1]
    points = sum(k.shape[0] for k in blocks)
    shape = jax.ShapeDtypeStruct((outputs // 2, m_dev), f32)
    return pl.pallas_call(
        functools.partial(image_kernel, tile),
        out_shape=(shape, shape),
        in_specs=[SMEM] + [VMEM] * (1 + len(blocks)),
        out_specs=(VMEM, VMEM),
        scratch_shapes=[pltpu.VMEM((outputs, m_dev), f32)],
        compiler_params=pltpu.CompilerParams(vmem_limit_bytes=LIMIT),
        cost_estimate=pl.CostEstimate(
            flops=2 * 256 * points * m_dev, bytes_accessed=2 * points * m_dev, transcendentals=0
        ),
        name="image",
    )(core, w, *blocks)


def exchange(x, axis):
    return lax.all_to_all(x, axis, 0, 0, tiled=True)


def copies(x, axis):
    n = lax.axis_size(axis)
    return exchange(jnp.broadcast_to(x[None], (n, *x.shape)), axis)


def swap(x, bit):
    n = lax.axis_size("pts")
    return lax.ppermute(x, "pts", [(i, i ^ bit) for i in range(n)])


def joined(first, mine, other):
    return jnp.where(
        first, jnp.concatenate([mine, other], axis=0), jnp.concatenate([other, mine], axis=0)
    )


def shards(points, centers, panel_inverse, direction, residual):
    n_ctr = lax.axis_size(CTR)
    n_near = lax.axis_size(NEAR)
    n_far = lax.axis_size(FAR)
    n_pts = lax.axis_size("pts")
    ctr_index = lax.axis_index(CTR)
    pts_index = lax.axis_index("pts")
    core = pts_index & 1
    m_dev, features = centers.shape
    npg = points.shape[0]
    panel = panel_inverse.shape[1]
    outputs = direction.shape[0]
    w_scale = 1.0 / (2.0 * math.sqrt(m_dev * n_ctr))
    image_scale = 1.0 / (2.0 * math.sqrt(npg * n_pts))

    vals = direction[:, :panel].astype(bf16)
    vals = jnp.moveaxis(vals.reshape(outputs, panel // features, features), 1, 0)
    head = jnp.concatenate([centers[:panel], vals.reshape(-1, features)], axis=0)
    piece = exchange(head.reshape(n_near, -1, features), NEAR)[0]
    piece = copies(piece, FAR)[0]
    head = copies(piece, NEAR).reshape(-1, features)

    pair = joined(core == 0, panel_inverse, swap(panel_inverse, 1))
    pinv = joined(pts_index < 2, pair, swap(pair, 2))

    halves = [points[: npg // 2], points[npg // 2 :]]
    by_center = [kernel_block(centers, h, f"by_center_{i}") for i, h in enumerate(halves)]

    z, zz, k_panel = panel_step(ctr_index.reshape(1), centers, head, pinv, direction)
    high, both = values(zz, by_center)

    parts = exchange(high.reshape(n_near, n_far * outputs, 128), NEAR)
    parts = jnp.sum(parts, axis=0)
    parts = exchange(parts.reshape(n_far, outputs, 128), FAR)
    owned = (jnp.sum(parts, axis=0) * w_scale).astype(bf16)
    w = copies(owned, FAR)
    w = copies(w.reshape(n_far * outputs, 128), NEAR).reshape(-1, outputs, 128)

    by_point = [kernel_block(h, centers, f"by_point_{i}") for i, h in enumerate(halves)]
    panel_rows = lax.dot_general(
        k_panel, panel_inverse, LAST, preferred_element_type=f32
    ).astype(bf16)

    mine = jnp.sum(w.astype(f32) * both, axis=(0, 2)) * image_scale
    mine = mine + (RIDGE_TERM / n_pts) * jnp.sum(z * z, axis=1)
    squares = jnp.sum(residual * residual, axis=1) * (1.0 / n_pts)
    scalars = jnp.concatenate([mine, squares])[None]
    scalars = scalars + swap(scalars, 1)
    scalars = scalars + swap(scalars, 2)
    scalars = jnp.sum(copies(scalars, CTR), axis=(0, 1))
    curvature, r_squares = scalars[:outputs], scalars[outputs:]

    keep, send = image(core.reshape(1), w, by_point)
    keep = keep + swap(send, 1)
    keep = keep + swap(keep, 2)
    total = joined(core == 0, keep, swap(keep, 1))
    operator_image = total * image_scale + RIDGE_TERM * z
    new_residual = residual - (r_squares / curvature)[:, None] * operator_image
    return (panel_rows, operator_image, new_residual)


def solution(mesh):
    split = Mesh(
        mesh.devices.reshape(mesh.shape["pts"], 8, 2, 4), ("pts", "ctr_0", "ctr_1", "ctr_2")
    )
    placed = (P("pts", None), P(CTR, None), P("pts", None), P(None, CTR), P(None, CTR))
    return jax.shard_map(
        shards,
        mesh=split,
        in_specs=placed,
        out_specs=(P(CTR, "pts"), P(None, CTR), P(None, CTR)),
        check_vma=False,
    )
```

```python
import functools
import math

import jax
import jax.numpy as jnp
from jax import lax
from jax.experimental import pallas as pl
from jax.experimental.pallas import tpu as pltpu
from jax.sharding import Mesh
from jax.sharding import PartitionSpec as P

CTR = ("ctr_0", "ctr_1", "ctr_2")
NEAR = ("ctr_1", "ctr_2")
FAR = "ctr_0"
RIDGE_TERM = 0.002

bf16, f32 = jnp.bfloat16, jnp.float32
LAST = (((1,), (1,)), ((), ()))
VMEM = pl.BlockSpec(memory_space=pltpu.VMEM)
SMEM = pl.BlockSpec(memory_space=pltpu.SMEM)
ANY = pl.BlockSpec(memory_space=pl.ANY)
TOKEN = jax.ShapeDtypeStruct((8, 128), jnp.float32)
LIMIT = 12 << 20


def widened(x, side):
    xf = x.astype(f32)
    n = jnp.sum(xf * xf, axis=1, keepdims=True)
    high = n.astype(bf16).astype(f32)
    rest = n - high
    mid = rest.astype(bf16).astype(f32)
    low = rest - mid
    lane = lax.broadcasted_iota(jnp.int32, x.shape, 1)
    if side == 0:
        extra = jnp.where(lane < 6, 1.0, 0.0)
        extra = jnp.where(lane == 0, high, extra)
        extra = jnp.where(lane == 1, mid, extra)
        extra = jnp.where(lane == 2, low, extra)
        return jnp.concatenate([x, extra.astype(bf16)], axis=1)
    extra = jnp.where(lane < 3, -1.0, 0.0)
    extra = jnp.where(lane == 3, -high, extra)
    extra = jnp.where(lane == 4, -mid, extra)
    extra = jnp.where(lane == 5, -low, extra)
    return jnp.concatenate([(xf * 2.0).astype(bf16), extra.astype(bf16)], axis=1)


def similar(a, b, features):
    t = lax.dot_general(a, b, LAST, preferred_element_type=f32)
    return jnp.exp2(t * (math.log2(math.e) / (2 * features))).astype(bf16)


def by_center_kernel(cols, centers_ref, points_ref, out_ref, token_ref, wide):
    features = centers_ref.shape[1]

    @pl.when(pl.program_id(0) == 0)
    def _():
        wide[...] = widened(centers_ref[...], 0)
        token_ref[...] = jnp.zeros_like(token_ref)

    right = widened(points_ref[...], 1)
    for j in range(right.shape[0] // cols):
        cut = slice(j * cols, (j + 1) * cols)
        out_ref[0, :, cut] = similar(wide[...], right[cut], features)


def by_point_kernel(cols, tie_ref, points_ref, centers_ref, out_ref, token_ref, wide):
    features = centers_ref.shape[1]

    @pl.when(pl.program_id(0) == 0)
    def _():
        wide[...] = widened(centers_ref[...], 1)
        token_ref[...] = jnp.zeros_like(token_ref)

    left = widened(points_ref[...], 0)
    for j in range(wide.shape[0] // cols):
        cut = slice(j * cols, (j + 1) * cols)
        out_ref[0, :, cut] = similar(left, wide[cut], features)


def block_cost(rows, columns, features):
    return pl.CostEstimate(
        flops=4 * rows * columns * features,
        bytes_accessed=2 * rows * columns,
        transcendentals=rows * columns,
    )


def by_center_block(centers, points, part, parts, chunk=512, cols=256):
    m_dev, features = centers.shape
    count = points.shape[0] // parts // chunk
    return pl.pallas_call(
        functools.partial(by_center_kernel, cols),
        out_shape=(jax.ShapeDtypeStruct((count, m_dev, chunk), bf16), TOKEN),
        grid=(count,),
        in_specs=[
            pl.BlockSpec((m_dev, features), lambda i: (0, 0)),
            pl.BlockSpec((chunk, features), lambda i: (part * count + i, 0)),
        ],
        out_specs=(
            pl.BlockSpec((1, m_dev, chunk), lambda i: (i, 0, 0)),
            pl.BlockSpec(TOKEN.shape, lambda i: (0, 0)),
        ),
        scratch_shapes=[pltpu.VMEM((m_dev, 2 * features), bf16)],
        compiler_params=pltpu.CompilerParams(vmem_limit_bytes=60 << 20),
        cost_estimate=block_cost(m_dev, count * chunk, features),
        name=f"by_center_{part}",
    )(centers, points)


def by_point_block(tie, points, centers, part, parts, chunk=1024, cols=256):
    m_dev, features = centers.shape
    count = points.shape[0] // parts // chunk
    return pl.pallas_call(
        functools.partial(by_point_kernel, cols),
        out_shape=(jax.ShapeDtypeStruct((count, chunk, m_dev), bf16), TOKEN),
        grid=(count,),
        in_specs=[
            ANY,
            pl.BlockSpec((chunk, features), lambda i: (part * count + i, 0)),
            pl.BlockSpec((m_dev, features), lambda i: (0, 0)),
        ],
        out_specs=(
            pl.BlockSpec((1, chunk, m_dev), lambda i: (i, 0, 0)),
            pl.BlockSpec(TOKEN.shape, lambda i: (0, 0)),
        ),
        scratch_shapes=[pltpu.VMEM((m_dev, 2 * features), bf16)],
        compiler_params=pltpu.CompilerParams(vmem_limit_bytes=60 << 20),
        cost_estimate=block_cost(m_dev, count * chunk, features),
        name=f"by_point_{part}",
    )(tie, points, centers)


def head_kernel(flags_ref, centers_ref, dir_ref, out_ref, rows_ref, vals_ref, sems):
    panel, features = rows_ref.shape
    outputs = vals_ref.shape[0]
    first = pltpu.make_async_copy(centers_ref.at[pl.ds(0, panel)], rows_ref, sems.at[0])
    second = pltpu.make_async_copy(dir_ref.at[:, pl.ds(0, panel)], vals_ref, sems.at[1])
    first.start()
    second.start()
    first.wait()
    second.wait()
    per = out_ref.shape[1] // 16
    for g in range(out_ref.shape[0] * per):
        row = 16 * g
        if row < panel:
            x = rows_ref[row : row + 16]
        else:
            b, r = divmod(row - panel, outputs)
            x = vals_ref[r : r + 16, b * features : (b + 1) * features].astype(bf16)
        out_ref[g // per, (g % per) * 16 : (g % per + 1) * 16] = x


def head_payload(flags, centers, direction, panel, ways):
    outputs, features = direction.shape[0], centers.shape[1]
    rows = panel + outputs * panel // features
    return pl.pallas_call(
        head_kernel,
        out_shape=jax.ShapeDtypeStruct((ways, rows // ways, features), bf16),
        in_specs=[SMEM, ANY, ANY],
        out_specs=VMEM,
        scratch_shapes=[
            pltpu.VMEM((panel, features), bf16),
            pltpu.VMEM((outputs, panel), f32),
            pltpu.SemaphoreType.DMA((2,)),
        ],
        compiler_params=pltpu.CompilerParams(vmem_limit_bytes=60 << 20),
        name="head",
    )(flags, centers, direction)


def spread_kernel(x_ref, *refs):
    out_ref = refs[-1]
    x = x_ref[0] if len(x_ref.shape) == len(out_ref.shape) else x_ref[...]
    for i in range(out_ref.shape[0]):
        out_ref[i] = x


def spread(x, ways, ties=()):
    shape = x.shape[1:] if len(x.shape) == 3 else x.shape
    return pl.pallas_call(
        spread_kernel,
        out_shape=jax.ShapeDtypeStruct((ways, *shape), x.dtype),
        in_specs=[VMEM] + [ANY] * len(ties),
        out_specs=VMEM,
        compiler_params=pltpu.CompilerParams(vmem_limit_bytes=LIMIT),
        name="spread",
    )(x, *ties)


def sum_kernel(x_ref, out_ref):
    total = x_ref[0]
    for i in range(1, x_ref.shape[0]):
        total = total + x_ref[i]
    out_ref[...] = total


def summed(x):
    return pl.pallas_call(
        sum_kernel,
        out_shape=jax.ShapeDtypeStruct(x.shape[1:], x.dtype),
        in_specs=[VMEM],
        out_specs=VMEM,
        compiler_params=pltpu.CompilerParams(vmem_limit_bytes=LIMIT),
        name="summed",
    )(x)


def owned_kernel(scale, x_ref, *refs):
    out_ref = refs[-1]
    total = x_ref[0]
    for i in range(1, x_ref.shape[0]):
        total = total + x_ref[i]
    total = (total * scale).astype(bf16)
    for i in range(out_ref.shape[0]):
        out_ref[i] = total


def owned_copies(x, scale, ways, ties=()):
    return pl.pallas_call(
        functools.partial(owned_kernel, scale),
        out_shape=jax.ShapeDtypeStruct((ways, *x.shape[1:]), bf16),
        in_specs=[VMEM] + [ANY] * len(ties),
        out_specs=VMEM,
        compiler_params=pltpu.CompilerParams(vmem_limit_bytes=LIMIT),
        name="owned",
    )(x, *ties)


def chunk_copies(sources, buffer, sems):
    copies, at = [], 0
    for source in sources:
        for i in range(source.shape[0]):
            copies.append(pltpu.make_async_copy(source.at[i], buffer.at[at], sems.at[at]))
            at += 1
    return copies


def panel_kernel(
    parts, flags_ref, centers_ref, head_ref, mine_ref, other_ref, pair_ref, dir_ref, *refs
):
    sources, refs = refs[:parts], refs[parts:]
    z_out, kp_out, high_out, both_out, zsq_ref = refs[:5]
    blocks, pinv, zz, z_buf, kp_buf, high_buf, both_buf, sems, out_sems = refs[5:]
    copies = chunk_copies(sources, blocks, sems)
    for copy in copies:
        copy.start()
    share = mine_ref.shape[0]
    panel = pinv.shape[0]
    outputs = dir_ref.shape[0]
    features = centers_ref.shape[1]
    at = flags_ref[1]
    core = at % 2
    far = (2 - (at - core)) * share
    pinv[pl.ds(pl.multiple_of(at * share, share), share)] = mine_ref[...]
    pinv[pl.ds(pl.multiple_of((at + 1 - 2 * core) * share, share), share)] = other_ref[...]
    pinv[pl.ds(pl.multiple_of(far + core * share, share), share)] = pair_ref[:share]
    pinv[pl.ds(pl.multiple_of(far + (1 - core) * share, share), share)] = pair_ref[share:]
    head = jnp.concatenate([head_ref[i] for i in range(head_ref.shape[0])], axis=0)
    vals = jnp.concatenate(
        [head[panel + b * outputs : panel + (b + 1) * outputs] for b in range(panel // features)],
        axis=1,
    )
    z1 = lax.dot_general(vals, pinv[...], LAST, preferred_element_type=f32).astype(bf16)
    q = jnp.dot(z1, pinv[...], preferred_element_type=f32).astype(bf16)
    heads = widened(head[:panel], 1)
    tile = panel
    squares = jnp.zeros((outputs, 1), f32)
    for i in range(centers_ref.shape[0] // tile):
        rows = slice(i * tile, (i + 1) * tile)
        kp = similar(widened(centers_ref[rows], 0), heads, features)
        kp_buf[rows] = kp
        z = dir_ref[:, rows] - lax.dot_general(q, kp, LAST, preferred_element_type=f32)
        if i == 0:
            z = jnp.where(flags_ref[0] == 0, z1.astype(f32), z)
        z_buf[:, rows] = z
        squares = squares + jnp.sum(z * z, axis=1, keepdims=True)
        high = z.astype(bf16)
        zz[:outputs, rows] = high
        zz[outputs:, rows] = (z - high.astype(f32)).astype(bf16)
    zsq_ref[...] = squares
    puts = [
        pltpu.make_async_copy(z_buf, z_out, out_sems.at[0]),
        pltpu.make_async_copy(kp_buf, kp_out, out_sems.at[1]),
    ]
    for put in puts:
        put.start()
    per = blocks.shape[2] // 128
    for i, copy in enumerate(copies):
        copy.wait()
        u = jnp.dot(zz[...], blocks[i], preferred_element_type=f32)
        for b in range(per):
            part = u[:, b * 128 : (b + 1) * 128]
            high_buf[i * per + b] = part[:outputs]
            both_buf[i * per + b] = part[:outputs] + part[outputs:]
        span = pl.ds(i * per, per)
        for j, (buf, out) in enumerate(((high_buf, high_out), (both_buf, both_out))):
            puts.append(
                pltpu.make_async_copy(buf.at[span], out.at[span], out_sems.at[2 + 2 * i + j])
            )
            puts[-1].start()
    for put in puts:
        put.wait()


def panel_step(flags, centers, head, mine, other, pair, direction, blocks):
    outputs, m_dev = direction.shape
    panel = mine.shape[1]
    count, _, chunk = blocks[0].shape
    count = count * len(blocks)
    values = jax.ShapeDtypeStruct((count * chunk // 128, outputs, 128), f32)
    z = jax.ShapeDtypeStruct((outputs, m_dev), f32)
    k_panel = jax.ShapeDtypeStruct((m_dev, panel), bf16)
    return pl.pallas_call(
        functools.partial(panel_kernel, len(blocks)),
        out_shape=(z, k_panel, values, values, jax.ShapeDtypeStruct((outputs, 1), f32)),
        in_specs=[SMEM] + [VMEM] * 6 + [ANY] * len(blocks),
        out_specs=(ANY, ANY, ANY, ANY, VMEM),
        scratch_shapes=[
            pltpu.VMEM((count, m_dev, chunk), bf16),
            pltpu.VMEM((panel, panel), bf16),
            pltpu.VMEM((2 * outputs, m_dev), bf16),
            pltpu.VMEM(z.shape, f32),
            pltpu.VMEM(k_panel.shape, bf16),
            pltpu.VMEM(values.shape, f32),
            pltpu.VMEM(values.shape, f32),
            pltpu.SemaphoreType.DMA((count,)),
            pltpu.SemaphoreType.DMA((2 + 2 * count,)),
        ],
        compiler_params=pltpu.CompilerParams(vmem_limit_bytes=60 << 20),
        cost_estimate=pl.CostEstimate(
            flops=2 * 256 * m_dev * count * chunk,
            bytes_accessed=2 * m_dev * count * chunk,
            transcendentals=m_dev * panel,
        ),
        name="panel",
    )(flags, centers, head, mine, other, pair, direction, *blocks)


def image_kernel(parts, flags_ref, tie_ref, w_ref, *refs):
    sources = refs[:parts]
    keep_ref, send_ref, blocks, total, sems = refs[parts:]
    copies = chunk_copies(sources, blocks, sems)
    for copy in copies:
        copy.start()
    per = blocks.shape[1] // 128
    for i, copy in enumerate(copies):
        w = jnp.concatenate([w_ref[i * per + b] for b in range(per)], axis=1)
        copy.wait()
        part = jnp.dot(w, blocks[i], preferred_element_type=f32)
        total[...] = part if i == 0 else total[...] + part
    half = keep_ref.shape[0]
    mine = pl.multiple_of((flags_ref[1] % 2) * half, half)
    keep_ref[...] = total[pl.ds(mine, half)]
    send_ref[...] = total[pl.ds(half - mine, half)]


def image(flags, tie, w, blocks):
    outputs = w.shape[1]
    count, chunk, m_dev = blocks[0].shape
    count = count * len(blocks)
    shape = jax.ShapeDtypeStruct((outputs // 2, m_dev), f32)
    return pl.pallas_call(
        functools.partial(image_kernel, len(blocks)),
        out_shape=(shape, shape),
        in_specs=[SMEM, ANY, VMEM] + [ANY] * len(blocks),
        out_specs=(VMEM, VMEM),
        scratch_shapes=[
            pltpu.VMEM((count, chunk, m_dev), bf16),
            pltpu.VMEM((outputs, m_dev), f32),
            pltpu.SemaphoreType.DMA((count,)),
        ],
        compiler_params=pltpu.CompilerParams(vmem_limit_bytes=60 << 20),
        cost_estimate=pl.CostEstimate(
            flops=2 * 256 * count * chunk * m_dev,
            bytes_accessed=2 * count * chunk * m_dev,
            transcendentals=0,
        ),
        name="image",
    )(flags, tie, w, *blocks)


def exchange(x, axis):
    return lax.all_to_all(x, axis, 0, 0, tiled=True)


def products_kernel(scale, ridge, count, w_ref, both_ref, z_squares_ref, res_ref, out_ref):
    outputs = w_ref.shape[1]
    total = jnp.zeros(w_ref.shape[1:], f32)
    for i in range(w_ref.shape[0]):
        total = total + w_ref[i].astype(f32) * both_ref[i]
    mine = jnp.sum(total, axis=1, keepdims=True) * scale + ridge * z_squares_ref[...]
    squares = jnp.sum(res_ref[...] * res_ref[...], axis=1, keepdims=True) * (1.0 / count)
    lane = lax.broadcasted_iota(jnp.int32, total.shape, 1)
    row = lax.broadcasted_iota(jnp.int32, total.shape, 0)
    spread_out = jnp.where(lane == row, mine, jnp.where(lane == row + outputs, squares, 0.0))
    out_ref[...] = jnp.sum(spread_out, axis=0, keepdims=True)


def products(w, both, z_squares, residual, scale, count):
    return pl.pallas_call(
        functools.partial(products_kernel, scale, RIDGE_TERM / count, count),
        out_shape=jax.ShapeDtypeStruct((1, 128), f32),
        in_specs=[VMEM] * 4,
        out_specs=VMEM,
        compiler_params=pltpu.CompilerParams(vmem_limit_bytes=LIMIT),
        name="products",
    )(w, both, z_squares, residual)


def swap(x, bit):
    n = lax.axis_size("pts")
    return lax.ppermute(x, "pts", [(i, i ^ bit) for i in range(n)])


def rows_kernel(tie_ref, k_ref, pinv_ref, out_ref):
    out_ref[...] = lax.dot_general(
        k_ref[...], pinv_ref[...], LAST, preferred_element_type=f32
    ).astype(bf16)


def rows_step(tie, k_panel, share):
    return pl.pallas_call(
        rows_kernel,
        out_shape=jax.ShapeDtypeStruct((k_panel.shape[0], share.shape[0]), bf16),
        in_specs=[ANY, VMEM, VMEM],
        out_specs=VMEM,
        compiler_params=pltpu.CompilerParams(vmem_limit_bytes=LIMIT),
        cost_estimate=pl.CostEstimate(
            flops=2 * k_panel.size * share.shape[0],
            bytes_accessed=2 * k_panel.size,
            transcendentals=0,
        ),
        name="rows",
    )(tie, k_panel, share)


def final_kernel(scale, flags_ref, keep_ref, other_ref, z_ref, res_ref, sums_ref, op_ref, new_ref):
    outputs = z_ref.shape[0]
    half = keep_ref.shape[0]
    sums = jnp.sum(sums_ref[...], axis=0)
    lane = lax.broadcasted_iota(jnp.int32, (outputs, sums.shape[1]), 1)
    row = lax.broadcasted_iota(jnp.int32, (outputs, sums.shape[1]), 0)
    curvature = jnp.sum(jnp.where(lane == row, sums, 0.0), axis=1, keepdims=True)
    squares = jnp.sum(jnp.where(lane == row + outputs, sums, 0.0), axis=1, keepdims=True)
    op_ref[...] = RIDGE_TERM * z_ref[...]
    mine = pl.multiple_of((flags_ref[1] % 2) * half, half)
    op_ref[pl.ds(mine, half)] += keep_ref[...] * scale
    op_ref[pl.ds(half - mine, half)] += other_ref[...] * scale
    new_ref[...] = res_ref[...] - (squares / curvature) * op_ref[...]


def final_step(flags, keep, other, z, residual, sums, scale):
    shape = jax.ShapeDtypeStruct(z.shape, f32)
    return pl.pallas_call(
        functools.partial(final_kernel, scale),
        out_shape=(shape, shape),
        in_specs=[SMEM] + [VMEM] * 5,
        out_specs=(VMEM, VMEM),
        compiler_params=pltpu.CompilerParams(vmem_limit_bytes=LIMIT),
        name="final",
    )(flags, keep, other, z, residual, sums)


def shards(points, centers, panel_inverse, direction, residual):
    n_ctr = lax.axis_size(CTR)
    n_near = lax.axis_size(NEAR)
    n_far = lax.axis_size(FAR)
    n_pts = lax.axis_size("pts")
    flags = jnp.stack([lax.axis_index(CTR), lax.axis_index("pts")])
    m_dev, features = centers.shape
    npg = points.shape[0]
    panel = panel_inverse.shape[1]
    outputs = direction.shape[0]
    w_scale = 1.0 / (2.0 * math.sqrt(m_dev * n_ctr))
    image_scale = 1.0 / (2.0 * math.sqrt(npg * n_pts))

    head = exchange(head_payload(flags, centers, direction, panel, n_near), NEAR)
    by_center = [by_center_block(centers, points, i, 2) for i in range(2)]
    other = swap(panel_inverse, 1)
    pair = swap(jnp.concatenate([panel_inverse, other], axis=0), 2)
    head = exchange(spread(head, n_far), FAR)
    by_center, made = zip(*by_center)
    head = exchange(spread(head, n_near, (*made, pair)), NEAR)

    z, k_panel, high, both, z_squares = panel_step(
        flags, centers, head, panel_inverse, other, pair, direction, by_center
    )

    parts = exchange(high.reshape(n_near, n_far * outputs, 128), NEAR)
    by_point = [by_point_block(z_squares, points, centers, i, 2) for i in range(2)]
    by_point, made = zip(*by_point)
    parts = exchange(summed(parts).reshape(n_far, outputs, 128), FAR)
    w = exchange(owned_copies(parts, w_scale, n_far, made), FAR)
    w = exchange(spread(w.reshape(n_far * outputs, 128), n_near), NEAR)
    w = w.reshape(-1, outputs, 128)

    scalars = products(w, both, z_squares, residual, image_scale, n_pts)
    scalars = scalars + swap(scalars, 1)
    keep, send = image(flags, scalars, w, by_point)
    scalars = scalars + swap(scalars, 2)
    sums = exchange(jnp.broadcast_to(scalars[None], (n_ctr, *scalars.shape)), CTR)
    panel_rows = rows_step(keep, k_panel, panel_inverse)
    keep = keep + swap(send, 1)
    keep = keep + swap(keep, 2)
    operator_image, new_residual = final_step(
        flags, keep, swap(keep, 1), z, residual, sums, image_scale
    )
    return (panel_rows, operator_image, new_residual)


def solution(mesh):
    split = Mesh(
        mesh.devices.reshape(mesh.shape["pts"], 8, 2, 4), ("pts", "ctr_0", "ctr_1", "ctr_2")
    )
    placed = (P("pts", None), P(CTR, None), P("pts", None), P(None, CTR), P(None, CTR))
    return jax.shard_map(
        shards,
        mesh=split,
        in_specs=placed,
        out_specs=(P(CTR, "pts"), P(None, CTR), P(None, CTR)),
        check_vma=False,
    )
```

```python
import functools
import math

import jax
import jax.numpy as jnp
from jax import lax
from jax.experimental import pallas as pl
from jax.experimental.pallas import tpu as pltpu
from jax.sharding import Mesh
from jax.sharding import PartitionSpec as P


CTR = ("ctr_0", "ctr_1", "ctr_2")
NEAR = ("ctr_1", "ctr_2")
FAR = "ctr_0"
RIDGE_TERM = 0.002

bf16, f32 = jnp.bfloat16, jnp.float32
LAST = (((1,), (1,)), ((), ()))
VMEM = pl.BlockSpec(memory_space=pltpu.VMEM)
SMEM = pl.BlockSpec(memory_space=pltpu.SMEM)
ANY = pl.BlockSpec(memory_space=pl.ANY)
LIMIT = 12 << 20


def widened(x, side):
    xf = x.astype(f32)
    n = jnp.sum(xf * xf, axis=1, keepdims=True)
    high = n.astype(bf16).astype(f32)
    rest = n - high
    mid = rest.astype(bf16).astype(f32)
    low = rest - mid
    lane = lax.broadcasted_iota(jnp.int32, x.shape, 1)
    if side == 0:
        extra = jnp.where(lane < 6, 1.0, 0.0)
        extra = jnp.where(lane == 0, high, extra)
        extra = jnp.where(lane == 1, mid, extra)
        extra = jnp.where(lane == 2, low, extra)
        return jnp.concatenate([x, extra.astype(bf16)], axis=1)
    extra = jnp.where(lane < 3, -1.0, 0.0)
    extra = jnp.where(lane == 3, -high, extra)
    extra = jnp.where(lane == 4, -mid, extra)
    extra = jnp.where(lane == 5, -low, extra)
    return jnp.concatenate([(xf * 2.0).astype(bf16), extra.astype(bf16)], axis=1)


def similar(a, b, features):
    t = lax.dot_general(a, b, LAST, preferred_element_type=f32)
    return jnp.exp2(t * (math.log2(math.e) / (2 * features))).astype(bf16)


def chunk_loop(first, count, make, out_ref, buffers, sems):
    def put(i):
        slot = lax.rem(i, 2)
        return pltpu.make_async_copy(buffers.at[slot], out_ref.at[first + i], sems.at[slot])

    def step(i, carry):
        @pl.when(i >= 2)
        def _():
            put(i - 2).wait()

        make(first + i, buffers.at[lax.rem(i, 2)])
        put(i).start()
        return carry

    lax.fori_loop(0, count, step, 0)
    for i in range(max(count - 2, 0), count):
        put(jnp.int32(i)).wait()


def centers_major(cols, wide, points, out):
    right = widened(points, 1)
    for j in range(right.shape[0] // cols):
        cut = slice(j * cols, (j + 1) * cols)
        out[:, cut] = similar(wide[...], right[cut], points.shape[1])


def points_major(cols, wide, points, out):
    left = widened(points, 0)
    for j in range(wide.shape[0] // cols):
        cut = slice(j * cols, (j + 1) * cols)
        out[:, cut] = similar(left, wide[cut], points.shape[1])


def block_kernel(side, first, count, chunk, cols, *refs):
    points_ref, centers_ref = refs[-6:-4]
    out_ref, wide, buffers, sems = refs[-4:]
    wide[...] = widened(centers_ref[...], side)
    fill = points_major if side else centers_major

    def make(i, out):
        rows = pl.ds(pl.multiple_of(i * chunk, chunk), chunk)
        fill(cols, wide, points_ref[rows], out)

    chunk_loop(first, count, make, out_ref, buffers, sems)


def block_part(side, shape, first, count, points, centers, made=None, tie=None, cols=256):
    m_dev, features = centers.shape
    chunk = shape[2] if side == 0 else shape[1]
    extra = [x for x in (made, tie) if x is not None]
    return pl.pallas_call(
        functools.partial(block_kernel, side, first, count, chunk, cols),
        out_shape=jax.ShapeDtypeStruct(shape, bf16),
        in_specs=[ANY] * len(extra) + [VMEM, VMEM],
        out_specs=ANY,
        scratch_shapes=[
            pltpu.VMEM((m_dev, 2 * features), bf16),
            pltpu.VMEM((2, *shape[1:]), bf16),
            pltpu.SemaphoreType.DMA((2,)),
        ],
        input_output_aliases={} if made is None else {0: 0},
        compiler_params=pltpu.CompilerParams(vmem_limit_bytes=44 << 20),
        cost_estimate=pl.CostEstimate(
            flops=4 * m_dev * count * chunk * features,
            bytes_accessed=2 * m_dev * count * chunk,
            transcendentals=m_dev * count * chunk,
        ),
    )(*extra, points, centers)


def head_kernel(centers_ref, dir_ref, out_ref, rows_ref, vals_ref, sems):
    panel, features = rows_ref.shape
    outputs = vals_ref.shape[0]
    first = pltpu.make_async_copy(centers_ref.at[pl.ds(0, panel)], rows_ref, sems.at[0])
    second = pltpu.make_async_copy(dir_ref.at[:, pl.ds(0, panel)], vals_ref, sems.at[1])
    first.start()
    second.start()
    first.wait()
    second.wait()
    per = out_ref.shape[1] // 16
    for g in range(out_ref.shape[0] * per):
        row = 16 * g
        if row < panel:
            x = rows_ref[row : row + 16]
        else:
            b, r = divmod(row - panel, outputs)
            x = vals_ref[r : r + 16, b * features : (b + 1) * features].astype(bf16)
        out_ref[g // per, (g % per) * 16 : (g % per + 1) * 16] = x


def head_payload(centers, direction, panel, ways):
    outputs, features = direction.shape[0], centers.shape[1]
    rows = panel + outputs * panel // features
    return pl.pallas_call(
        head_kernel,
        out_shape=jax.ShapeDtypeStruct((ways, rows // ways, features), bf16),
        in_specs=[ANY, ANY],
        out_specs=VMEM,
        scratch_shapes=[
            pltpu.VMEM((panel, features), bf16),
            pltpu.VMEM((outputs, panel), f32),
            pltpu.SemaphoreType.DMA((2,)),
        ],
        compiler_params=pltpu.CompilerParams(vmem_limit_bytes=60 << 20),
        name="head",
    )(centers, direction)


def spread_kernel(x_ref, *refs):
    out_ref = refs[-1]
    x = x_ref[0] if len(x_ref.shape) == len(out_ref.shape) else x_ref[...]
    for i in range(out_ref.shape[0]):
        out_ref[i] = x


def spread(x, ways):
    shape = x.shape[1:] if len(x.shape) == 3 else x.shape
    return pl.pallas_call(
        spread_kernel,
        out_shape=jax.ShapeDtypeStruct((ways, *shape), x.dtype),
        in_specs=[VMEM],
        out_specs=VMEM,
        compiler_params=pltpu.CompilerParams(vmem_limit_bytes=LIMIT),
        name="spread",
    )(x)


def sum_kernel(x_ref, out_ref):
    total = x_ref[0]
    for i in range(1, x_ref.shape[0]):
        total = total + x_ref[i]
    out_ref[...] = total


def summed(x):
    return pl.pallas_call(
        sum_kernel,
        out_shape=jax.ShapeDtypeStruct(x.shape[1:], x.dtype),
        in_specs=[VMEM],
        out_specs=VMEM,
        compiler_params=pltpu.CompilerParams(vmem_limit_bytes=LIMIT),
        name="summed",
    )(x)


def owned_kernel(scale, x_ref, *refs):
    out_ref = refs[-1]
    total = x_ref[0]
    for i in range(1, x_ref.shape[0]):
        total = total + x_ref[i]
    total = (total * scale).astype(bf16)
    for i in range(out_ref.shape[0]):
        out_ref[i] = total


def owned_copies(x, scale, ways):
    return pl.pallas_call(
        functools.partial(owned_kernel, scale),
        out_shape=jax.ShapeDtypeStruct((ways, *x.shape[1:]), bf16),
        in_specs=[VMEM],
        out_specs=VMEM,
        compiler_params=pltpu.CompilerParams(vmem_limit_bytes=LIMIT),
        name="owned",
    )(x)


def chunk_copies(source, buffer, sems):
    return [
        pltpu.make_async_copy(source.at[i], buffer.at[i], sems.at[i])
        for i in range(buffer.shape[0])
    ]


def panel_kernel(
    cols, flags_ref, centers_ref, head_ref, mine_ref, other_ref, pair_ref, dir_ref, points_ref,
    source_ref, z_ref, rows_ref, high_ref, both_ref, zsq_ref, blocks, made, wide, pinv, zz, sems,
):
    copies = chunk_copies(source_ref, blocks, sems)
    for copy in copies:
        copy.start()
    share = mine_ref.shape[0]
    panel = pinv.shape[0]
    outputs = dir_ref.shape[0]
    features = centers_ref.shape[1]
    at = flags_ref[1]
    core = at % 2
    far = (2 - (at - core)) * share
    pinv[pl.ds(pl.multiple_of(at * share, share), share)] = mine_ref[...]
    pinv[pl.ds(pl.multiple_of((at + 1 - 2 * core) * share, share), share)] = other_ref[...]
    pinv[pl.ds(pl.multiple_of(far + core * share, share), share)] = pair_ref[:share]
    pinv[pl.ds(pl.multiple_of(far + (1 - core) * share, share), share)] = pair_ref[share:]
    head = jnp.concatenate([head_ref[i] for i in range(head_ref.shape[0])], axis=0)
    vals = jnp.concatenate(
        [head[panel + b * outputs : panel + (b + 1) * outputs] for b in range(panel // features)],
        axis=1,
    )
    z1 = lax.dot_general(vals, pinv[...], LAST, preferred_element_type=f32).astype(bf16)
    q = jnp.dot(z1, pinv[...], preferred_element_type=f32).astype(bf16)
    heads = widened(head[:panel], 1)
    tile = panel
    squares = jnp.zeros((outputs, 1), f32)
    for i in range(centers_ref.shape[0] // tile):
        rows = slice(i * tile, (i + 1) * tile)
        wide[rows] = widened(centers_ref[rows], 0)
        kp = similar(wide[rows], heads, features)
        rows_ref[rows] = lax.dot_general(
            kp, mine_ref[...], LAST, preferred_element_type=f32
        ).astype(bf16)
        z = dir_ref[:, rows] - lax.dot_general(q, kp, LAST, preferred_element_type=f32)
        if i == 0:
            z = jnp.where(flags_ref[0] == 0, z1.astype(f32), z)
        z_ref[:, rows] = z
        squares = squares + jnp.sum(z * z, axis=1, keepdims=True)
        high = z.astype(bf16)
        zz[:outputs, rows] = high
        zz[outputs:, rows] = (z - high.astype(f32)).astype(bf16)
    zsq_ref[...] = squares
    chunk = blocks.shape[2]
    per = chunk // 128
    stored = len(copies)
    total = points_ref.shape[0] // chunk
    for i in [*range(stored, total), *range(stored)]:
        if i >= stored:
            centers_major(cols, wide, points_ref[i * chunk : (i + 1) * chunk], made)
            u = jnp.dot(zz[...], made[...], preferred_element_type=f32)
        else:
            copies[i].wait()
            u = jnp.dot(zz[...], blocks[i], preferred_element_type=f32)
        for b in range(per):
            part = u[:, b * 128 : (b + 1) * 128]
            high_ref[i * per + b] = part[:outputs]
            both_ref[i * per + b] = part[:outputs] + part[outputs:]


def panel_step(flags, centers, head, mine, other, pair, direction, points, block, cols=256):
    outputs, m_dev = direction.shape
    share, panel = mine.shape
    count, _, chunk = block.shape
    values = jax.ShapeDtypeStruct((points.shape[0] // 128, outputs, 128), f32)
    return pl.pallas_call(
        functools.partial(panel_kernel, cols),
        out_shape=(
            jax.ShapeDtypeStruct((outputs, m_dev), f32),
            jax.ShapeDtypeStruct((m_dev, share), bf16),
            values,
            values,
            jax.ShapeDtypeStruct((outputs, 1), f32),
        ),
        in_specs=[SMEM] + [VMEM] * 7 + [ANY],
        out_specs=(VMEM,) * 5,
        scratch_shapes=[
            pltpu.VMEM((count, m_dev, chunk), bf16),
            pltpu.VMEM((m_dev, chunk), bf16),
            pltpu.VMEM((m_dev, 2 * centers.shape[1]), bf16),
            pltpu.VMEM((panel, panel), bf16),
            pltpu.VMEM((2 * outputs, m_dev), bf16),
            pltpu.SemaphoreType.DMA((count,)),
        ],
        compiler_params=pltpu.CompilerParams(vmem_limit_bytes=44 << 20),
        cost_estimate=pl.CostEstimate(
            flops=2 * 256 * m_dev * points.shape[0],
            bytes_accessed=2 * m_dev * points.shape[0],
            transcendentals=m_dev * panel,
        ),
        name="panel",
    )(flags, centers, head, mine, other, pair, direction, points, block)


def image_kernel(
    cols, flags_ref, tie_ref, w_ref, centers_ref, points_ref, source_ref, keep_ref, send_ref,
    blocks, made, wide, total, sems,
):
    copies = chunk_copies(source_ref, blocks, sems)
    for copy in copies:
        copy.start()
    wide[...] = widened(centers_ref[...], 1)
    chunk = blocks.shape[1]
    per = chunk // 128
    stored = len(copies)
    count = points_ref.shape[0] // chunk
    total[...] = jnp.zeros_like(total)
    for i in [*range(stored, count), *range(stored)]:
        w = jnp.concatenate([w_ref[i * per + b] for b in range(per)], axis=1)
        if i >= stored:
            points_major(cols, wide, points_ref[i * chunk : (i + 1) * chunk], made)
            total[...] += jnp.dot(w, made[...], preferred_element_type=f32)
        else:
            copies[i].wait()
            total[...] += jnp.dot(w, blocks[i], preferred_element_type=f32)
    half = keep_ref.shape[0]
    mine = pl.multiple_of((flags_ref[1] % 2) * half, half)
    keep_ref[...] = total[pl.ds(mine, half)]
    send_ref[...] = total[pl.ds(half - mine, half)]


def image(flags, tie, w, centers, points, block, cols=256):
    outputs = w.shape[1]
    count, chunk, m_dev = block.shape
    shape = jax.ShapeDtypeStruct((outputs // 2, m_dev), f32)
    return pl.pallas_call(
        functools.partial(image_kernel, cols),
        out_shape=(shape, shape),
        in_specs=[SMEM, VMEM, VMEM, VMEM, VMEM, ANY],
        out_specs=(VMEM, VMEM),
        scratch_shapes=[
            pltpu.VMEM((count, chunk, m_dev), bf16),
            pltpu.VMEM((chunk, m_dev), bf16),
            pltpu.VMEM((m_dev, 2 * centers.shape[1]), bf16),
            pltpu.VMEM((outputs, m_dev), f32),
            pltpu.SemaphoreType.DMA((count,)),
        ],
        compiler_params=pltpu.CompilerParams(vmem_limit_bytes=44 << 20),
        cost_estimate=pl.CostEstimate(
            flops=2 * 256 * points.shape[0] * m_dev,
            bytes_accessed=2 * points.shape[0] * m_dev,
            transcendentals=0,
        ),
        name="image",
    )(flags, tie, w, centers, points, block)


def exchange(x, axis):
    return lax.all_to_all(x, axis, 0, 0, tiled=True)


def products_kernel(scale, ridge, count, w_ref, both_ref, z_squares_ref, res_ref, out_ref):
    outputs = w_ref.shape[1]
    total = jnp.zeros(w_ref.shape[1:], f32)
    for i in range(w_ref.shape[0]):
        total = total + w_ref[i].astype(f32) * both_ref[i]
    mine = jnp.sum(total, axis=1, keepdims=True) * scale + ridge * z_squares_ref[...]
    squares = jnp.sum(res_ref[...] * res_ref[...], axis=1, keepdims=True) * (1.0 / count)
    lane = lax.broadcasted_iota(jnp.int32, total.shape, 1)
    row = lax.broadcasted_iota(jnp.int32, total.shape, 0)
    spread_out = jnp.where(lane == row, mine, jnp.where(lane == row + outputs, squares, 0.0))
    out_ref[...] = jnp.sum(spread_out, axis=0, keepdims=True)


def products(w, both, z_squares, residual, scale, count):
    return pl.pallas_call(
        functools.partial(products_kernel, scale, RIDGE_TERM / count, count),
        out_shape=jax.ShapeDtypeStruct((1, 128), f32),
        in_specs=[VMEM] * 4,
        out_specs=VMEM,
        compiler_params=pltpu.CompilerParams(vmem_limit_bytes=LIMIT),
        name="products",
    )(w, both, z_squares, residual)


def swap(x, bit):
    n = lax.axis_size("pts")
    return lax.ppermute(x, "pts", [(i, i ^ bit) for i in range(n)])


def final_kernel(scale, flags_ref, keep_ref, other_ref, z_ref, res_ref, sums_ref, op_ref, new_ref):
    outputs = z_ref.shape[0]
    half = keep_ref.shape[0]
    sums = jnp.sum(sums_ref[...], axis=0)
    lane = lax.broadcasted_iota(jnp.int32, (outputs, sums.shape[1]), 1)
    row = lax.broadcasted_iota(jnp.int32, (outputs, sums.shape[1]), 0)
    curvature = jnp.sum(jnp.where(lane == row, sums, 0.0), axis=1, keepdims=True)
    squares = jnp.sum(jnp.where(lane == row + outputs, sums, 0.0), axis=1, keepdims=True)
    op_ref[...] = RIDGE_TERM * z_ref[...]
    mine = pl.multiple_of((flags_ref[1] % 2) * half, half)
    op_ref[pl.ds(mine, half)] += keep_ref[...] * scale
    op_ref[pl.ds(half - mine, half)] += other_ref[...] * scale
    new_ref[...] = res_ref[...] - (squares / curvature) * op_ref[...]


def final_step(flags, keep, other, z, residual, sums, scale):
    shape = jax.ShapeDtypeStruct(z.shape, f32)
    return pl.pallas_call(
        functools.partial(final_kernel, scale),
        out_shape=(shape, shape),
        in_specs=[SMEM] + [VMEM] * 5,
        out_specs=(VMEM, VMEM),
        compiler_params=pltpu.CompilerParams(vmem_limit_bytes=LIMIT),
        name="final",
    )(flags, keep, other, z, residual, sums)


def step(points, centers, panel_inverse, direction, residual):
    n_ctr = lax.axis_size(CTR)
    n_near = lax.axis_size(NEAR)
    n_far = lax.axis_size(FAR)
    n_pts = lax.axis_size("pts")
    flags = jnp.stack([lax.axis_index(CTR), lax.axis_index("pts")])
    m_dev, _ = centers.shape
    npg = points.shape[0]
    panel = panel_inverse.shape[1]
    outputs = direction.shape[0]
    w_scale = 1.0 / (2.0 * math.sqrt(m_dev * n_ctr))
    image_scale = 1.0 / (2.0 * math.sqrt(npg * n_pts))

    head = exchange(head_payload(centers, direction, panel, n_near), NEAR)
    shape = (13, m_dev, 512)
    block = None
    for first, count in ((0, 4), (4, 5), (9, 4)):
        block = block_part(0, shape, first, count, points, centers, block)
    other = swap(panel_inverse, 1)
    pair = swap(jnp.concatenate([panel_inverse, other], axis=0), 2)
    head = exchange(spread(head, n_far), FAR)
    head = exchange(spread(head, n_near), NEAR)

    z, panel_rows, high, both, z_squares = panel_step(
        flags, centers, head, panel_inverse, other, pair, direction, points, block
    )

    parts = exchange(high.reshape(n_near, n_far * outputs, 128), NEAR)
    parts = summed(parts).reshape(n_far, outputs, 128)
    parts = exchange(parts, FAR)
    shape = (6, 1024, m_dev)
    block = None
    for first, count in ((0, 4), (4, 2)):
        block = block_part(1, shape, first, count, points, centers, block, z_squares)
    w = exchange(owned_copies(parts, w_scale, n_far), FAR)
    w = exchange(spread(w.reshape(n_far * outputs, 128), n_near), NEAR)
    w = w.reshape(-1, outputs, 128)

    scalars = products(w, both, z_squares, residual, image_scale, n_pts)
    scalars = scalars + swap(scalars, 1)
    keep, send = image(flags, scalars, w, centers, points, block)
    scalars = scalars + swap(scalars, 2)
    sums = jnp.broadcast_to(scalars[None], (n_ctr, *scalars.shape))
    sums = exchange(sums, CTR)
    keep = keep + swap(send, 1)
    keep = keep + swap(keep, 2)
    operator_image, new_residual = final_step(
        flags, keep, swap(keep, 1), z, residual, sums, image_scale
    )
    return (panel_rows, operator_image, new_residual)


def solution(mesh):
    split = Mesh(
        mesh.devices.reshape(mesh.shape["pts"], 8, 2, 4), ("pts", "ctr_0", "ctr_1", "ctr_2")
    )
    placed = (P("pts", None), P(CTR, None), P("pts", None), P(None, CTR), P(None, CTR))
    return jax.shard_map(
        step,
        mesh=split,
        in_specs=placed,
        out_specs=(P(CTR, "pts"), P(None, CTR), P(None, CTR)),
        check_vma=False,
    )
```

```python
import functools
import math

import jax
import jax.numpy as jnp
from jax import lax
from jax.experimental import pallas as pl
from jax.experimental.pallas import tpu as pltpu
from jax.sharding import Mesh
from jax.sharding import PartitionSpec as P


CTR = ("ctr_0", "ctr_1", "ctr_2")
NEAR = ("ctr_1", "ctr_2")
FAR = "ctr_0"
RIDGE_TERM = 0.002

bf16, f32 = jnp.bfloat16, jnp.float32
LAST = (((1,), (1,)), ((), ()))
VMEM = pl.BlockSpec(memory_space=pltpu.VMEM)
SMEM = pl.BlockSpec(memory_space=pltpu.SMEM)
ANY = pl.BlockSpec(memory_space=pl.ANY)
LIMIT = 12 << 20
CHUNK = 1024
WIDTH = 256


def widened(x, side):
    xf = x.astype(f32)
    n = jnp.sum(xf * xf, axis=1, keepdims=True)
    high = n.astype(bf16).astype(f32)
    rest = n - high
    mid = rest.astype(bf16).astype(f32)
    low = rest - mid
    lane = lax.broadcasted_iota(jnp.int32, x.shape, 1)
    if side == 0:
        extra = jnp.where(lane < 6, 1.0, 0.0)
        extra = jnp.where(lane == 0, high, extra)
        extra = jnp.where(lane == 1, mid, extra)
        extra = jnp.where(lane == 2, low, extra)
        return jnp.concatenate([x, extra.astype(bf16)], axis=1)
    extra = jnp.where(lane < 3, -1.0, 0.0)
    extra = jnp.where(lane == 3, -high, extra)
    extra = jnp.where(lane == 4, -mid, extra)
    extra = jnp.where(lane == 5, -low, extra)
    return jnp.concatenate([(xf * 2.0).astype(bf16), extra.astype(bf16)], axis=1)


def similar(a, b, features):
    t = lax.dot_general(a, b, LAST, preferred_element_type=f32)
    return jnp.exp2(t * (math.log2(math.e) / (2 * features))).astype(bf16)


def tiles(side, wide, points):
    features = points.shape[1]
    extended = widened(points, 1 - side)
    columns = extended if side == 0 else wide
    for j in range(columns.shape[0] // WIDTH):
        cut = columns[j * WIDTH : (j + 1) * WIDTH]
        yield similar(wide[...], cut, features) if side == 0 else similar(extended, cut, features)


def block_kernel(side, first, count, *refs):
    points_ref, centers_ref = refs[-9:-7]
    out_ref, points_buf, centers_buf, wide, buffers, sems, in_sems = refs[-7:]
    per = buffers.shape[1]
    load = points_buf.shape[0]
    loads = [
        pltpu.make_async_copy(centers_ref, centers_buf, in_sems.at[0]),
        pltpu.make_async_copy(
            points_ref.at[pl.ds(first * CHUNK, load)], points_buf, in_sems.at[1]
        ),
    ]
    for copy in loads:
        copy.start()
    loads[0].wait()
    wide[...] = widened(centers_buf[...], side)
    loads[1].wait()

    def put(i, j):
        slot = lax.rem(i, 2)
        return pltpu.make_async_copy(
            buffers.at[slot, j], out_ref.at[(first + i) * per + j], sems.at[slot, j]
        )

    def step(i, carry):
        rows = pl.ds(pl.multiple_of(i * CHUNK, CHUNK), CHUNK)
        for j, tile in enumerate(tiles(side, wide, points_buf[rows])):
            if count > 2:

                @pl.when(i >= 2)
                def _(j=j):
                    put(i - 2, j).wait()

            buffers[lax.rem(i, 2), j] = tile
            put(i, j).start()
        return carry

    lax.fori_loop(0, count, step, 0)
    for i in range(max(count - 2, 0), count):
        for j in range(per):
            put(jnp.int32(i), j).wait()


def block_part(side, chunks, first, count, points, centers, made=None, tie=None):
    m_dev, features = centers.shape
    per, rows = (CHUNK // WIDTH, m_dev) if side == 0 else (m_dev // WIDTH, CHUNK)
    extra = [x for x in (made, tie) if x is not None]
    return pl.pallas_call(
        functools.partial(block_kernel, side, first, count),
        out_shape=jax.ShapeDtypeStruct((chunks * per, rows, WIDTH), bf16),
        in_specs=[ANY] * (len(extra) + 2),
        out_specs=ANY,
        scratch_shapes=[
            pltpu.VMEM((count * CHUNK, features), bf16),
            pltpu.VMEM((m_dev, features), bf16),
            pltpu.VMEM((m_dev, 2 * features), bf16),
            pltpu.VMEM((2, per, rows, WIDTH), bf16),
            pltpu.SemaphoreType.DMA((2, per)),
            pltpu.SemaphoreType.DMA((2,)),
        ],
        input_output_aliases={} if made is None else {0: 0},
        compiler_params=pltpu.CompilerParams(vmem_limit_bytes=60 << 20),
        cost_estimate=pl.CostEstimate(
            flops=4 * m_dev * count * CHUNK * features,
            bytes_accessed=2 * m_dev * count * CHUNK,
            transcendentals=m_dev * count * CHUNK,
        ),
    )(*extra, points, centers)


def head_kernel(centers_ref, dir_ref, out_ref, rows_ref, vals_ref, sems):
    panel, features = rows_ref.shape
    outputs = vals_ref.shape[0]
    first = pltpu.make_async_copy(centers_ref.at[pl.ds(0, panel)], rows_ref, sems.at[0])
    second = pltpu.make_async_copy(dir_ref.at[:, pl.ds(0, panel)], vals_ref, sems.at[1])
    first.start()
    second.start()
    first.wait()
    second.wait()
    per = out_ref.shape[1] // 16
    for g in range(out_ref.shape[0] * per):
        row = 16 * g
        if row < panel:
            x = rows_ref[row : row + 16]
        else:
            b, r = divmod(row - panel, outputs)
            x = vals_ref[r : r + 16, b * features : (b + 1) * features].astype(bf16)
        out_ref[g // per, (g % per) * 16 : (g % per + 1) * 16] = x


def head_payload(centers, direction, panel, ways):
    outputs, features = direction.shape[0], centers.shape[1]
    rows = panel + outputs * panel // features
    return pl.pallas_call(
        head_kernel,
        out_shape=jax.ShapeDtypeStruct((ways, rows // ways, features), bf16),
        in_specs=[ANY, ANY],
        out_specs=VMEM,
        scratch_shapes=[
            pltpu.VMEM((panel, features), bf16),
            pltpu.VMEM((outputs, panel), f32),
            pltpu.SemaphoreType.DMA((2,)),
        ],
        compiler_params=pltpu.CompilerParams(vmem_limit_bytes=60 << 20),
        name="head",
    )(centers, direction)


def spread_kernel(x_ref, *refs):
    out_ref = refs[-1]
    x = x_ref[0] if len(x_ref.shape) == len(out_ref.shape) else x_ref[...]
    for i in range(out_ref.shape[0]):
        out_ref[i] = x


def spread(x, ways):
    shape = x.shape[1:] if len(x.shape) == 3 else x.shape
    return pl.pallas_call(
        spread_kernel,
        out_shape=jax.ShapeDtypeStruct((ways, *shape), x.dtype),
        in_specs=[VMEM],
        out_specs=VMEM,
        compiler_params=pltpu.CompilerParams(vmem_limit_bytes=LIMIT),
        name="spread",
    )(x)


def sum_kernel(x_ref, out_ref):
    total = x_ref[0]
    for i in range(1, x_ref.shape[0]):
        total = total + x_ref[i]
    out_ref[...] = total


def summed(x, steps=4):
    ways, rows, lanes = x.shape
    block = rows // steps
    return pl.pallas_call(
        sum_kernel,
        out_shape=jax.ShapeDtypeStruct((rows, lanes), x.dtype),
        grid=(steps,),
        in_specs=[pl.BlockSpec((ways, block, lanes), lambda i: (0, i, 0))],
        out_specs=pl.BlockSpec((block, lanes), lambda i: (i, 0)),
        compiler_params=pltpu.CompilerParams(vmem_limit_bytes=LIMIT),
        name="summed",
    )(x)


def owned_kernel(scale, x_ref, *refs):
    out_ref = refs[-1]
    total = x_ref[0]
    for i in range(1, x_ref.shape[0]):
        total = total + x_ref[i]
    total = (total * scale).astype(bf16)
    for i in range(out_ref.shape[0]):
        out_ref[i] = total


def owned_copies(x, scale, ways):
    return pl.pallas_call(
        functools.partial(owned_kernel, scale),
        out_shape=jax.ShapeDtypeStruct((ways, *x.shape[1:]), bf16),
        in_specs=[VMEM],
        out_specs=VMEM,
        compiler_params=pltpu.CompilerParams(vmem_limit_bytes=LIMIT),
        name="owned",
    )(x)


def chunk_copy(source, buffer, sems, i):
    per = buffer.shape[0] // sems.shape[0]
    span = pl.ds(i * per, per)
    return pltpu.make_async_copy(source.at[span], buffer.at[span], sems.at[i])


def panel_kernel(
    flags_ref, centers_ref, head_ref, mine_ref, other_ref, pair_ref, dir_ref, points_ref,
    source_ref, z_ref, rows_ref, high_out, both_out, zsq_ref, blocks, made, wide, pinv, zz,
    points_buf, high_ref, both_ref, sems, points_sem, out_sems,
):
    stored = sems.shape[0]
    local = pltpu.make_async_copy(
        points_ref.at[pl.ds(stored * CHUNK, points_buf.shape[0])], points_buf, points_sem
    )
    local.start()
    for i in range(stored):
        chunk_copy(source_ref, blocks, sems, i).start()
    share = mine_ref.shape[0]
    panel = pinv.shape[0]
    outputs = dir_ref.shape[0]
    features = centers_ref.shape[1]
    at = flags_ref[1]
    core = at % 2
    far = (2 - (at - core)) * share
    pinv[pl.ds(pl.multiple_of(at * share, share), share)] = mine_ref[...]
    pinv[pl.ds(pl.multiple_of((at + 1 - 2 * core) * share, share), share)] = other_ref[...]
    pinv[pl.ds(pl.multiple_of(far + core * share, share), share)] = pair_ref[:share]
    pinv[pl.ds(pl.multiple_of(far + (1 - core) * share, share), share)] = pair_ref[share:]
    head = jnp.concatenate([head_ref[i] for i in range(head_ref.shape[0])], axis=0)
    vals = jnp.concatenate(
        [head[panel + b * outputs : panel + (b + 1) * outputs] for b in range(panel // features)],
        axis=1,
    )
    z1 = lax.dot_general(vals, pinv[...], LAST, preferred_element_type=f32).astype(bf16)
    q = jnp.dot(z1, pinv[...], preferred_element_type=f32).astype(bf16)
    heads = widened(head[:panel], 1)
    tile = panel
    squares = jnp.zeros((outputs, 1), f32)
    for i in range(centers_ref.shape[0] // tile):
        rows = slice(i * tile, (i + 1) * tile)
        wide[rows] = widened(centers_ref[rows], 0)
        kp = similar(wide[rows], heads, features)
        rows_ref[rows] = lax.dot_general(
            kp, mine_ref[...], LAST, preferred_element_type=f32
        ).astype(bf16)
        z = dir_ref[:, rows] - lax.dot_general(q, kp, LAST, preferred_element_type=f32)
        if i == 0:
            z = jnp.where(flags_ref[0] == 0, z1.astype(f32), z)
        z_ref[:, rows] = z
        squares = squares + jnp.sum(z * z, axis=1, keepdims=True)
        high = z.astype(bf16)
        zz[:outputs, rows] = high
        zz[outputs:, rows] = (z - high.astype(f32)).astype(bf16)
    zsq_ref[...] = squares
    local.wait()
    total = points_ref.shape[0] // CHUNK
    width = WIDTH // 128
    per = CHUNK // WIDTH

    def puts(i):
        span = pl.ds(i * per * width, per * width)
        return [
            pltpu.make_async_copy(buf.at[span], out.at[span], out_sems.at[i, k])
            for k, (buf, out) in enumerate(((high_ref, high_out), (both_ref, both_out)))
        ]

    def use(i, source, at):
        for j in range(per):
            u = jnp.dot(zz[...], source[at + j], preferred_element_type=f32)
            for b in range(width):
                part = u[:, b * 128 : (b + 1) * 128]
                row = (i * per + j) * width + b
                high_ref[row] = part[:outputs]
                both_ref[row] = part[:outputs] + part[outputs:]
        for put in puts(i):
            put.start()

    def local_step(i, carry):
        rows = pl.ds(pl.multiple_of((i - stored) * CHUNK, CHUNK), CHUNK)
        for j, tile in enumerate(tiles(0, wide, points_buf[rows])):
            made[j] = tile
        use(i, made, 0)
        return carry

    def stored_step(i, carry):
        chunk_copy(source_ref, blocks, sems, i).wait()
        use(i, blocks, i * per)
        return carry

    lax.fori_loop(stored, total, local_step, 0)
    lax.fori_loop(0, stored, stored_step, 0)
    for i in range(total):
        for put in puts(i):
            put.wait()


def panel_step(flags, centers, head, mine, other, pair, direction, points, block):
    outputs, m_dev = direction.shape
    share, panel = mine.shape
    features = centers.shape[1]
    count = points.shape[0] // CHUNK
    stored = block.shape[0] * WIDTH // CHUNK
    values = jax.ShapeDtypeStruct((points.shape[0] // 128, outputs, 128), f32)
    return pl.pallas_call(
        panel_kernel,
        out_shape=(
            jax.ShapeDtypeStruct((outputs, m_dev), f32),
            jax.ShapeDtypeStruct((m_dev, share), bf16),
            values,
            values,
            jax.ShapeDtypeStruct((outputs, 1), f32),
        ),
        in_specs=[SMEM] + [VMEM] * 6 + [ANY, ANY],
        out_specs=(VMEM, VMEM, ANY, ANY, VMEM),
        scratch_shapes=[
            pltpu.VMEM(block.shape, bf16),
            pltpu.VMEM((CHUNK // WIDTH, m_dev, WIDTH), bf16),
            pltpu.VMEM((m_dev, 2 * features), bf16),
            pltpu.VMEM((panel, panel), bf16),
            pltpu.VMEM((2 * outputs, m_dev), bf16),
            pltpu.VMEM(((count - stored) * CHUNK, features), bf16),
            pltpu.VMEM(values.shape, f32),
            pltpu.VMEM(values.shape, f32),
            pltpu.SemaphoreType.DMA((stored,)),
            pltpu.SemaphoreType.DMA,
            pltpu.SemaphoreType.DMA((count, 2)),
        ],
        compiler_params=pltpu.CompilerParams(vmem_limit_bytes=60 << 20),
        cost_estimate=pl.CostEstimate(
            flops=2 * 256 * m_dev * points.shape[0],
            bytes_accessed=2 * m_dev * points.shape[0],
            transcendentals=m_dev * panel,
        ),
        name="panel",
    )(flags, centers, head, mine, other, pair, direction, points, block)


def image_kernel(
    flags_ref, tie_ref, w_ref, centers_ref, points_ref, source_ref, keep_ref, send_ref,
    blocks, wide, total, points_buf, sems, points_sem,
):
    stored = sems.shape[0]
    local = pltpu.make_async_copy(
        points_ref.at[pl.ds(stored * CHUNK, points_buf.shape[0])], points_buf, points_sem
    )
    local.start()
    for i in range(stored):
        chunk_copy(source_ref, blocks, sems, i).start()
    wide[...] = widened(centers_ref[...], 1)
    total[...] = jnp.zeros_like(total)
    local.wait()
    count = points_ref.shape[0] // CHUNK
    width = CHUNK // 128
    per = wide.shape[0] // WIDTH

    def use(i, made):
        w = jnp.concatenate([w_ref[i * width + b] for b in range(width)], axis=1)
        for j, tile in enumerate(made):
            cut = slice(j * WIDTH, (j + 1) * WIDTH)
            total[:, cut] += jnp.dot(w, tile, preferred_element_type=f32)

    def local_step(i, carry):
        rows = pl.ds(pl.multiple_of((i - stored) * CHUNK, CHUNK), CHUNK)
        use(i, tiles(1, wide, points_buf[rows]))
        return carry

    def stored_step(i, carry):
        chunk_copy(source_ref, blocks, sems, i).wait()
        use(i, (blocks[i * per + j] for j in range(per)))
        return carry

    lax.fori_loop(stored, count, local_step, 0)
    lax.fori_loop(0, stored, stored_step, 0)
    half = keep_ref.shape[0]
    mine = pl.multiple_of((flags_ref[1] % 2) * half, half)
    keep_ref[...] = total[pl.ds(mine, half)]
    send_ref[...] = total[pl.ds(half - mine, half)]


def image(flags, tie, w, centers, points, block):
    outputs = w.shape[1]
    m_dev, features = centers.shape
    count = points.shape[0] // CHUNK
    stored = block.shape[0] * WIDTH // m_dev
    shape = jax.ShapeDtypeStruct((outputs // 2, m_dev), f32)
    return pl.pallas_call(
        image_kernel,
        out_shape=(shape, shape),
        in_specs=[SMEM, VMEM, VMEM, VMEM, ANY, ANY],
        out_specs=(VMEM, VMEM),
        scratch_shapes=[
            pltpu.VMEM(block.shape, bf16),
            pltpu.VMEM((m_dev, 2 * features), bf16),
            pltpu.VMEM((outputs, m_dev), f32),
            pltpu.VMEM(((count - stored) * CHUNK, features), bf16),
            pltpu.SemaphoreType.DMA((stored,)),
            pltpu.SemaphoreType.DMA,
        ],
        compiler_params=pltpu.CompilerParams(vmem_limit_bytes=44 << 20),
        cost_estimate=pl.CostEstimate(
            flops=2 * 256 * points.shape[0] * m_dev,
            bytes_accessed=2 * points.shape[0] * m_dev,
            transcendentals=0,
        ),
        name="image",
    )(flags, tie, w, centers, points, block)


def exchange(x, axis):
    return lax.all_to_all(x, axis, 0, 0, tiled=True)


def products_kernel(scale, ridge, count, w_ref, both_ref, z_squares_ref, res_ref, out_ref):
    outputs = w_ref.shape[1]
    total = jnp.zeros(w_ref.shape[1:], f32)
    for i in range(w_ref.shape[0]):
        total = total + w_ref[i].astype(f32) * both_ref[i]
    mine = jnp.sum(total, axis=1, keepdims=True) * scale + ridge * z_squares_ref[...]
    squares = jnp.sum(res_ref[...] * res_ref[...], axis=1, keepdims=True) * (1.0 / count)
    lane = lax.broadcasted_iota(jnp.int32, total.shape, 1)
    row = lax.broadcasted_iota(jnp.int32, total.shape, 0)
    spread_out = jnp.where(lane == row, mine, jnp.where(lane == row + outputs, squares, 0.0))
    out_ref[...] = jnp.sum(spread_out, axis=0, keepdims=True)


def products(w, both, z_squares, residual, scale, count):
    return pl.pallas_call(
        functools.partial(products_kernel, scale, RIDGE_TERM / count, count),
        out_shape=jax.ShapeDtypeStruct((1, 128), f32),
        in_specs=[VMEM] * 4,
        out_specs=VMEM,
        compiler_params=pltpu.CompilerParams(vmem_limit_bytes=LIMIT),
        name="products",
    )(w, both, z_squares, residual)


def swap(x, bit):
    n = lax.axis_size("pts")
    return lax.ppermute(x, "pts", [(i, i ^ bit) for i in range(n)])


def final_kernel(scale, flags_ref, keep_ref, other_ref, z_ref, res_ref, sums_ref, op_ref, new_ref):
    outputs = z_ref.shape[0]
    half = keep_ref.shape[0]
    sums = jnp.sum(sums_ref[...], axis=0)
    lane = lax.broadcasted_iota(jnp.int32, (outputs, sums.shape[1]), 1)
    row = lax.broadcasted_iota(jnp.int32, (outputs, sums.shape[1]), 0)
    curvature = jnp.sum(jnp.where(lane == row, sums, 0.0), axis=1, keepdims=True)
    squares = jnp.sum(jnp.where(lane == row + outputs, sums, 0.0), axis=1, keepdims=True)
    op_ref[...] = RIDGE_TERM * z_ref[...]
    mine = pl.multiple_of((flags_ref[1] % 2) * half, half)
    op_ref[pl.ds(mine, half)] += keep_ref[...] * scale
    op_ref[pl.ds(half - mine, half)] += other_ref[...] * scale
    new_ref[...] = res_ref[...] - (squares / curvature) * op_ref[...]


def final_step(flags, keep, other, z, residual, sums, scale):
    shape = jax.ShapeDtypeStruct(z.shape, f32)
    return pl.pallas_call(
        functools.partial(final_kernel, scale),
        out_shape=(shape, shape),
        in_specs=[SMEM] + [VMEM] * 5,
        out_specs=(VMEM, VMEM),
        compiler_params=pltpu.CompilerParams(vmem_limit_bytes=LIMIT),
        name="final",
    )(flags, keep, other, z, residual, sums)


def step(points, centers, panel_inverse, direction, residual):
    n_ctr = lax.axis_size(CTR)
    n_near = lax.axis_size(NEAR)
    n_far = lax.axis_size(FAR)
    n_pts = lax.axis_size("pts")
    flags = jnp.stack([lax.axis_index(CTR), lax.axis_index("pts")])
    m_dev, _ = centers.shape
    npg = points.shape[0]
    panel = panel_inverse.shape[1]
    outputs = direction.shape[0]
    w_scale = 1.0 / (2.0 * math.sqrt(m_dev * n_ctr))
    image_scale = 1.0 / (2.0 * math.sqrt(npg * n_pts))

    head = exchange(head_payload(centers, direction, panel, n_near), NEAR)
    block = None
    for i in range(3):
        block = block_part(0, 6, 2 * i, 2, points, centers, block)
    other = swap(panel_inverse, 1)
    pair = swap(jnp.concatenate([panel_inverse, other], axis=0), 2)
    head = exchange(spread(head, n_far), FAR)
    head = exchange(spread(head, n_near), NEAR)

    z, panel_rows, high, both, z_squares = panel_step(
        flags, centers, head, panel_inverse, other, pair, direction, points, block
    )

    parts = exchange(high.reshape(n_near, n_far * outputs, 128), NEAR)
    parts = summed(parts).reshape(n_far, outputs, 128)
    parts = exchange(parts, FAR)
    block = None
    for first, count in ((0, 4), (4, 2)):
        block = block_part(1, 6, first, count, points, centers, block, z_squares)
    w = exchange(owned_copies(parts, w_scale, n_far), FAR)
    w = exchange(spread(w.reshape(n_far * outputs, 128), n_near), NEAR)
    w = w.reshape(-1, outputs, 128)

    scalars = products(w, both, z_squares, residual, image_scale, n_pts)
    scalars = scalars + swap(scalars, 1)
    keep, send = image(flags, scalars, w, centers, points, block)
    scalars = scalars + swap(scalars, 2)
    sums = jnp.broadcast_to(scalars[None], (n_ctr, *scalars.shape))
    sums = exchange(sums, CTR)
    keep = keep + swap(send, 1)
    keep = keep + swap(keep, 2)
    operator_image, new_residual = final_step(
        flags, keep, swap(keep, 1), z, residual, sums, image_scale
    )
    return (panel_rows, operator_image, new_residual)


def solution(mesh):
    split = Mesh(
        mesh.devices.reshape(mesh.shape["pts"], 8, 2, 4), ("pts", "ctr_0", "ctr_1", "ctr_2")
    )
    placed = (P("pts", None), P(CTR, None), P("pts", None), P(None, CTR), P(None, CTR))
    return jax.shard_map(
        step,
        mesh=split,
        in_specs=placed,
        out_specs=(P(CTR, "pts"), P(None, CTR), P(None, CTR)),
        check_vma=False,
    )
```

```python
import functools
import math

import jax
import jax.numpy as jnp
from jax import lax
from jax.experimental import pallas as pl
from jax.experimental.pallas import tpu as pltpu
from jax.sharding import Mesh
from jax.sharding import PartitionSpec as P


CTR = ("ctr_0", "ctr_1", "ctr_2")
NEAR = ("ctr_1", "ctr_2")
FAR = "ctr_0"
RIDGE_TERM = 0.002

bf16, f32 = jnp.bfloat16, jnp.float32
LAST = (((1,), (1,)), ((), ()))
VMEM = pl.BlockSpec(memory_space=pltpu.VMEM)
SMEM = pl.BlockSpec(memory_space=pltpu.SMEM)
ANY = pl.BlockSpec(memory_space=pl.ANY)
LIMIT = 12 << 20
CHUNK = 1024
HALF = 512
WIDTH = 256


def widened(x, side):
    xf = x.astype(f32)
    n = jnp.sum(xf * xf, axis=1, keepdims=True)
    high = n.astype(bf16).astype(f32)
    rest = n - high
    mid = rest.astype(bf16).astype(f32)
    low = rest - mid
    lane = lax.broadcasted_iota(jnp.int32, x.shape, 1)
    if side == 0:
        extra = jnp.where(lane < 6, 1.0, 0.0)
        extra = jnp.where(lane == 0, high, extra)
        extra = jnp.where(lane == 1, mid, extra)
        extra = jnp.where(lane == 2, low, extra)
        return jnp.concatenate([x, extra.astype(bf16)], axis=1)
    extra = jnp.where(lane < 3, -1.0, 0.0)
    extra = jnp.where(lane == 3, -high, extra)
    extra = jnp.where(lane == 4, -mid, extra)
    extra = jnp.where(lane == 5, -low, extra)
    return jnp.concatenate([(xf * 2.0).astype(bf16), extra.astype(bf16)], axis=1)


def similar(a, b, features):
    t = lax.dot_general(a, b, LAST, preferred_element_type=f32)
    return jnp.exp2(t * (math.log2(math.e) / (2 * features))).astype(bf16)


def fill(side, wide, points, out):
    features = points.shape[1]
    extended = widened(points, 1 - side)
    columns = extended if side == 0 else wide
    for j in range(columns.shape[0] // WIDTH):
        cut = slice(j * WIDTH, (j + 1) * WIDTH)
        rows = wide[...] if side == 0 else extended
        out[:, cut] = similar(rows, columns[cut], features)


def block_kernel(side, size, first, count, *refs):
    points_ref, centers_ref = refs[-9:-7]
    out_ref, points_buf, centers_buf, wide, buffers, sems, in_sems = refs[-7:]
    slots = buffers.shape[0]
    loads = [
        pltpu.make_async_copy(centers_ref, centers_buf, in_sems.at[0]),
        pltpu.make_async_copy(
            points_ref.at[pl.ds(first * size, count * size)], points_buf, in_sems.at[1]
        ),
    ]
    for copy in loads:
        copy.start()
    loads[0].wait()
    wide[...] = widened(centers_buf[...], side)
    loads[1].wait()

    def put(i):
        slot = lax.rem(i, slots)
        return pltpu.make_async_copy(buffers.at[slot], out_ref.at[first + i], sems.at[slot])

    def step(i, carry):
        if count > slots:

            @pl.when(i >= slots)
            def _():
                put(i - slots).wait()

        rows = pl.ds(pl.multiple_of(i * size, size), size)
        fill(side, wide, points_buf[rows], buffers.at[lax.rem(i, slots)])
        put(i).start()
        return carry

    lax.fori_loop(0, count, step, 0)
    for i in range(max(count - slots, 0), count):
        put(jnp.int32(i)).wait()


def block_part(side, size, chunks, first, count, points, centers, made=None, tie=None):
    m_dev, features = centers.shape
    rows, columns = (m_dev, size) if side == 0 else (size, m_dev)
    slots = min(count, 2)
    extra = [x for x in (made, tie) if x is not None]
    return pl.pallas_call(
        functools.partial(block_kernel, side, size, first, count),
        out_shape=jax.ShapeDtypeStruct((chunks, rows, columns), bf16),
        in_specs=[ANY] * (len(extra) + 2),
        out_specs=ANY,
        scratch_shapes=[
            pltpu.VMEM((count * size, features), bf16),
            pltpu.VMEM((m_dev, features), bf16),
            pltpu.VMEM((m_dev, 2 * features), bf16),
            pltpu.VMEM((slots, rows, columns), bf16),
            pltpu.SemaphoreType.DMA((slots,)),
            pltpu.SemaphoreType.DMA((2,)),
        ],
        input_output_aliases={} if made is None else {0: 0},
        compiler_params=pltpu.CompilerParams(vmem_limit_bytes=60 << 20),
        cost_estimate=pl.CostEstimate(
            flops=4 * m_dev * count * size * features,
            bytes_accessed=2 * m_dev * count * size,
            transcendentals=m_dev * count * size,
        ),
    )(*extra, points, centers)


def head_kernel(centers_ref, dir_ref, out_ref, rows_ref, vals_ref, sems):
    panel, features = rows_ref.shape
    outputs = vals_ref.shape[0]
    first = pltpu.make_async_copy(centers_ref.at[pl.ds(0, panel)], rows_ref, sems.at[0])
    second = pltpu.make_async_copy(dir_ref.at[:, pl.ds(0, panel)], vals_ref, sems.at[1])
    first.start()
    second.start()
    first.wait()
    second.wait()
    per = out_ref.shape[1] // 16
    for g in range(out_ref.shape[0] * per):
        row = 16 * g
        if row < panel:
            x = rows_ref[row : row + 16]
        else:
            b, r = divmod(row - panel, outputs)
            x = vals_ref[r : r + 16, b * features : (b + 1) * features].astype(bf16)
        out_ref[g // per, (g % per) * 16 : (g % per + 1) * 16] = x


def head_payload(centers, direction, panel, ways):
    outputs, features = direction.shape[0], centers.shape[1]
    rows = panel + outputs * panel // features
    return pl.pallas_call(
        head_kernel,
        out_shape=jax.ShapeDtypeStruct((ways, rows // ways, features), bf16),
        in_specs=[ANY, ANY],
        out_specs=VMEM,
        scratch_shapes=[
            pltpu.VMEM((panel, features), bf16),
            pltpu.VMEM((outputs, panel), f32),
            pltpu.SemaphoreType.DMA((2,)),
        ],
        compiler_params=pltpu.CompilerParams(vmem_limit_bytes=60 << 20),
        name="head",
    )(centers, direction)


def spread_kernel(x_ref, *refs):
    out_ref = refs[-1]
    x = x_ref[0] if len(x_ref.shape) == len(out_ref.shape) else x_ref[...]
    for i in range(out_ref.shape[0]):
        out_ref[i] = x


def spread(x, ways):
    shape = x.shape[1:] if len(x.shape) == 3 else x.shape
    return pl.pallas_call(
        spread_kernel,
        out_shape=jax.ShapeDtypeStruct((ways, *shape), x.dtype),
        in_specs=[VMEM],
        out_specs=VMEM,
        compiler_params=pltpu.CompilerParams(vmem_limit_bytes=LIMIT),
        name="spread",
    )(x)


def sum_kernel(x_ref, out_ref):
    total = x_ref[0]
    for i in range(1, x_ref.shape[0]):
        total = total + x_ref[i]
    out_ref[...] = total


def summed(x, steps=4):
    ways, rows, lanes = x.shape
    block = rows // steps
    return pl.pallas_call(
        sum_kernel,
        out_shape=jax.ShapeDtypeStruct((rows, lanes), x.dtype),
        grid=(steps,),
        in_specs=[pl.BlockSpec((ways, block, lanes), lambda i: (0, i, 0))],
        out_specs=pl.BlockSpec((block, lanes), lambda i: (i, 0)),
        compiler_params=pltpu.CompilerParams(vmem_limit_bytes=LIMIT),
        name="summed",
    )(x)


def owned_kernel(scale, x_ref, *refs):
    out_ref = refs[-1]
    total = x_ref[0]
    for i in range(1, x_ref.shape[0]):
        total = total + x_ref[i]
    total = (total * scale).astype(bf16)
    for i in range(out_ref.shape[0]):
        out_ref[i] = total


def owned_copies(x, scale, ways):
    return pl.pallas_call(
        functools.partial(owned_kernel, scale),
        out_shape=jax.ShapeDtypeStruct((ways, *x.shape[1:]), bf16),
        in_specs=[VMEM],
        out_specs=VMEM,
        compiler_params=pltpu.CompilerParams(vmem_limit_bytes=LIMIT),
        name="owned",
    )(x)


def chunk_copy(source, buffer, sems, i):
    return pltpu.make_async_copy(source.at[i], buffer.at[i], sems.at[i])


def panel_kernel(
    flags_ref, centers_ref, head_ref, mine_ref, other_ref, pair_ref, dir_ref, points_ref,
    source_ref, z_ref, rows_ref, high_out, both_out, zsq_ref, blocks, made, wide, pinv, zz,
    points_buf, high_ref, both_ref, sems, points_sem, out_sems,
):
    stored = sems.shape[0]
    local = pltpu.make_async_copy(
        points_ref.at[pl.ds(stored * HALF, points_buf.shape[0])], points_buf, points_sem
    )
    local.start()
    for i in range(stored):
        chunk_copy(source_ref, blocks, sems, i).start()
    share = mine_ref.shape[0]
    panel = pinv.shape[0]
    outputs = dir_ref.shape[0]
    features = centers_ref.shape[1]
    at = flags_ref[1]
    core = at % 2
    far = (2 - (at - core)) * share
    pinv[pl.ds(pl.multiple_of(at * share, share), share)] = mine_ref[...]
    pinv[pl.ds(pl.multiple_of((at + 1 - 2 * core) * share, share), share)] = other_ref[...]
    pinv[pl.ds(pl.multiple_of(far + core * share, share), share)] = pair_ref[:share]
    pinv[pl.ds(pl.multiple_of(far + (1 - core) * share, share), share)] = pair_ref[share:]
    head = jnp.concatenate([head_ref[i] for i in range(head_ref.shape[0])], axis=0)
    vals = jnp.concatenate(
        [head[panel + b * outputs : panel + (b + 1) * outputs] for b in range(panel // features)],
        axis=1,
    )
    z1 = lax.dot_general(vals, pinv[...], LAST, preferred_element_type=f32).astype(bf16)
    q = jnp.dot(z1, pinv[...], preferred_element_type=f32).astype(bf16)
    heads = widened(head[:panel], 1)
    tile = panel
    squares = jnp.zeros((outputs, 1), f32)
    for i in range(centers_ref.shape[0] // tile):
        rows = slice(i * tile, (i + 1) * tile)
        wide[rows] = widened(centers_ref[rows], 0)
        kp = similar(wide[rows], heads, features)
        rows_ref[rows] = lax.dot_general(
            kp, mine_ref[...], LAST, preferred_element_type=f32
        ).astype(bf16)
        z = dir_ref[:, rows] - lax.dot_general(q, kp, LAST, preferred_element_type=f32)
        if i == 0:
            z = jnp.where(flags_ref[0] == 0, z1.astype(f32), z)
        z_ref[:, rows] = z
        squares = squares + jnp.sum(z * z, axis=1, keepdims=True)
        high = z.astype(bf16)
        zz[:outputs, rows] = high
        zz[outputs:, rows] = (z - high.astype(f32)).astype(bf16)
    zsq_ref[...] = squares
    local.wait()
    total = points_ref.shape[0] // HALF
    per = HALF // 128
    pair = made.shape[1] // HALF

    def puts(i):
        span = pl.ds(i * per, per)
        return [
            pltpu.make_async_copy(buf.at[span], out.at[span], out_sems.at[i, k])
            for k, (buf, out) in enumerate(((high_ref, high_out), (both_ref, both_out)))
        ]

    def use(i, block):
        u = jnp.dot(zz[...], block, preferred_element_type=f32)
        for b in range(block.shape[1] // 128):
            part = u[:, b * 128 : (b + 1) * 128]
            high_ref[i * per + b] = part[:outputs]
            both_ref[i * per + b] = part[:outputs] + part[outputs:]
        for k in range(block.shape[1] // HALF):
            for put in puts(i + k):
                put.start()

    def local_step(i, carry):
        rows = pl.ds(pl.multiple_of(i * pair * HALF, pair * HALF), pair * HALF)
        fill(0, wide, points_buf[rows], made)
        use(stored + pair * i, made[...])
        return carry

    def stored_step(i, carry):
        chunk_copy(source_ref, blocks, sems, i).wait()
        use(i, blocks[i])
        return carry

    lax.fori_loop(0, (total - stored) // pair, local_step, 0)
    lax.fori_loop(0, stored, stored_step, 0)
    for i in range(total):
        for put in puts(i):
            put.wait()


def panel_step(flags, centers, head, mine, other, pair, direction, points, block):
    outputs, m_dev = direction.shape
    share, panel = mine.shape
    features = centers.shape[1]
    count = points.shape[0] // HALF
    stored = block.shape[0]
    values = jax.ShapeDtypeStruct((points.shape[0] // 128, outputs, 128), f32)
    return pl.pallas_call(
        panel_kernel,
        out_shape=(
            jax.ShapeDtypeStruct((outputs, m_dev), f32),
            jax.ShapeDtypeStruct((m_dev, share), bf16),
            values,
            values,
            jax.ShapeDtypeStruct((outputs, 1), f32),
        ),
        in_specs=[SMEM] + [VMEM] * 6 + [ANY, ANY],
        out_specs=(VMEM, VMEM, ANY, ANY, VMEM),
        scratch_shapes=[
            pltpu.VMEM(block.shape, bf16),
            pltpu.VMEM((m_dev, CHUNK), bf16),
            pltpu.VMEM((m_dev, 2 * features), bf16),
            pltpu.VMEM((panel, panel), bf16),
            pltpu.VMEM((2 * outputs, m_dev), bf16),
            pltpu.VMEM(((count - stored) * HALF, features), bf16),
            pltpu.VMEM(values.shape, f32),
            pltpu.VMEM(values.shape, f32),
            pltpu.SemaphoreType.DMA((stored,)),
            pltpu.SemaphoreType.DMA,
            pltpu.SemaphoreType.DMA((count, 2)),
        ],
        compiler_params=pltpu.CompilerParams(vmem_limit_bytes=60 << 20),
        cost_estimate=pl.CostEstimate(
            flops=2 * 256 * m_dev * points.shape[0],
            bytes_accessed=2 * m_dev * points.shape[0],
            transcendentals=m_dev * panel,
        ),
        name="panel",
    )(flags, centers, head, mine, other, pair, direction, points, block)


def image_kernel(
    flags_ref, tie_ref, w_ref, centers_ref, points_ref, source_ref, keep_ref, send_ref,
    blocks, made, wide, total, points_buf, sems, points_sem,
):
    stored = sems.shape[0]
    local = pltpu.make_async_copy(
        points_ref.at[pl.ds(stored * CHUNK, points_buf.shape[0])], points_buf, points_sem
    )
    local.start()
    for i in range(stored):
        chunk_copy(source_ref, blocks, sems, i).start()
    wide[...] = widened(centers_ref[...], 1)
    total[...] = jnp.zeros_like(total)
    local.wait()
    count = points_ref.shape[0] // CHUNK
    width = CHUNK // 128

    def use(i, block):
        w = jnp.concatenate([w_ref[i * width + b] for b in range(width)], axis=1)
        total[...] += jnp.dot(w, block, preferred_element_type=f32)

    def local_step(i, carry):
        rows = pl.ds(pl.multiple_of((i - stored) * CHUNK, CHUNK), CHUNK)
        fill(1, wide, points_buf[rows], made)
        use(i, made[...])
        return carry

    def stored_step(i, carry):
        chunk_copy(source_ref, blocks, sems, i).wait()
        use(i, blocks[i])
        return carry

    lax.fori_loop(stored, count, local_step, 0)
    lax.fori_loop(0, stored, stored_step, 0)
    half = keep_ref.shape[0]
    mine = pl.multiple_of((flags_ref[1] % 2) * half, half)
    keep_ref[...] = total[pl.ds(mine, half)]
    send_ref[...] = total[pl.ds(half - mine, half)]


def image(flags, tie, w, centers, points, block):
    outputs = w.shape[1]
    m_dev, features = centers.shape
    count = points.shape[0] // CHUNK
    stored = block.shape[0]
    shape = jax.ShapeDtypeStruct((outputs // 2, m_dev), f32)
    return pl.pallas_call(
        image_kernel,
        out_shape=(shape, shape),
        in_specs=[SMEM, VMEM, VMEM, VMEM, ANY, ANY],
        out_specs=(VMEM, VMEM),
        scratch_shapes=[
            pltpu.VMEM(block.shape, bf16),
            pltpu.VMEM((CHUNK, m_dev), bf16),
            pltpu.VMEM((m_dev, 2 * features), bf16),
            pltpu.VMEM((outputs, m_dev), f32),
            pltpu.VMEM(((count - stored) * CHUNK, features), bf16),
            pltpu.SemaphoreType.DMA((stored,)),
            pltpu.SemaphoreType.DMA,
        ],
        compiler_params=pltpu.CompilerParams(vmem_limit_bytes=44 << 20),
        cost_estimate=pl.CostEstimate(
            flops=2 * 256 * points.shape[0] * m_dev,
            bytes_accessed=2 * points.shape[0] * m_dev,
            transcendentals=0,
        ),
        name="image",
    )(flags, tie, w, centers, points, block)


def exchange(x, axis):
    return lax.all_to_all(x, axis, 0, 0, tiled=True)


def products_kernel(scale, ridge, count, w_ref, both_ref, z_squares_ref, res_ref, out_ref):
    outputs = w_ref.shape[1]
    total = jnp.zeros(w_ref.shape[1:], f32)
    for i in range(w_ref.shape[0]):
        total = total + w_ref[i].astype(f32) * both_ref[i]
    mine = jnp.sum(total, axis=1, keepdims=True) * scale + ridge * z_squares_ref[...]
    squares = jnp.sum(res_ref[...] * res_ref[...], axis=1, keepdims=True) * (1.0 / count)
    lane = lax.broadcasted_iota(jnp.int32, total.shape, 1)
    row = lax.broadcasted_iota(jnp.int32, total.shape, 0)
    spread_out = jnp.where(lane == row, mine, jnp.where(lane == row + outputs, squares, 0.0))
    out_ref[...] = jnp.sum(spread_out, axis=0, keepdims=True)


def products(w, both, z_squares, residual, scale, count):
    return pl.pallas_call(
        functools.partial(products_kernel, scale, RIDGE_TERM / count, count),
        out_shape=jax.ShapeDtypeStruct((1, 128), f32),
        in_specs=[VMEM] * 4,
        out_specs=VMEM,
        compiler_params=pltpu.CompilerParams(vmem_limit_bytes=LIMIT),
        name="products",
    )(w, both, z_squares, residual)


def swap(x, bit):
    n = lax.axis_size("pts")
    return lax.ppermute(x, "pts", [(i, i ^ bit) for i in range(n)])


def final_kernel(scale, flags_ref, keep_ref, other_ref, z_ref, res_ref, sums_ref, op_ref, new_ref):
    outputs = z_ref.shape[0]
    half = keep_ref.shape[0]
    sums = jnp.sum(sums_ref[...], axis=0)
    lane = lax.broadcasted_iota(jnp.int32, (outputs, sums.shape[1]), 1)
    row = lax.broadcasted_iota(jnp.int32, (outputs, sums.shape[1]), 0)
    curvature = jnp.sum(jnp.where(lane == row, sums, 0.0), axis=1, keepdims=True)
    squares = jnp.sum(jnp.where(lane == row + outputs, sums, 0.0), axis=1, keepdims=True)
    op_ref[...] = RIDGE_TERM * z_ref[...]
    mine = pl.multiple_of((flags_ref[1] % 2) * half, half)
    op_ref[pl.ds(mine, half)] += keep_ref[...] * scale
    op_ref[pl.ds(half - mine, half)] += other_ref[...] * scale
    new_ref[...] = res_ref[...] - (squares / curvature) * op_ref[...]


def final_step(flags, keep, other, z, residual, sums, scale):
    shape = jax.ShapeDtypeStruct(z.shape, f32)
    return pl.pallas_call(
        functools.partial(final_kernel, scale),
        out_shape=(shape, shape),
        in_specs=[SMEM] + [VMEM] * 5,
        out_specs=(VMEM, VMEM),
        compiler_params=pltpu.CompilerParams(vmem_limit_bytes=LIMIT),
        name="final",
    )(flags, keep, other, z, residual, sums)


def step(points, centers, panel_inverse, direction, residual):
    n_ctr = lax.axis_size(CTR)
    n_near = lax.axis_size(NEAR)
    n_far = lax.axis_size(FAR)
    n_pts = lax.axis_size("pts")
    flags = jnp.stack([lax.axis_index(CTR), lax.axis_index("pts")])
    m_dev, _ = centers.shape
    npg = points.shape[0]
    panel = panel_inverse.shape[1]
    outputs = direction.shape[0]
    w_scale = 1.0 / (2.0 * math.sqrt(m_dev * n_ctr))
    image_scale = 1.0 / (2.0 * math.sqrt(npg * n_pts))

    head = exchange(head_payload(centers, direction, panel, n_near), NEAR)
    block = None
    for i in range(3):
        block = block_part(0, HALF, 6, 2 * i, 2, points, centers, block)
    other = swap(panel_inverse, 1)
    pair = swap(jnp.concatenate([panel_inverse, other], axis=0), 2)
    head = exchange(spread(head, n_far), FAR)
    head = exchange(spread(head, n_near), NEAR)

    z, panel_rows, high, both, z_squares = panel_step(
        flags, centers, head, panel_inverse, other, pair, direction, points, block
    )

    parts = exchange(high.reshape(n_near, n_far * outputs, 128), NEAR)
    parts = summed(parts).reshape(n_far, outputs, 128)
    parts = exchange(parts, FAR)
    block = None
    for first, count in ((0, 4), (4, 1), (5, 1)):
        block = block_part(1, CHUNK, 6, first, count, points, centers, block, z_squares)
    w = exchange(owned_copies(parts, w_scale, n_far), FAR)
    w = exchange(spread(w.reshape(n_far * outputs, 128), n_near), NEAR)
    w = w.reshape(-1, outputs, 128)

    scalars = products(w, both, z_squares, residual, image_scale, n_pts)
    scalars = scalars + swap(scalars, 1)
    keep, send = image(flags, scalars, w, centers, points, block)
    scalars = scalars + swap(scalars, 2)
    sums = jnp.broadcast_to(scalars[None], (n_ctr, *scalars.shape))
    sums = exchange(sums, CTR)
    keep = keep + swap(send, 1)
    keep = keep + swap(keep, 2)
    operator_image, new_residual = final_step(
        flags, keep, swap(keep, 1), z, residual, sums, image_scale
    )
    return (panel_rows, operator_image, new_residual)


def solution(mesh):
    split = Mesh(
        mesh.devices.reshape(mesh.shape["pts"], 8, 2, 4), ("pts", "ctr_0", "ctr_1", "ctr_2")
    )
    placed = (P("pts", None), P(CTR, None), P("pts", None), P(None, CTR), P(None, CTR))
    return jax.shard_map(
        step,
        mesh=split,
        in_specs=placed,
        out_specs=(P(CTR, "pts"), P(None, CTR), P(None, CTR)),
        check_vma=False,
    )
```

```python
import functools
import math

import jax
import jax.numpy as jnp
from jax import lax
from jax.experimental import pallas as pl
from jax.experimental.pallas import tpu as pltpu
from jax.sharding import Mesh
from jax.sharding import PartitionSpec as P


CTR = ("ctr_0", "ctr_1", "ctr_2")
NEAR = ("ctr_1", "ctr_2")
FAR = "ctr_0"
RIDGE_TERM = 0.002

bf16, f32 = jnp.bfloat16, jnp.float32
LAST = (((1,), (1,)), ((), ()))
VMEM = pl.BlockSpec(memory_space=pltpu.VMEM)
SMEM = pl.BlockSpec(memory_space=pltpu.SMEM)
ANY = pl.BlockSpec(memory_space=pl.ANY)
LIMIT = 12 << 20
CHUNK = 1024
WIDTH = 256


def widened(x, side):
    xf = x.astype(f32)
    n = jnp.sum(xf * xf, axis=1, keepdims=True)
    high = n.astype(bf16).astype(f32)
    rest = n - high
    mid = rest.astype(bf16).astype(f32)
    low = rest - mid
    lane = lax.broadcasted_iota(jnp.int32, x.shape, 1)
    if side == 0:
        extra = jnp.where(lane < 6, 1.0, 0.0)
        extra = jnp.where(lane == 0, high, extra)
        extra = jnp.where(lane == 1, mid, extra)
        extra = jnp.where(lane == 2, low, extra)
        return jnp.concatenate([x, extra.astype(bf16)], axis=1)
    extra = jnp.where(lane < 3, -1.0, 0.0)
    extra = jnp.where(lane == 3, -high, extra)
    extra = jnp.where(lane == 4, -mid, extra)
    extra = jnp.where(lane == 5, -low, extra)
    return jnp.concatenate([(xf * 2.0).astype(bf16), extra.astype(bf16)], axis=1)


def similar(a, b, features):
    t = lax.dot_general(a, b, LAST, preferred_element_type=f32)
    return jnp.exp2(t * (math.log2(math.e) / (2 * features))).astype(bf16)


def fill(side, wide, points, out):
    features = points.shape[1]
    extended = widened(points, 1 - side)
    columns = extended if side == 0 else wide
    for j in range(columns.shape[0] // WIDTH):
        cut = slice(j * WIDTH, (j + 1) * WIDTH)
        rows = wide[...] if side == 0 else extended
        out[:, cut] = similar(rows, columns[cut], features)


def block_kernel(side, size, first, count, *refs):
    points_ref, centers_ref = refs[-9:-7]
    out_ref, points_buf, centers_buf, wide, buffers, sems, in_sems = refs[-7:]
    slots = buffers.shape[0]
    loads = [
        pltpu.make_async_copy(centers_ref, centers_buf, in_sems.at[0]),
        pltpu.make_async_copy(
            points_ref.at[pl.ds(first * size, count * size)], points_buf, in_sems.at[1]
        ),
    ]
    for copy in loads:
        copy.start()
    loads[0].wait()
    wide[...] = widened(centers_buf[...], side)
    loads[1].wait()

    def put(i):
        slot = lax.rem(i, slots)
        return pltpu.make_async_copy(buffers.at[slot], out_ref.at[first + i], sems.at[slot])

    def step(i, carry):
        if count > slots:

            @pl.when(i >= slots)
            def _():
                put(i - slots).wait()

        rows = pl.ds(pl.multiple_of(i * size, size), size)
        fill(side, wide, points_buf[rows], buffers.at[lax.rem(i, slots)])
        put(i).start()
        return carry

    lax.fori_loop(0, count, step, 0)
    for i in range(max(count - slots, 0), count):
        put(jnp.int32(i)).wait()


def block_part(side, size, chunks, first, count, points, centers, made=None, tie=None):
    m_dev, features = centers.shape
    rows, columns = (m_dev, size) if side == 0 else (size, m_dev)
    slots = min(count, 2)
    extra = [x for x in (made, tie) if x is not None]
    return pl.pallas_call(
        functools.partial(block_kernel, side, size, first, count),
        out_shape=jax.ShapeDtypeStruct((chunks, rows, columns), bf16),
        in_specs=[ANY] * (len(extra) + 2),
        out_specs=ANY,
        scratch_shapes=[
            pltpu.VMEM((count * size, features), bf16),
            pltpu.VMEM((m_dev, features), bf16),
            pltpu.VMEM((m_dev, 2 * features), bf16),
            pltpu.VMEM((slots, rows, columns), bf16),
            pltpu.SemaphoreType.DMA((slots,)),
            pltpu.SemaphoreType.DMA((2,)),
        ],
        input_output_aliases={} if made is None else {0: 0},
        compiler_params=pltpu.CompilerParams(vmem_limit_bytes=60 << 20),
        cost_estimate=pl.CostEstimate(
            flops=4 * m_dev * count * size * features,
            bytes_accessed=2 * m_dev * count * size,
            transcendentals=m_dev * count * size,
        ),
    )(*extra, points, centers)


def resident_kernel(points_ref, centers_ref, out_ref, points_buf, centers_buf, wide, sems):
    loads = [
        pltpu.make_async_copy(centers_ref, centers_buf, sems.at[0]),
        pltpu.make_async_copy(points_ref, points_buf, sems.at[1]),
    ]
    for copy in loads:
        copy.start()
    for copy in loads:
        copy.wait()
    wide[...] = widened(centers_buf[...], 0)
    for i in range(points_buf.shape[0] // CHUNK):
        rows = slice(i * CHUNK, (i + 1) * CHUNK)
        fill(0, wide, points_buf[rows], out_ref.at[:, rows])


def resident_part(first, count, points, centers, limit):
    m_dev, features = centers.shape

    def kernel(points_ref, *refs):
        resident_kernel(points_ref.at[pl.ds(first * CHUNK, count * CHUNK)], *refs)

    return pl.pallas_call(
        kernel,
        out_shape=jax.ShapeDtypeStruct((m_dev, count * CHUNK), bf16),
        in_specs=[ANY, ANY],
        out_specs=VMEM,
        scratch_shapes=[
            pltpu.VMEM((count * CHUNK, features), bf16),
            pltpu.VMEM((m_dev, features), bf16),
            pltpu.VMEM((m_dev, 2 * features), bf16),
            pltpu.SemaphoreType.DMA((2,)),
        ],
        compiler_params=pltpu.CompilerParams(vmem_limit_bytes=limit << 20),
        cost_estimate=pl.CostEstimate(
            flops=4 * m_dev * count * CHUNK * features,
            bytes_accessed=2 * m_dev * count * CHUNK,
            transcendentals=m_dev * count * CHUNK,
        ),
    )(points, centers)


def head_kernel(flags_ref, centers_ref, dir_ref, out_ref, rows_ref, vals_ref, sems):
    panel, features = rows_ref.shape
    outputs = vals_ref.shape[0]
    first = pltpu.make_async_copy(centers_ref.at[pl.ds(0, panel)], rows_ref, sems.at[0])
    second = pltpu.make_async_copy(dir_ref.at[:, pl.ds(0, panel)], vals_ref, sems.at[1])
    first.start()
    second.start()
    first.wait()
    second.wait()
    root = flags_ref[0] == 0
    core = flags_ref[1] % 2
    half = out_ref.shape[0]

    def piece(row):
        if row < panel:
            return rows_ref[row : row + 16]
        b, r = divmod(row - panel, outputs)
        return vals_ref[r : r + 16, b * features : (b + 1) * features].astype(bf16)

    for row in range(0, half, 16):
        x = jnp.where(core == 0, piece(row).astype(f32), piece(row + half).astype(f32))
        out_ref[row : row + 16] = jnp.where(root, x, 0.0).astype(bf16)


def head_payload(flags, centers, direction, panel):
    outputs, features = direction.shape[0], centers.shape[1]
    rows = panel + outputs * panel // features
    return pl.pallas_call(
        head_kernel,
        out_shape=jax.ShapeDtypeStruct((rows // 2, features), bf16),
        in_specs=[SMEM, ANY, ANY],
        out_specs=VMEM,
        scratch_shapes=[
            pltpu.VMEM((panel, features), bf16),
            pltpu.VMEM((outputs, panel), f32),
            pltpu.SemaphoreType.DMA((2,)),
        ],
        compiler_params=pltpu.CompilerParams(vmem_limit_bytes=60 << 20),
        name="head",
    )(flags, centers, direction)


def spread_kernel(x_ref, *refs):
    out_ref = refs[-1]
    x = x_ref[0] if len(x_ref.shape) == len(out_ref.shape) else x_ref[...]
    for i in range(out_ref.shape[0]):
        out_ref[i] = x


def spread(x, ways):
    shape = x.shape[1:] if len(x.shape) == 3 else x.shape
    return pl.pallas_call(
        spread_kernel,
        out_shape=jax.ShapeDtypeStruct((ways, *shape), x.dtype),
        in_specs=[VMEM],
        out_specs=VMEM,
        compiler_params=pltpu.CompilerParams(vmem_limit_bytes=LIMIT),
        name="spread",
    )(x)


def sum_kernel(x_ref, out_ref):
    total = x_ref[0]
    for i in range(1, x_ref.shape[0]):
        total = total + x_ref[i]
    out_ref[...] = total


def summed(x, steps=4):
    ways, rows, lanes = x.shape
    block = rows // steps
    return pl.pallas_call(
        sum_kernel,
        out_shape=jax.ShapeDtypeStruct((rows, lanes), x.dtype),
        grid=(steps,),
        in_specs=[pl.BlockSpec((ways, block, lanes), lambda i: (0, i, 0))],
        out_specs=pl.BlockSpec((block, lanes), lambda i: (i, 0)),
        compiler_params=pltpu.CompilerParams(vmem_limit_bytes=LIMIT),
        name="summed",
    )(x)


def owned_kernel(scale, x_ref, *refs):
    out_ref = refs[-1]
    total = x_ref[0]
    for i in range(1, x_ref.shape[0]):
        total = total + x_ref[i]
    total = (total * scale).astype(bf16)
    for i in range(out_ref.shape[0]):
        out_ref[i] = total


def owned_copies(x, scale, ways):
    return pl.pallas_call(
        functools.partial(owned_kernel, scale),
        out_shape=jax.ShapeDtypeStruct((ways, *x.shape[1:]), bf16),
        in_specs=[VMEM],
        out_specs=VMEM,
        compiler_params=pltpu.CompilerParams(vmem_limit_bytes=LIMIT),
        name="owned",
    )(x)


def chunk_copy(source, buffer, sems, i):
    return pltpu.make_async_copy(source.at[i], buffer.at[i], sems.at[i])


def panel_kernel(
    parts, flags_ref, centers_ref, head_ref, head_other_ref, mine_ref, other_ref, pair_ref, dir_ref,
    *refs
):
    blocks, refs = refs[:parts], refs[parts:]
    z_ref, rows_ref, high_out, both_out, zsq_ref = refs[:5]
    head, pinv, zz, high_ref, both_ref, out_sems = refs[5:]
    share = mine_ref.shape[0]
    panel = pinv.shape[0]
    outputs = dir_ref.shape[0]
    features = centers_ref.shape[1]
    at = flags_ref[1]
    core = at % 2
    far = (2 - (at - core)) * share
    pinv[pl.ds(pl.multiple_of(at * share, share), share)] = mine_ref[...]
    pinv[pl.ds(pl.multiple_of((at + 1 - 2 * core) * share, share), share)] = other_ref[...]
    pinv[pl.ds(pl.multiple_of(far + core * share, share), share)] = pair_ref[:share]
    pinv[pl.ds(pl.multiple_of(far + (1 - core) * share, share), share)] = pair_ref[share:]
    half = head_other_ref.shape[0]
    head[pl.ds(pl.multiple_of(core * half, half), half)] = head_ref[...]
    head[pl.ds(pl.multiple_of(half - core * half, half), half)] = head_other_ref[...]
    vals = jnp.concatenate(
        [head[panel + b * outputs : panel + (b + 1) * outputs] for b in range(panel // features)],
        axis=1,
    )
    z1 = lax.dot_general(vals, pinv[...], LAST, preferred_element_type=f32).astype(bf16)
    q = jnp.dot(z1, pinv[...], preferred_element_type=f32).astype(bf16)
    heads = widened(head[:panel], 1)
    tile = panel
    squares = jnp.zeros((outputs, 1), f32)
    for i in range(centers_ref.shape[0] // tile):
        rows = slice(i * tile, (i + 1) * tile)
        kp = similar(widened(centers_ref[rows], 0), heads, features)
        rows_ref[rows] = lax.dot_general(
            kp, mine_ref[...], LAST, preferred_element_type=f32
        ).astype(bf16)
        z = dir_ref[:, rows] - lax.dot_general(q, kp, LAST, preferred_element_type=f32)
        if i == 0:
            z = jnp.where(flags_ref[0] == 0, z1.astype(f32), z)
        z_ref[:, rows] = z
        squares = squares + jnp.sum(z * z, axis=1, keepdims=True)
        high = z.astype(bf16)
        zz[:outputs, rows] = high
        zz[outputs:, rows] = (z - high.astype(f32)).astype(bf16)
    zsq_ref[...] = squares
    puts = []
    done = 0
    for block in blocks:
        for i in range(block.shape[1] // CHUNK):
            chunk = block[:, i * CHUNK : (i + 1) * CHUNK]
            u = jnp.dot(zz[...], chunk, preferred_element_type=f32)
            for b in range(CHUNK // 128):
                part = u[:, b * 128 : (b + 1) * 128]
                high_ref[done + b] = part[:outputs]
                both_ref[done + b] = part[:outputs] + part[outputs:]
            span = pl.ds(done, CHUNK // 128)
            for buf, out in ((high_ref, high_out), (both_ref, both_out)):
                puts.append(
                    pltpu.make_async_copy(buf.at[span], out.at[span], out_sems.at[len(puts)])
                )
                puts[-1].start()
            done += CHUNK // 128
    for put in puts:
        put.wait()


def panel_step(flags, centers, head, head_other, mine, other, pair, direction, blocks):
    outputs, m_dev = direction.shape
    share, panel = mine.shape
    features = centers.shape[1]
    count = sum(block.shape[1] for block in blocks)
    values = jax.ShapeDtypeStruct((count // 128, outputs, 128), f32)
    return pl.pallas_call(
        functools.partial(panel_kernel, len(blocks)),
        out_shape=(
            jax.ShapeDtypeStruct((outputs, m_dev), f32),
            jax.ShapeDtypeStruct((m_dev, share), bf16),
            values,
            values,
            jax.ShapeDtypeStruct((outputs, 1), f32),
        ),
        in_specs=[SMEM] + [VMEM] * (7 + len(blocks)),
        out_specs=(VMEM, VMEM, ANY, ANY, VMEM),
        scratch_shapes=[
            pltpu.VMEM((2 * head_other.shape[0], features), bf16),
            pltpu.VMEM((panel, panel), bf16),
            pltpu.VMEM((2 * outputs, m_dev), bf16),
            pltpu.VMEM(values.shape, f32),
            pltpu.VMEM(values.shape, f32),
            pltpu.SemaphoreType.DMA((2 * count // CHUNK,)),
        ],
        compiler_params=pltpu.CompilerParams(vmem_limit_bytes=16 << 20),
        cost_estimate=pl.CostEstimate(
            flops=2 * 256 * m_dev * count,
            bytes_accessed=2 * m_dev * count,
            transcendentals=m_dev * panel,
        ),
        name="panel",
    )(flags, centers, head, head_other, mine, other, pair, direction, *blocks)


def image_kernel(
    flags_ref, tie_ref, w_ref, centers_ref, points_ref, source_ref, keep_ref, send_ref,
    blocks, made, wide, total, points_buf, sems, points_sem,
):
    stored = sems.shape[0]
    local = pltpu.make_async_copy(
        points_ref.at[pl.ds(stored * CHUNK, points_buf.shape[0])], points_buf, points_sem
    )
    local.start()
    for i in range(stored):
        chunk_copy(source_ref, blocks, sems, i).start()
    wide[...] = widened(centers_ref[...], 1)
    total[...] = jnp.zeros_like(total)
    local.wait()
    count = points_ref.shape[0] // CHUNK
    width = CHUNK // 128

    def use(i, block):
        w = jnp.concatenate([w_ref[i * width + b] for b in range(width)], axis=1)
        total[...] += jnp.dot(w, block, preferred_element_type=f32)

    def local_step(i, carry):
        rows = pl.ds(pl.multiple_of((i - stored) * CHUNK, CHUNK), CHUNK)
        fill(1, wide, points_buf[rows], made)
        use(i, made[...])
        return carry

    def stored_step(i, carry):
        chunk_copy(source_ref, blocks, sems, i).wait()
        use(i, blocks[i])
        return carry

    lax.fori_loop(stored, count, local_step, 0)
    lax.fori_loop(0, stored, stored_step, 0)
    half = keep_ref.shape[0]
    mine = pl.multiple_of((flags_ref[1] % 2) * half, half)
    keep_ref[...] = total[pl.ds(mine, half)]
    send_ref[...] = total[pl.ds(half - mine, half)]


def image(flags, tie, w, centers, points, block):
    outputs = w.shape[1]
    m_dev, features = centers.shape
    count = points.shape[0] // CHUNK
    stored = block.shape[0]
    shape = jax.ShapeDtypeStruct((outputs // 2, m_dev), f32)
    return pl.pallas_call(
        image_kernel,
        out_shape=(shape, shape),
        in_specs=[SMEM, VMEM, VMEM, VMEM, ANY, ANY],
        out_specs=(VMEM, VMEM),
        scratch_shapes=[
            pltpu.VMEM(block.shape, bf16),
            pltpu.VMEM((CHUNK, m_dev), bf16),
            pltpu.VMEM((m_dev, 2 * features), bf16),
            pltpu.VMEM((outputs, m_dev), f32),
            pltpu.VMEM(((count - stored) * CHUNK, features), bf16),
            pltpu.SemaphoreType.DMA((stored,)),
            pltpu.SemaphoreType.DMA,
        ],
        compiler_params=pltpu.CompilerParams(vmem_limit_bytes=44 << 20),
        cost_estimate=pl.CostEstimate(
            flops=2 * 256 * points.shape[0] * m_dev,
            bytes_accessed=2 * points.shape[0] * m_dev,
            transcendentals=0,
        ),
        name="image",
    )(flags, tie, w, centers, points, block)


def exchange(x, axis):
    return lax.all_to_all(x, axis, 0, 0, tiled=True)


def products_kernel(scale, ridge, count, w_ref, both_ref, z_squares_ref, res_ref, out_ref):
    outputs = w_ref.shape[1]
    total = jnp.zeros(w_ref.shape[1:], f32)
    for i in range(w_ref.shape[0]):
        total = total + w_ref[i].astype(f32) * both_ref[i]
    mine = jnp.sum(total, axis=1, keepdims=True) * scale + ridge * z_squares_ref[...]
    squares = jnp.sum(res_ref[...] * res_ref[...], axis=1, keepdims=True) * (1.0 / count)
    lane = lax.broadcasted_iota(jnp.int32, total.shape, 1)
    row = lax.broadcasted_iota(jnp.int32, total.shape, 0)
    spread_out = jnp.where(lane == row, mine, jnp.where(lane == row + outputs, squares, 0.0))
    out_ref[...] = jnp.sum(spread_out, axis=0, keepdims=True)


def products(w, both, z_squares, residual, scale, count):
    return pl.pallas_call(
        functools.partial(products_kernel, scale, RIDGE_TERM / count, count),
        out_shape=jax.ShapeDtypeStruct((1, 128), f32),
        in_specs=[VMEM] * 4,
        out_specs=VMEM,
        compiler_params=pltpu.CompilerParams(vmem_limit_bytes=LIMIT),
        name="products",
    )(w, both, z_squares, residual)


def tree_stage(x, axis, stride):
    pairs = [(i, i + stride) for i in range(0, lax.axis_size(axis), 2 * stride)]
    return x + lax.ppermute(x, axis, pairs)


def swap(x, bit):
    n = lax.axis_size("pts")
    return lax.ppermute(x, "pts", [(i, i ^ bit) for i in range(n)])


def final_kernel(scale, flags_ref, keep_ref, other_ref, z_ref, res_ref, sums_ref, op_ref, new_ref):
    outputs = z_ref.shape[0]
    half = keep_ref.shape[0]
    sums = jnp.sum(sums_ref[...], axis=0)
    lane = lax.broadcasted_iota(jnp.int32, (outputs, sums.shape[1]), 1)
    row = lax.broadcasted_iota(jnp.int32, (outputs, sums.shape[1]), 0)
    curvature = jnp.sum(jnp.where(lane == row, sums, 0.0), axis=1, keepdims=True)
    squares = jnp.sum(jnp.where(lane == row + outputs, sums, 0.0), axis=1, keepdims=True)
    op_ref[...] = RIDGE_TERM * z_ref[...]
    mine = pl.multiple_of((flags_ref[1] % 2) * half, half)
    op_ref[pl.ds(mine, half)] += keep_ref[...] * scale
    op_ref[pl.ds(half - mine, half)] += other_ref[...] * scale
    new_ref[...] = res_ref[...] - (squares / curvature) * op_ref[...]


def final_step(flags, keep, other, z, residual, sums, scale):
    shape = jax.ShapeDtypeStruct(z.shape, f32)
    return pl.pallas_call(
        functools.partial(final_kernel, scale),
        out_shape=(shape, shape),
        in_specs=[SMEM] + [VMEM] * 5,
        out_specs=(VMEM, VMEM),
        compiler_params=pltpu.CompilerParams(vmem_limit_bytes=LIMIT),
        name="final",
    )(flags, keep, other, z, residual, sums)


def step(points, centers, panel_inverse, direction, residual):
    n_ctr = lax.axis_size(CTR)
    n_near = lax.axis_size(NEAR)
    n_far = lax.axis_size(FAR)
    n_pts = lax.axis_size("pts")
    flags = jnp.stack([lax.axis_index(CTR), lax.axis_index("pts")])
    m_dev, _ = centers.shape
    npg = points.shape[0]
    panel = panel_inverse.shape[1]
    outputs = direction.shape[0]
    w_scale = 1.0 / (2.0 * math.sqrt(m_dev * n_ctr))
    image_scale = 1.0 / (2.0 * math.sqrt(npg * n_pts))

    head = head_payload(flags, centers, direction, panel)
    by_center = []
    first = 0
    stages = n_far.bit_length() - 1
    for count, limit in ((3, 12), (3, 12), (2, 12)):
        by_center.append(resident_part(first, count, points, centers, limit))
        first += count
    for i in range(stages):
        head = tree_stage(head, FAR, n_far >> (i + 1))
    other = swap(panel_inverse, 1)
    pair = swap(jnp.concatenate([panel_inverse, other], axis=0), 2)
    head = exchange(spread(head, n_near), NEAR)[0]
    z, panel_rows, high, both, z_squares = panel_step(
        flags, centers, head, swap(head, 1),
        panel_inverse, other, pair, direction, by_center,
    )

    parts = exchange(high.reshape(n_near, n_far * outputs, 128), NEAR)
    parts = summed(parts).reshape(n_far, outputs, 128)
    parts = exchange(parts, FAR)
    block = None
    for first, count in ((0, 5), (5, 1)):
        block = block_part(1, CHUNK, 6, first, count, points, centers, block, z_squares)
    w = exchange(owned_copies(parts, w_scale, n_far), FAR)
    w = exchange(spread(w.reshape(n_far * outputs, 128), n_near), NEAR)
    w = w.reshape(-1, outputs, 128)

    scalars = products(w, both, z_squares, residual, image_scale, n_pts)
    scalars = scalars + swap(scalars, 1)
    keep, send = image(flags, scalars, w, centers, points, block)
    scalars = scalars + swap(scalars, 2)
    sums = jnp.broadcast_to(scalars[None], (n_ctr, *scalars.shape))
    sums = exchange(sums, CTR)
    keep = keep + swap(send, 1)
    keep = keep + swap(keep, 2)
    operator_image, new_residual = final_step(
        flags, keep, swap(keep, 1), z, residual, sums, image_scale
    )
    return (panel_rows, operator_image, new_residual)


def solution(mesh):
    split = Mesh(
        mesh.devices.reshape(mesh.shape["pts"], 8, 2, 4), ("pts", "ctr_0", "ctr_1", "ctr_2")
    )
    placed = (P("pts", None), P(CTR, None), P("pts", None), P(None, CTR), P(None, CTR))
    return jax.shard_map(
        step,
        mesh=split,
        in_specs=placed,
        out_specs=(P(CTR, "pts"), P(None, CTR), P(None, CTR)),
        check_vma=False,
    )
```

```python
import functools
import math

import jax
import jax.numpy as jnp
from jax import lax
from jax.experimental import pallas as pl
from jax.experimental.pallas import tpu as pltpu
from jax.sharding import Mesh
from jax.sharding import PartitionSpec as P


CTR = ("ctr_0", "ctr_1", "ctr_2")
NEAR = ("ctr_1", "ctr_2")
FAR = "ctr_0"
RIDGE_TERM = 0.002

bf16, f32 = jnp.bfloat16, jnp.float32
LAST = (((1,), (1,)), ((), ()))
VMEM = pl.BlockSpec(memory_space=pltpu.VMEM)
SMEM = pl.BlockSpec(memory_space=pltpu.SMEM)
ANY = pl.BlockSpec(memory_space=pl.ANY)
LIMIT = 12 << 20
CHUNK = 1024
WIDTH = 256


def widened(x, side):
    xf = x.astype(f32)
    n = jnp.sum(xf * xf, axis=1, keepdims=True)
    high = n.astype(bf16).astype(f32)
    rest = n - high
    mid = rest.astype(bf16).astype(f32)
    low = rest - mid
    lane = lax.broadcasted_iota(jnp.int32, x.shape, 1)
    if side == 0:
        extra = jnp.where(lane < 6, 1.0, 0.0)
        extra = jnp.where(lane == 0, high, extra)
        extra = jnp.where(lane == 1, mid, extra)
        extra = jnp.where(lane == 2, low, extra)
        return jnp.concatenate([x, extra.astype(bf16)], axis=1)
    extra = jnp.where(lane < 3, -1.0, 0.0)
    extra = jnp.where(lane == 3, -high, extra)
    extra = jnp.where(lane == 4, -mid, extra)
    extra = jnp.where(lane == 5, -low, extra)
    return jnp.concatenate([(xf * 2.0).astype(bf16), extra.astype(bf16)], axis=1)


def similar(a, b, features):
    t = lax.dot_general(a, b, LAST, preferred_element_type=f32)
    return jnp.exp2(t * (math.log2(math.e) / (2 * features))).astype(bf16)


def fill(side, wide, points, out):
    features = points.shape[1]
    extended = widened(points, 1 - side)
    columns = extended if side == 0 else wide
    for j in range(columns.shape[0] // WIDTH):
        cut = slice(j * WIDTH, (j + 1) * WIDTH)
        rows = wide[...] if side == 0 else extended
        out[:, cut] = similar(rows, columns[cut], features)


def block_kernel(side, size, first, count, *refs):
    points_ref, centers_ref = refs[-9:-7]
    out_ref, points_buf, centers_buf, wide, buffers, sems, in_sems = refs[-7:]
    slots = buffers.shape[0]
    loads = [
        pltpu.make_async_copy(centers_ref, centers_buf, in_sems.at[0]),
        pltpu.make_async_copy(
            points_ref.at[pl.ds(first * size, count * size)], points_buf, in_sems.at[1]
        ),
    ]
    for copy in loads:
        copy.start()
    loads[0].wait()
    wide[...] = widened(centers_buf[...], side)
    loads[1].wait()

    def put(i):
        slot = lax.rem(i, slots)
        return pltpu.make_async_copy(buffers.at[slot], out_ref.at[first + i], sems.at[slot])

    def step(i, carry):
        if count > slots:

            @pl.when(i >= slots)
            def _():
                put(i - slots).wait()

        rows = pl.ds(pl.multiple_of(i * size, size), size)
        fill(side, wide, points_buf[rows], buffers.at[lax.rem(i, slots)])
        put(i).start()
        return carry

    lax.fori_loop(0, count, step, 0)
    for i in range(max(count - slots, 0), count):
        put(jnp.int32(i)).wait()


def block_part(side, size, chunks, first, count, points, centers, made=None, tie=None):
    m_dev, features = centers.shape
    rows, columns = (m_dev, size) if side == 0 else (size, m_dev)
    slots = min(count, 2)
    extra = [x for x in (made, tie) if x is not None]
    return pl.pallas_call(
        functools.partial(block_kernel, side, size, first, count),
        out_shape=jax.ShapeDtypeStruct((chunks, rows, columns), bf16),
        in_specs=[ANY] * (len(extra) + 2),
        out_specs=ANY,
        scratch_shapes=[
            pltpu.VMEM((count * size, features), bf16),
            pltpu.VMEM((m_dev, features), bf16),
            pltpu.VMEM((m_dev, 2 * features), bf16),
            pltpu.VMEM((slots, rows, columns), bf16),
            pltpu.SemaphoreType.DMA((slots,)),
            pltpu.SemaphoreType.DMA((2,)),
        ],
        input_output_aliases={} if made is None else {0: 0},
        compiler_params=pltpu.CompilerParams(vmem_limit_bytes=60 << 20),
        cost_estimate=pl.CostEstimate(
            flops=4 * m_dev * count * size * features,
            bytes_accessed=2 * m_dev * count * size,
            transcendentals=m_dev * count * size,
        ),
    )(*extra, points, centers)


def resident_kernel(points_ref, centers_ref, out_ref, points_buf, centers_buf, wide, sems):
    loads = [
        pltpu.make_async_copy(centers_ref, centers_buf, sems.at[0]),
        pltpu.make_async_copy(points_ref, points_buf, sems.at[1]),
    ]
    for copy in loads:
        copy.start()
    for copy in loads:
        copy.wait()
    wide[...] = widened(centers_buf[...], 0)
    for i in range(points_buf.shape[0] // CHUNK):
        rows = slice(i * CHUNK, (i + 1) * CHUNK)
        fill(0, wide, points_buf[rows], out_ref.at[:, rows])


def resident_part(first, count, points, centers, limit):
    m_dev, features = centers.shape

    def kernel(points_ref, *refs):
        resident_kernel(points_ref.at[pl.ds(first * CHUNK, count * CHUNK)], *refs)

    return pl.pallas_call(
        kernel,
        out_shape=jax.ShapeDtypeStruct((m_dev, count * CHUNK), bf16),
        in_specs=[ANY, ANY],
        out_specs=VMEM,
        scratch_shapes=[
            pltpu.VMEM((count * CHUNK, features), bf16),
            pltpu.VMEM((m_dev, features), bf16),
            pltpu.VMEM((m_dev, 2 * features), bf16),
            pltpu.SemaphoreType.DMA((2,)),
        ],
        compiler_params=pltpu.CompilerParams(vmem_limit_bytes=limit << 20),
        cost_estimate=pl.CostEstimate(
            flops=4 * m_dev * count * CHUNK * features,
            bytes_accessed=2 * m_dev * count * CHUNK,
            transcendentals=m_dev * count * CHUNK,
        ),
    )(points, centers)


def head_kernel(flags_ref, centers_ref, dir_ref, out_ref, rows_ref, vals_ref, sems):
    panel, features = rows_ref.shape
    outputs = vals_ref.shape[0]
    first = pltpu.make_async_copy(centers_ref.at[pl.ds(0, panel)], rows_ref, sems.at[0])
    second = pltpu.make_async_copy(dir_ref.at[:, pl.ds(0, panel)], vals_ref, sems.at[1])
    first.start()
    second.start()
    first.wait()
    second.wait()
    root = flags_ref[0] == 0
    core = flags_ref[1] % 2
    half = out_ref.shape[0]

    def piece(row):
        if row < panel:
            return rows_ref[row : row + 16]
        b, r = divmod(row - panel, outputs)
        return vals_ref[r : r + 16, b * features : (b + 1) * features].astype(bf16)

    for row in range(0, half, 16):
        x = jnp.where(core == 0, piece(row).astype(f32), piece(row + half).astype(f32))
        out_ref[row : row + 16] = jnp.where(root, x, 0.0).astype(bf16)


def head_payload(flags, centers, direction, panel):
    outputs, features = direction.shape[0], centers.shape[1]
    rows = panel + outputs * panel // features
    return pl.pallas_call(
        head_kernel,
        out_shape=jax.ShapeDtypeStruct((rows // 2, features), bf16),
        in_specs=[SMEM, ANY, ANY],
        out_specs=VMEM,
        scratch_shapes=[
            pltpu.VMEM((panel, features), bf16),
            pltpu.VMEM((outputs, panel), f32),
            pltpu.SemaphoreType.DMA((2,)),
        ],
        compiler_params=pltpu.CompilerParams(vmem_limit_bytes=60 << 20),
        name="head",
    )(flags, centers, direction)


def spread_kernel(x_ref, *refs):
    out_ref = refs[-1]
    x = x_ref[0] if len(x_ref.shape) == len(out_ref.shape) else x_ref[...]
    for i in range(out_ref.shape[0]):
        out_ref[i] = x


def spread(x, ways):
    shape = x.shape[1:] if len(x.shape) == 3 else x.shape
    return pl.pallas_call(
        spread_kernel,
        out_shape=jax.ShapeDtypeStruct((ways, *shape), x.dtype),
        in_specs=[VMEM],
        out_specs=VMEM,
        compiler_params=pltpu.CompilerParams(vmem_limit_bytes=LIMIT),
        name="spread",
    )(x)


def sum_kernel(x_ref, out_ref):
    total = x_ref[0]
    for i in range(1, x_ref.shape[0]):
        total = total + x_ref[i]
    out_ref[...] = total


def summed(x, steps=4):
    ways, rows, lanes = x.shape
    block = rows // steps
    return pl.pallas_call(
        sum_kernel,
        out_shape=jax.ShapeDtypeStruct((rows, lanes), x.dtype),
        grid=(steps,),
        in_specs=[pl.BlockSpec((ways, block, lanes), lambda i: (0, i, 0))],
        out_specs=pl.BlockSpec((block, lanes), lambda i: (i, 0)),
        compiler_params=pltpu.CompilerParams(vmem_limit_bytes=LIMIT),
        name="summed",
    )(x)


def owned_kernel(scale, x_ref, *refs):
    out_ref = refs[-1]
    total = x_ref[0]
    for i in range(1, x_ref.shape[0]):
        total = total + x_ref[i]
    total = (total * scale).astype(bf16)
    for i in range(out_ref.shape[0]):
        out_ref[i] = total


def owned_copies(x, scale, ways):
    return pl.pallas_call(
        functools.partial(owned_kernel, scale),
        out_shape=jax.ShapeDtypeStruct((ways, *x.shape[1:]), bf16),
        in_specs=[VMEM],
        out_specs=VMEM,
        compiler_params=pltpu.CompilerParams(vmem_limit_bytes=LIMIT),
        name="owned",
    )(x)


def chunk_copy(source, buffer, sems, i):
    return pltpu.make_async_copy(source.at[i], buffer.at[i], sems.at[i])


def panel_kernel(
    parts, flags_ref, centers_ref, head_ref, head_other_ref, mine_ref, other_ref, pair_ref, dir_ref,
    *refs
):
    blocks, refs = refs[:parts], refs[parts:]
    z_ref, rows_ref, high_out, both_out, zsq_ref = refs[:5]
    head, pinv, zz, high_ref, both_ref, out_sems = refs[5:]
    share = mine_ref.shape[0]
    panel = pinv.shape[0]
    outputs = dir_ref.shape[0]
    features = centers_ref.shape[1]
    at = flags_ref[1]
    core = at % 2
    far = (2 - (at - core)) * share
    pinv[pl.ds(pl.multiple_of(at * share, share), share)] = mine_ref[...]
    pinv[pl.ds(pl.multiple_of((at + 1 - 2 * core) * share, share), share)] = other_ref[...]
    pinv[pl.ds(pl.multiple_of(far + core * share, share), share)] = pair_ref[:share]
    pinv[pl.ds(pl.multiple_of(far + (1 - core) * share, share), share)] = pair_ref[share:]
    half = head_other_ref.shape[0]
    head[pl.ds(pl.multiple_of(core * half, half), half)] = head_ref[...]
    head[pl.ds(pl.multiple_of(half - core * half, half), half)] = head_other_ref[...]
    vals = jnp.concatenate(
        [head[panel + b * outputs : panel + (b + 1) * outputs] for b in range(panel // features)],
        axis=1,
    )
    z1 = lax.dot_general(vals, pinv[...], LAST, preferred_element_type=f32).astype(bf16)
    q = jnp.dot(z1, pinv[...], preferred_element_type=f32).astype(bf16)
    heads = widened(head[:panel], 1)
    tile = panel
    squares = jnp.zeros((outputs, 1), f32)
    for i in range(centers_ref.shape[0] // tile):
        rows = slice(i * tile, (i + 1) * tile)
        kp = similar(widened(centers_ref[rows], 0), heads, features)
        rows_ref[rows] = lax.dot_general(
            kp, mine_ref[...], LAST, preferred_element_type=f32
        ).astype(bf16)
        z = dir_ref[:, rows] - lax.dot_general(q, kp, LAST, preferred_element_type=f32)
        if i == 0:
            z = jnp.where(flags_ref[0] == 0, z1.astype(f32), z)
        z_ref[:, rows] = z
        squares = squares + jnp.sum(z * z, axis=1, keepdims=True)
        high = z.astype(bf16)
        zz[:outputs, rows] = high
        zz[outputs:, rows] = (z - high.astype(f32)).astype(bf16)
    zsq_ref[...] = squares
    puts = []
    done = 0
    for block in blocks:
        for i in range(block.shape[1] // CHUNK):
            chunk = block[:, i * CHUNK : (i + 1) * CHUNK]
            u = jnp.dot(zz[...], chunk, preferred_element_type=f32)
            for b in range(CHUNK // 128):
                part = u[:, b * 128 : (b + 1) * 128]
                high_ref[done + b] = part[:outputs]
                both_ref[done + b] = part[:outputs] + part[outputs:]
            span = pl.ds(done, CHUNK // 128)
            for buf, out in ((high_ref, high_out), (both_ref, both_out)):
                puts.append(
                    pltpu.make_async_copy(buf.at[span], out.at[span], out_sems.at[len(puts)])
                )
                puts[-1].start()
            done += CHUNK // 128
    for put in puts:
        put.wait()


def panel_step(flags, centers, head, head_other, mine, other, pair, direction, blocks):
    outputs, m_dev = direction.shape
    share, panel = mine.shape
    features = centers.shape[1]
    count = sum(block.shape[1] for block in blocks)
    values = jax.ShapeDtypeStruct((count // 128, outputs, 128), f32)
    return pl.pallas_call(
        functools.partial(panel_kernel, len(blocks)),
        out_shape=(
            jax.ShapeDtypeStruct((outputs, m_dev), f32),
            jax.ShapeDtypeStruct((m_dev, share), bf16),
            values,
            values,
            jax.ShapeDtypeStruct((outputs, 1), f32),
        ),
        in_specs=[SMEM] + [VMEM] * (7 + len(blocks)),
        out_specs=(VMEM, VMEM, ANY, ANY, VMEM),
        scratch_shapes=[
            pltpu.VMEM((2 * head_other.shape[0], features), bf16),
            pltpu.VMEM((panel, panel), bf16),
            pltpu.VMEM((2 * outputs, m_dev), bf16),
            pltpu.VMEM(values.shape, f32),
            pltpu.VMEM(values.shape, f32),
            pltpu.SemaphoreType.DMA((2 * count // CHUNK,)),
        ],
        compiler_params=pltpu.CompilerParams(vmem_limit_bytes=16 << 20),
        cost_estimate=pl.CostEstimate(
            flops=2 * 256 * m_dev * count,
            bytes_accessed=2 * m_dev * count,
            transcendentals=m_dev * panel,
        ),
        name="panel",
    )(flags, centers, head, head_other, mine, other, pair, direction, *blocks)


def image_kernel(
    flags_ref, tie_ref, w_ref, centers_ref, points_ref, source_ref, keep_ref, send_ref,
    blocks, made, wide, total, points_buf, sems, points_sem,
):
    stored = sems.shape[0]
    local = pltpu.make_async_copy(
        points_ref.at[pl.ds(stored * CHUNK, points_buf.shape[0])], points_buf, points_sem
    )
    local.start()
    for i in range(stored):
        chunk_copy(source_ref, blocks, sems, i).start()
    wide[...] = widened(centers_ref[...], 1)
    total[...] = jnp.zeros_like(total)
    local.wait()
    count = points_ref.shape[0] // CHUNK
    width = CHUNK // 128

    def use(i, block):
        w = jnp.concatenate([w_ref[i * width + b] for b in range(width)], axis=1)
        total[...] += jnp.dot(w, block, preferred_element_type=f32)

    def local_step(i, carry):
        rows = pl.ds(pl.multiple_of((i - stored) * CHUNK, CHUNK), CHUNK)
        fill(1, wide, points_buf[rows], made)
        use(i, made[...])
        return carry

    def stored_step(i, carry):
        chunk_copy(source_ref, blocks, sems, i).wait()
        use(i, blocks[i])
        return carry

    lax.fori_loop(stored, count, local_step, 0)
    lax.fori_loop(0, stored, stored_step, 0)
    half = keep_ref.shape[0]
    mine = pl.multiple_of((flags_ref[1] % 2) * half, half)
    keep_ref[...] = total[pl.ds(mine, half)]
    send_ref[...] = total[pl.ds(half - mine, half)]


def image(flags, tie, w, centers, points, block):
    outputs = w.shape[1]
    m_dev, features = centers.shape
    count = points.shape[0] // CHUNK
    stored = block.shape[0]
    shape = jax.ShapeDtypeStruct((outputs // 2, m_dev), f32)
    return pl.pallas_call(
        image_kernel,
        out_shape=(shape, shape),
        in_specs=[SMEM, VMEM, VMEM, VMEM, ANY, ANY],
        out_specs=(VMEM, VMEM),
        scratch_shapes=[
            pltpu.VMEM(block.shape, bf16),
            pltpu.VMEM((CHUNK, m_dev), bf16),
            pltpu.VMEM((m_dev, 2 * features), bf16),
            pltpu.VMEM((outputs, m_dev), f32),
            pltpu.VMEM(((count - stored) * CHUNK, features), bf16),
            pltpu.SemaphoreType.DMA((stored,)),
            pltpu.SemaphoreType.DMA,
        ],
        compiler_params=pltpu.CompilerParams(vmem_limit_bytes=44 << 20),
        cost_estimate=pl.CostEstimate(
            flops=2 * 256 * points.shape[0] * m_dev,
            bytes_accessed=2 * points.shape[0] * m_dev,
            transcendentals=0,
        ),
        name="image",
    )(flags, tie, w, centers, points, block)


def exchange(x, axis):
    return lax.all_to_all(x, axis, 0, 0, tiled=True)


def products_kernel(scale, ridge, count, w_ref, both_ref, z_squares_ref, res_ref, out_ref):
    outputs = w_ref.shape[1]
    total = jnp.zeros(w_ref.shape[1:], f32)
    for i in range(w_ref.shape[0]):
        total = total + w_ref[i].astype(f32) * both_ref[i]
    mine = jnp.sum(total, axis=1, keepdims=True) * scale + ridge * z_squares_ref[...]
    squares = jnp.sum(res_ref[...] * res_ref[...], axis=1, keepdims=True) * (1.0 / count)
    lane = lax.broadcasted_iota(jnp.int32, total.shape, 1)
    row = lax.broadcasted_iota(jnp.int32, total.shape, 0)
    spread_out = jnp.where(lane == row, mine, jnp.where(lane == row + outputs, squares, 0.0))
    out_ref[...] = jnp.sum(spread_out, axis=0, keepdims=True)


def products(w, both, z_squares, residual, scale, count):
    return pl.pallas_call(
        functools.partial(products_kernel, scale, RIDGE_TERM / count, count),
        out_shape=jax.ShapeDtypeStruct((1, 128), f32),
        in_specs=[VMEM] * 4,
        out_specs=VMEM,
        compiler_params=pltpu.CompilerParams(vmem_limit_bytes=LIMIT),
        name="products",
    )(w, both, z_squares, residual)


def tree_pairs(sizes):
    n_far, n_near = sizes
    stages, holders, stride = [], [0], n_near
    while stride > 1:
        stride //= 2
        stages.append([(i, i + stride) for i in holders])
        holders = holders + [i + stride for i in holders]
    stride = n_far
    while stride > 1:
        stride //= 2
        stages.append([(i, i + stride * n_near) for i in holders])
        holders = holders + [i + stride * n_near for i in holders]
    return stages


def tree_stage(x, pairs):
    return x + lax.ppermute(x, CTR, pairs)


def swap(x, bit):
    n = lax.axis_size("pts")
    return lax.ppermute(x, "pts", [(i, i ^ bit) for i in range(n)])


def final_kernel(scale, flags_ref, keep_ref, other_ref, z_ref, res_ref, sums_ref, op_ref, new_ref):
    outputs = z_ref.shape[0]
    half = keep_ref.shape[0]
    sums = jnp.sum(sums_ref[...], axis=0)
    lane = lax.broadcasted_iota(jnp.int32, (outputs, sums.shape[1]), 1)
    row = lax.broadcasted_iota(jnp.int32, (outputs, sums.shape[1]), 0)
    curvature = jnp.sum(jnp.where(lane == row, sums, 0.0), axis=1, keepdims=True)
    squares = jnp.sum(jnp.where(lane == row + outputs, sums, 0.0), axis=1, keepdims=True)
    op_ref[...] = RIDGE_TERM * z_ref[...]
    mine = pl.multiple_of((flags_ref[1] % 2) * half, half)
    op_ref[pl.ds(mine, half)] += keep_ref[...] * scale
    op_ref[pl.ds(half - mine, half)] += other_ref[...] * scale
    new_ref[...] = res_ref[...] - (squares / curvature) * op_ref[...]


def final_step(flags, keep, other, z, residual, sums, scale):
    shape = jax.ShapeDtypeStruct(z.shape, f32)
    return pl.pallas_call(
        functools.partial(final_kernel, scale),
        out_shape=(shape, shape),
        in_specs=[SMEM] + [VMEM] * 5,
        out_specs=(VMEM, VMEM),
        compiler_params=pltpu.CompilerParams(vmem_limit_bytes=LIMIT),
        name="final",
    )(flags, keep, other, z, residual, sums)


def step(points, centers, panel_inverse, direction, residual):
    n_ctr = lax.axis_size(CTR)
    n_near = lax.axis_size(NEAR)
    n_far = lax.axis_size(FAR)
    n_pts = lax.axis_size("pts")
    flags = jnp.stack([lax.axis_index(CTR), lax.axis_index("pts")])
    m_dev, _ = centers.shape
    npg = points.shape[0]
    panel = panel_inverse.shape[1]
    outputs = direction.shape[0]
    w_scale = 1.0 / (2.0 * math.sqrt(m_dev * n_ctr))
    image_scale = 1.0 / (2.0 * math.sqrt(npg * n_pts))

    head = head_payload(flags, centers, direction, panel)
    by_center = []
    first = 0
    for count, limit in ((3, 12), (3, 12), (2, 12)):
        by_center.append(resident_part(first, count, points, centers, limit))
        first += count
    for links in tree_pairs((n_far, n_near)):
        head = tree_stage(head, links)
    other = swap(panel_inverse, 1)
    pair = swap(jnp.concatenate([panel_inverse, other], axis=0), 2)
    z, panel_rows, high, both, z_squares = panel_step(
        flags, centers, head, swap(head, 1),
        panel_inverse, other, pair, direction, by_center,
    )

    parts = exchange(high.reshape(n_near, n_far * outputs, 128), NEAR)
    parts = summed(parts).reshape(n_far, outputs, 128)
    parts = exchange(parts, FAR)
    block = None
    for first, count in ((0, 5), (5, 1)):
        block = block_part(1, CHUNK, 6, first, count, points, centers, block, z_squares)
    w = exchange(owned_copies(parts, w_scale, n_far), FAR)
    w = exchange(spread(w.reshape(n_far * outputs, 128), n_near), NEAR)
    w = w.reshape(-1, outputs, 128)

    scalars = products(w, both, z_squares, residual, image_scale, n_pts)
    scalars = scalars + swap(scalars, 1)
    keep, send = image(flags, scalars, w, centers, points, block)
    scalars = scalars + swap(scalars, 2)
    sums = jnp.broadcast_to(scalars[None], (n_ctr, *scalars.shape))
    sums = exchange(sums, CTR)
    keep = keep + swap(send, 1)
    keep = keep + swap(keep, 2)
    operator_image, new_residual = final_step(
        flags, keep, swap(keep, 1), z, residual, sums, image_scale
    )
    return (panel_rows, operator_image, new_residual)


def solution(mesh):
    split = Mesh(
        mesh.devices.reshape(mesh.shape["pts"], 8, 2, 4), ("pts", "ctr_0", "ctr_1", "ctr_2")
    )
    placed = (P("pts", None), P(CTR, None), P("pts", None), P(None, CTR), P(None, CTR))
    return jax.shard_map(
        step,
        mesh=split,
        in_specs=placed,
        out_specs=(P(CTR, "pts"), P(None, CTR), P(None, CTR)),
        check_vma=False,
    )
```

```python
import functools
import math

import jax
import jax.numpy as jnp
from jax import lax
from jax.experimental import pallas as pl
from jax.experimental.pallas import tpu as pltpu
from jax.sharding import Mesh
from jax.sharding import PartitionSpec as P


CTR = ("ctr_0", "ctr_1", "ctr_2")
NEAR = ("ctr_1", "ctr_2")
FAR = "ctr_0"
RIDGE_TERM = 0.002

bf16, f32 = jnp.bfloat16, jnp.float32
LAST = (((1,), (1,)), ((), ()))
VMEM = pl.BlockSpec(memory_space=pltpu.VMEM)
SMEM = pl.BlockSpec(memory_space=pltpu.SMEM)
ANY = pl.BlockSpec(memory_space=pl.ANY)
LIMIT = 12 << 20
CHUNK = 1024
WIDTH = 256
EXTRA = 16


def widened(x, side):
    xf = x.astype(f32)
    n = jnp.sum(xf * xf, axis=1, keepdims=True)
    high = n.astype(bf16).astype(f32)
    rest = n - high
    mid = rest.astype(bf16).astype(f32)
    low = rest - mid
    lane = lax.broadcasted_iota(jnp.int32, x.shape, 1)
    if side == 0:
        extra = jnp.where(lane < 6, 1.0, 0.0)
        extra = jnp.where(lane == 0, high, extra)
        extra = jnp.where(lane == 1, mid, extra)
        extra = jnp.where(lane == 2, low, extra)
        return jnp.concatenate([x, extra.astype(bf16)], axis=1)
    extra = jnp.where(lane < 3, -1.0, 0.0)
    extra = jnp.where(lane == 3, -high, extra)
    extra = jnp.where(lane == 4, -mid, extra)
    extra = jnp.where(lane == 5, -low, extra)
    return jnp.concatenate([(xf * 2.0).astype(bf16), extra.astype(bf16)], axis=1)


def similar(a, b, features):
    t = lax.dot_general(a, b, LAST, preferred_element_type=f32)
    return jnp.exp2(t * (math.log2(math.e) / (2 * features))).astype(bf16)


def fill(side, wide, points, out):
    features = points.shape[1]
    extended = widened(points, 1 - side)
    columns = extended if side == 0 else wide
    for j in range(columns.shape[0] // WIDTH):
        cut = slice(j * WIDTH, (j + 1) * WIDTH)
        rows = wide[...] if side == 0 else extended
        out[:, cut] = similar(rows, columns[cut], features)


def block_kernel(side, size, first, count, *refs):
    points_ref, centers_ref = refs[-9:-7]
    out_ref, points_buf, centers_buf, wide, buffers, sems, in_sems = refs[-7:]
    slots = buffers.shape[0]
    loads = [
        pltpu.make_async_copy(centers_ref, centers_buf, in_sems.at[0]),
        pltpu.make_async_copy(
            points_ref.at[pl.ds(first * size, count * size)], points_buf, in_sems.at[1]
        ),
    ]
    for copy in loads:
        copy.start()
    loads[0].wait()
    wide[...] = widened(centers_buf[...], side)
    loads[1].wait()

    def put(i):
        slot = lax.rem(i, slots)
        return pltpu.make_async_copy(buffers.at[slot], out_ref.at[first + i], sems.at[slot])

    def step(i, carry):
        if count > slots:

            @pl.when(i >= slots)
            def _():
                put(i - slots).wait()

        rows = pl.ds(pl.multiple_of(i * size, size), size)
        fill(side, wide, points_buf[rows], buffers.at[lax.rem(i, slots)])
        put(i).start()
        return carry

    lax.fori_loop(0, count, step, 0)
    for i in range(max(count - slots, 0), count):
        put(jnp.int32(i)).wait()


def block_part(side, size, chunks, first, count, points, centers, made=None, tie=None):
    m_dev, features = centers.shape
    rows, columns = (m_dev, size) if side == 0 else (size, m_dev)
    slots = min(count, 2)
    extra = [x for x in (made, tie) if x is not None]
    return pl.pallas_call(
        functools.partial(block_kernel, side, size, first, count),
        out_shape=jax.ShapeDtypeStruct((chunks, rows, columns), bf16),
        in_specs=[ANY] * (len(extra) + 2),
        out_specs=ANY,
        scratch_shapes=[
            pltpu.VMEM((count * size, features), bf16),
            pltpu.VMEM((m_dev, features), bf16),
            pltpu.VMEM((m_dev, 2 * features), bf16),
            pltpu.VMEM((slots, rows, columns), bf16),
            pltpu.SemaphoreType.DMA((slots,)),
            pltpu.SemaphoreType.DMA((2,)),
        ],
        input_output_aliases={} if made is None else {0: 0},
        compiler_params=pltpu.CompilerParams(vmem_limit_bytes=60 << 20),
        cost_estimate=pl.CostEstimate(
            flops=4 * m_dev * count * size * features,
            bytes_accessed=2 * m_dev * count * size,
            transcendentals=m_dev * count * size,
        ),
    )(*extra, points, centers)


def resident_kernel(points_ref, centers_ref, out_ref, points_buf, centers_buf, wide, sems):
    loads = [
        pltpu.make_async_copy(centers_ref, centers_buf, sems.at[0]),
        pltpu.make_async_copy(points_ref, points_buf, sems.at[1]),
    ]
    for copy in loads:
        copy.start()
    for copy in loads:
        copy.wait()
    wide[...] = widened(centers_buf[...], 0)
    for i in range(points_buf.shape[0] // CHUNK):
        rows = slice(i * CHUNK, (i + 1) * CHUNK)
        fill(0, wide, points_buf[rows], out_ref.at[:, rows])


def resident_part(first, count, points, centers, limit):
    m_dev, features = centers.shape

    def kernel(points_ref, *refs):
        resident_kernel(points_ref.at[pl.ds(first * CHUNK, count * CHUNK)], *refs)

    return pl.pallas_call(
        kernel,
        out_shape=jax.ShapeDtypeStruct((m_dev, count * CHUNK), bf16),
        in_specs=[ANY, ANY],
        out_specs=VMEM,
        scratch_shapes=[
            pltpu.VMEM((count * CHUNK, features), bf16),
            pltpu.VMEM((m_dev, features), bf16),
            pltpu.VMEM((m_dev, 2 * features), bf16),
            pltpu.SemaphoreType.DMA((2,)),
        ],
        compiler_params=pltpu.CompilerParams(vmem_limit_bytes=limit << 20),
        cost_estimate=pl.CostEstimate(
            flops=4 * m_dev * count * CHUNK * features,
            bytes_accessed=2 * m_dev * count * CHUNK,
            transcendentals=m_dev * count * CHUNK,
        ),
    )(points, centers)


def head_kernel(flags_ref, centers_ref, dir_ref, out_ref, rows_ref, vals_ref, sems):
    panel, features = rows_ref.shape
    outputs = vals_ref.shape[0]
    first = pltpu.make_async_copy(centers_ref.at[pl.ds(0, panel)], rows_ref, sems.at[0])
    second = pltpu.make_async_copy(dir_ref.at[:, pl.ds(0, panel)], vals_ref, sems.at[1])
    first.start()
    second.start()
    first.wait()
    second.wait()
    root = flags_ref[0] == 0
    core = flags_ref[1] % 2
    half = out_ref.shape[0]

    def piece(row):
        if row < panel:
            return rows_ref[row : row + 16]
        b, r = divmod(row - panel, outputs)
        return vals_ref[r : r + 16, b * features : (b + 1) * features].astype(bf16)

    for row in range(0, half, 16):
        x = jnp.where(core == 0, piece(row).astype(f32), piece(row + half).astype(f32))
        out_ref[row : row + 16] = jnp.where(root, x, 0.0).astype(bf16)


def head_payload(flags, centers, direction, panel):
    outputs, features = direction.shape[0], centers.shape[1]
    rows = panel + outputs * panel // features
    return pl.pallas_call(
        head_kernel,
        out_shape=jax.ShapeDtypeStruct((rows // 2, features), bf16),
        in_specs=[SMEM, ANY, ANY],
        out_specs=VMEM,
        scratch_shapes=[
            pltpu.VMEM((panel, features), bf16),
            pltpu.VMEM((outputs, panel), f32),
            pltpu.SemaphoreType.DMA((2,)),
        ],
        compiler_params=pltpu.CompilerParams(vmem_limit_bytes=60 << 20),
        name="head",
    )(flags, centers, direction)


def pieces(x, count):
    parts = []
    for i in range(count):
        part = x.astype(bf16)
        parts.append(part)
        if i + 1 < count:
            x = x - part.astype(f32)
    return parts


def partial_sums(ref, outputs, rows=slice(None)):
    totals = None
    for i in range(ref.shape[0]):
        x = ref[i, rows].astype(f32)
        x = (x[:outputs] + x[outputs : 2 * outputs], x[2 * outputs :])
        totals = x if totals is None else (totals[0] + x[0], totals[1] + x[1])
    return totals


def sum_kernel(x_ref, out_ref):
    rows = out_ref.shape[1]
    outputs = rows // 3
    for k in range(out_ref.shape[0]):
        high, low = partial_sums(x_ref, outputs, slice(k * rows, (k + 1) * rows))
        out_ref[k] = jnp.concatenate([*pieces(high, 2), low.astype(bf16)], axis=0)


def summed(x, rows, per=2):
    ways, lanes = x.shape[0], x.shape[2]
    count = x.shape[1] // rows
    return pl.pallas_call(
        sum_kernel,
        out_shape=jax.ShapeDtypeStruct((count, rows, lanes), bf16),
        grid=(count // per,),
        in_specs=[pl.BlockSpec((ways, per * rows, lanes), lambda i: (0, i, 0))],
        out_specs=pl.BlockSpec((per, rows, lanes), lambda i: (i, 0, 0)),
        compiler_params=pltpu.CompilerParams(vmem_limit_bytes=LIMIT),
        name="summed",
    )(x)


def scalar_rows(x):
    rows = jnp.concatenate([p.astype(f32) for p in pieces(x, 3)], axis=0)
    return jnp.concatenate([rows, jnp.zeros((EXTRA - 3, x.shape[1]), f32)], axis=0).astype(bf16)


def owned_kernel(scale, image_scale, count, x_ref, z_squares_ref, res_ref, out_ref):
    outputs = z_squares_ref.shape[0]
    high, low = partial_sums(x_ref, outputs)
    w = (high * scale).astype(bf16)
    mine = jnp.sum(w.astype(f32) * (high + low), axis=1, keepdims=True) * image_scale
    mine = mine + (RIDGE_TERM / count) * z_squares_ref[...]
    squares = jnp.sum(res_ref[...] * res_ref[...], axis=1, keepdims=True) * (1.0 / count)
    lane = lax.broadcasted_iota(jnp.int32, w.shape, 1)
    row = lax.broadcasted_iota(jnp.int32, w.shape, 0)
    scalars = jnp.where(lane == row, mine, jnp.where(lane == row + outputs, squares, 0.0))
    scalars = scalar_rows(jnp.sum(scalars, axis=0, keepdims=True))
    for i in range(out_ref.shape[0]):
        out_ref[i, :outputs] = w
        out_ref[i, outputs:] = scalars


def owned_copies(x, z_squares, residual, scale, image_scale, count, ways):
    outputs, lanes = z_squares.shape[0], x.shape[2]
    return pl.pallas_call(
        functools.partial(owned_kernel, scale, image_scale, count),
        out_shape=jax.ShapeDtypeStruct((ways, outputs + EXTRA, lanes), bf16),
        in_specs=[VMEM] * 3,
        out_specs=VMEM,
        compiler_params=pltpu.CompilerParams(vmem_limit_bytes=LIMIT),
        name="owned",
    )(x, z_squares, residual)


def scalar_sum(ref, first):
    total = ref[0, first : first + EXTRA].astype(f32)
    for i in range(1, ref.shape[0]):
        total = total + ref[i, first : first + EXTRA].astype(f32)
    return jnp.sum(total, axis=0, keepdims=True)


def relay_kernel(x_ref, out_ref):
    ways, rows, _ = x_ref.shape
    outputs = rows - EXTRA
    scalars = scalar_rows(scalar_sum(x_ref, outputs))
    for i in range(out_ref.shape[0]):
        for k in range(ways):
            out_ref[i, k * outputs : (k + 1) * outputs] = x_ref[k, :outputs]
        out_ref[i, ways * outputs :] = scalars


def relay_copies(x, ways):
    count, rows, lanes = x.shape
    return pl.pallas_call(
        relay_kernel,
        out_shape=jax.ShapeDtypeStruct((ways, count * (rows - EXTRA) + EXTRA, lanes), bf16),
        in_specs=[VMEM],
        out_specs=VMEM,
        compiler_params=pltpu.CompilerParams(vmem_limit_bytes=LIMIT),
        name="relay",
    )(x)


def chunk_copy(source, buffer, sems, i):
    return pltpu.make_async_copy(source.at[i], buffer.at[i], sems.at[i])


def panel_kernel(
    parts, flags_ref, centers_ref, head_ref, head_other_ref, mine_ref, other_ref, pair_ref, dir_ref,
    *refs
):
    blocks, refs = refs[:parts], refs[parts:]
    z_ref, rows_ref, parts_out, zsq_ref = refs[:4]
    head, pinv, zz, parts_buf, out_sems = refs[4:]
    share = mine_ref.shape[0]
    panel = pinv.shape[0]
    outputs = dir_ref.shape[0]
    features = centers_ref.shape[1]
    at = flags_ref[1]
    core = at % 2
    far = (2 - (at - core)) * share
    pinv[pl.ds(pl.multiple_of(at * share, share), share)] = mine_ref[...]
    pinv[pl.ds(pl.multiple_of((at + 1 - 2 * core) * share, share), share)] = other_ref[...]
    pinv[pl.ds(pl.multiple_of(far + core * share, share), share)] = pair_ref[:share]
    pinv[pl.ds(pl.multiple_of(far + (1 - core) * share, share), share)] = pair_ref[share:]
    half = head_other_ref.shape[0]
    head[pl.ds(pl.multiple_of(core * half, half), half)] = head_ref[...]
    head[pl.ds(pl.multiple_of(half - core * half, half), half)] = head_other_ref[...]
    vals = jnp.concatenate(
        [head[panel + b * outputs : panel + (b + 1) * outputs] for b in range(panel // features)],
        axis=1,
    )
    z1 = lax.dot_general(vals, pinv[...], LAST, preferred_element_type=f32).astype(bf16)
    q = jnp.dot(z1, pinv[...], preferred_element_type=f32).astype(bf16)
    heads = widened(head[:panel], 1)
    tile = panel
    squares = jnp.zeros((outputs, 1), f32)
    for i in range(centers_ref.shape[0] // tile):
        rows = slice(i * tile, (i + 1) * tile)
        kp = similar(widened(centers_ref[rows], 0), heads, features)
        rows_ref[rows] = lax.dot_general(
            kp, mine_ref[...], LAST, preferred_element_type=f32
        ).astype(bf16)
        z = dir_ref[:, rows] - lax.dot_general(q, kp, LAST, preferred_element_type=f32)
        if i == 0:
            z = jnp.where(flags_ref[0] == 0, z1.astype(f32), z)
        z_ref[:, rows] = z
        squares = squares + jnp.sum(z * z, axis=1, keepdims=True)
        high = z.astype(bf16)
        zz[:outputs, rows] = high
        zz[outputs:, rows] = (z - high.astype(f32)).astype(bf16)
    zsq_ref[...] = squares
    puts = []
    done = 0
    for block in blocks:
        for i in range(block.shape[1] // CHUNK):
            chunk = block[:, i * CHUNK : (i + 1) * CHUNK]
            u = jnp.dot(zz[...], chunk, preferred_element_type=f32)
            for b in range(CHUNK // 128):
                part = u[:, b * 128 : (b + 1) * 128]
                parts_buf[done + b] = jnp.concatenate(
                    [*pieces(part[:outputs], 2), part[outputs:].astype(bf16)], axis=0
                )
            span = pl.ds(done, CHUNK // 128)
            puts.append(
                pltpu.make_async_copy(
                    parts_buf.at[span], parts_out.at[span], out_sems.at[len(puts)]
                )
            )
            puts[-1].start()
            done += CHUNK // 128
    for put in puts:
        put.wait()


def panel_step(flags, centers, head, head_other, mine, other, pair, direction, blocks):
    outputs, m_dev = direction.shape
    share, panel = mine.shape
    features = centers.shape[1]
    count = sum(block.shape[1] for block in blocks)
    values = jax.ShapeDtypeStruct((count // 128, 3 * outputs, 128), bf16)
    return pl.pallas_call(
        functools.partial(panel_kernel, len(blocks)),
        out_shape=(
            jax.ShapeDtypeStruct((outputs, m_dev), f32),
            jax.ShapeDtypeStruct((m_dev, share), bf16),
            values,
            jax.ShapeDtypeStruct((outputs, 1), f32),
        ),
        in_specs=[SMEM] + [VMEM] * (7 + len(blocks)),
        out_specs=(VMEM, VMEM, ANY, VMEM),
        scratch_shapes=[
            pltpu.VMEM((2 * head_other.shape[0], features), bf16),
            pltpu.VMEM((panel, panel), bf16),
            pltpu.VMEM((2 * outputs, m_dev), bf16),
            pltpu.VMEM(values.shape, bf16),
            pltpu.SemaphoreType.DMA((count // CHUNK,)),
        ],
        compiler_params=pltpu.CompilerParams(vmem_limit_bytes=16 << 20),
        cost_estimate=pl.CostEstimate(
            flops=2 * 256 * m_dev * count,
            bytes_accessed=2 * m_dev * count,
            transcendentals=m_dev * panel,
        ),
        name="panel",
    )(flags, centers, head, head_other, mine, other, pair, direction, *blocks)


def image_kernel(
    flags_ref, w_ref, centers_ref, points_ref, source_ref, keep_ref, send_ref,
    blocks, made, wide, total, points_buf, sems, points_sem,
):
    stored = sems.shape[0]
    local = pltpu.make_async_copy(
        points_ref.at[pl.ds(stored * CHUNK, points_buf.shape[0])], points_buf, points_sem
    )
    local.start()
    for i in range(stored):
        chunk_copy(source_ref, blocks, sems, i).start()
    wide[...] = widened(centers_ref[...], 1)
    total[...] = jnp.zeros_like(total)
    local.wait()
    count = points_ref.shape[0] // CHUNK
    width = CHUNK // 128
    outputs, m_dev = total.shape

    def use(i, block):
        w = jnp.concatenate(
            [w_ref[i, b * outputs : (b + 1) * outputs] for b in range(width)], axis=1
        )
        total[...] += jnp.dot(w, block, preferred_element_type=f32)

    def local_step(i, carry):
        rows = pl.ds(pl.multiple_of((i - stored) * CHUNK, CHUNK), CHUNK)
        fill(1, wide, points_buf[rows], made)
        use(i, made[...])
        return carry

    def stored_step(i, carry):
        chunk_copy(source_ref, blocks, sems, i).wait()
        use(i, blocks[i])
        return carry

    lax.fori_loop(stored, count, local_step, 0)
    lax.fori_loop(0, stored, stored_step, 0)
    half = keep_ref.shape[0]
    mine = pl.multiple_of((flags_ref[1] % 2) * half, half)
    keep_ref[:, :m_dev] = total[pl.ds(mine, half)]
    send_ref[:, :m_dev] = total[pl.ds(half - mine, half)]
    scalars = jnp.broadcast_to(scalar_sum(w_ref, width * outputs), (half, 128))
    keep_ref[:, m_dev:] = scalars
    send_ref[:, m_dev:] = scalars


def image(flags, outputs, w, centers, points, block):
    m_dev, features = centers.shape
    count = points.shape[0] // CHUNK
    stored = block.shape[0]
    shape = jax.ShapeDtypeStruct((outputs // 2, m_dev + 128), f32)
    return pl.pallas_call(
        image_kernel,
        out_shape=(shape, shape),
        in_specs=[SMEM, VMEM, VMEM, ANY, ANY],
        out_specs=(VMEM, VMEM),
        scratch_shapes=[
            pltpu.VMEM(block.shape, bf16),
            pltpu.VMEM((CHUNK, m_dev), bf16),
            pltpu.VMEM((m_dev, 2 * features), bf16),
            pltpu.VMEM((outputs, m_dev), f32),
            pltpu.VMEM(((count - stored) * CHUNK, features), bf16),
            pltpu.SemaphoreType.DMA((stored,)),
            pltpu.SemaphoreType.DMA,
        ],
        compiler_params=pltpu.CompilerParams(vmem_limit_bytes=44 << 20),
        cost_estimate=pl.CostEstimate(
            flops=2 * 256 * points.shape[0] * m_dev,
            bytes_accessed=2 * points.shape[0] * m_dev,
            transcendentals=0,
        ),
        name="image",
    )(flags, w, centers, points, block)


def exchange(x, axis):
    return lax.all_to_all(x, axis, 0, 0, tiled=True)


def tree_pairs(sizes):
    n_far, n_near = sizes
    stages, holders, stride = [], [0], n_near
    while stride > 1:
        stride //= 2
        stages.append([(i, i + stride) for i in holders])
        holders = holders + [i + stride for i in holders]
    stride = n_far
    while stride > 1:
        stride //= 2
        stages.append([(i, i + stride * n_near) for i in holders])
        holders = holders + [i + stride * n_near for i in holders]
    return stages


def tree_stage(x, pairs):
    return x + lax.ppermute(x, CTR, pairs)


def swap(x, bit):
    n = lax.axis_size("pts")
    return lax.ppermute(x, "pts", [(i, i ^ bit) for i in range(n)])


def final_kernel(scale, flags_ref, keep_ref, other_ref, z_ref, res_ref, op_ref, new_ref):
    outputs, m_dev = z_ref.shape
    half = keep_ref.shape[0]
    sums = keep_ref[0:1, m_dev:]
    lane = lax.broadcasted_iota(jnp.int32, (outputs, sums.shape[1]), 1)
    row = lax.broadcasted_iota(jnp.int32, (outputs, sums.shape[1]), 0)
    curvature = jnp.sum(jnp.where(lane == row, sums, 0.0), axis=1, keepdims=True)
    squares = jnp.sum(jnp.where(lane == row + outputs, sums, 0.0), axis=1, keepdims=True)
    op_ref[...] = RIDGE_TERM * z_ref[...]
    mine = pl.multiple_of((flags_ref[1] % 2) * half, half)
    op_ref[pl.ds(mine, half)] += keep_ref[:, :m_dev] * scale
    op_ref[pl.ds(half - mine, half)] += other_ref[:, :m_dev] * scale
    new_ref[...] = res_ref[...] - (squares / curvature) * op_ref[...]


def final_step(flags, keep, other, z, residual, scale):
    shape = jax.ShapeDtypeStruct(z.shape, f32)
    return pl.pallas_call(
        functools.partial(final_kernel, scale),
        out_shape=(shape, shape),
        in_specs=[SMEM] + [VMEM] * 4,
        out_specs=(VMEM, VMEM),
        compiler_params=pltpu.CompilerParams(vmem_limit_bytes=LIMIT),
        name="final",
    )(flags, keep, other, z, residual)


def step(points, centers, panel_inverse, direction, residual):
    n_ctr = lax.axis_size(CTR)
    n_near = lax.axis_size(NEAR)
    n_far = lax.axis_size(FAR)
    n_pts = lax.axis_size("pts")
    flags = jnp.stack([lax.axis_index(CTR), lax.axis_index("pts")])
    m_dev, _ = centers.shape
    npg = points.shape[0]
    panel = panel_inverse.shape[1]
    outputs = direction.shape[0]
    w_scale = 1.0 / (2.0 * math.sqrt(m_dev * n_ctr))
    image_scale = 1.0 / (2.0 * math.sqrt(npg * n_pts))

    head = head_payload(flags, centers, direction, panel)
    by_center = []
    first = 0
    for count, limit in ((3, 12), (3, 12), (2, 12)):
        by_center.append(resident_part(first, count, points, centers, limit))
        first += count
    for links in tree_pairs((n_far, n_near)):
        head = tree_stage(head, links)
    other = swap(panel_inverse, 1)
    pair = swap(jnp.concatenate([panel_inverse, other], axis=0), 2)
    z, panel_rows, parts, z_squares = panel_step(
        flags, centers, head, swap(head, 1),
        panel_inverse, other, pair, direction, by_center,
    )

    rows = 3 * outputs
    parts = exchange(parts.reshape(n_near, n_far * rows, 128), NEAR)
    parts = exchange(summed(parts, rows), FAR)
    block = None
    for first, count in ((0, 5), (5, 1)):
        block = block_part(1, CHUNK, 6, first, count, points, centers, block, z_squares)
    w = owned_copies(parts, z_squares, residual, w_scale, image_scale, n_pts, n_far)
    w = exchange(w, FAR)
    w = exchange(relay_copies(w, n_near), NEAR)

    keep, send = image(flags, outputs, w, centers, points, block)
    keep = keep + swap(send, 1)
    keep = keep + swap(keep, 2)
    operator_image, new_residual = final_step(flags, keep, swap(keep, 1), z, residual, image_scale)
    return (panel_rows, operator_image, new_residual)


def solution(mesh):
    split = Mesh(
        mesh.devices.reshape(mesh.shape["pts"], 8, 2, 4), ("pts", "ctr_0", "ctr_1", "ctr_2")
    )
    placed = (P("pts", None), P(CTR, None), P("pts", None), P(None, CTR), P(None, CTR))
    return jax.shard_map(
        step,
        mesh=split,
        in_specs=placed,
        out_specs=(P(CTR, "pts"), P(None, CTR), P(None, CTR)),
        check_vma=False,
    )
```

```python
import functools
import math

import jax
import jax.numpy as jnp
from jax import lax
from jax.experimental import pallas as pl
from jax.experimental.pallas import tpu as pltpu
from jax.sharding import Mesh
from jax.sharding import PartitionSpec as P


CTR = ("ctr_0", "ctr_1", "ctr_2")
NEAR = ("ctr_1", "ctr_2")
FAR = "ctr_0"
RIDGE_TERM = 0.002

bf16, f32 = jnp.bfloat16, jnp.float32
LAST = (((1,), (1,)), ((), ()))
VMEM = pl.BlockSpec(memory_space=pltpu.VMEM)
SMEM = pl.BlockSpec(memory_space=pltpu.SMEM)
ANY = pl.BlockSpec(memory_space=pl.ANY)
LIMIT = 12 << 20
CHUNK = 1024
WIDTH = 256
EXTRA = 16


def widened(x, side):
    xf = x.astype(f32)
    n = jnp.sum(xf * xf, axis=1, keepdims=True)
    high = n.astype(bf16).astype(f32)
    rest = n - high
    mid = rest.astype(bf16).astype(f32)
    low = rest - mid
    lane = lax.broadcasted_iota(jnp.int32, x.shape, 1)
    if side == 0:
        extra = jnp.where(lane < 6, 1.0, 0.0)
        extra = jnp.where(lane == 0, high, extra)
        extra = jnp.where(lane == 1, mid, extra)
        extra = jnp.where(lane == 2, low, extra)
        return jnp.concatenate([x, extra.astype(bf16)], axis=1)
    extra = jnp.where(lane < 3, -1.0, 0.0)
    extra = jnp.where(lane == 3, -high, extra)
    extra = jnp.where(lane == 4, -mid, extra)
    extra = jnp.where(lane == 5, -low, extra)
    return jnp.concatenate([(xf * 2.0).astype(bf16), extra.astype(bf16)], axis=1)


def similar(a, b, features):
    t = lax.dot_general(a, b, LAST, preferred_element_type=f32)
    return jnp.exp2(t * (math.log2(math.e) / (2 * features))).astype(bf16)


def fill(side, wide, points, out):
    features = points.shape[1]
    extended = widened(points, 1 - side)
    columns = extended if side == 0 else wide
    for j in range(columns.shape[0] // WIDTH):
        cut = slice(j * WIDTH, (j + 1) * WIDTH)
        rows = wide[...] if side == 0 else extended
        out[:, cut] = similar(rows, columns[cut], features)


def block_kernel(side, size, first, count, *refs):
    points_ref, centers_ref = refs[-9:-7]
    out_ref, points_buf, centers_buf, wide, buffers, sems, in_sems = refs[-7:]
    slots = buffers.shape[0]
    loads = [
        pltpu.make_async_copy(centers_ref, centers_buf, in_sems.at[0]),
        pltpu.make_async_copy(
            points_ref.at[pl.ds(first * size, count * size)], points_buf, in_sems.at[1]
        ),
    ]
    for copy in loads:
        copy.start()
    loads[0].wait()
    wide[...] = widened(centers_buf[...], side)
    loads[1].wait()

    def put(i):
        slot = lax.rem(i, slots)
        return pltpu.make_async_copy(buffers.at[slot], out_ref.at[first + i], sems.at[slot])

    def step(i, carry):
        if count > slots:

            @pl.when(i >= slots)
            def _():
                put(i - slots).wait()

        rows = pl.ds(pl.multiple_of(i * size, size), size)
        fill(side, wide, points_buf[rows], buffers.at[lax.rem(i, slots)])
        put(i).start()
        return carry

    lax.fori_loop(0, count, step, 0)
    for i in range(max(count - slots, 0), count):
        put(jnp.int32(i)).wait()


def block_part(side, size, chunks, first, count, points, centers, made=None, tie=None):
    m_dev, features = centers.shape
    rows, columns = (m_dev, size) if side == 0 else (size, m_dev)
    slots = min(count, 2)
    extra = [x for x in (made, tie) if x is not None]
    return pl.pallas_call(
        functools.partial(block_kernel, side, size, first, count),
        out_shape=jax.ShapeDtypeStruct((chunks, rows, columns), bf16),
        in_specs=[ANY] * (len(extra) + 2),
        out_specs=ANY,
        scratch_shapes=[
            pltpu.VMEM((count * size, features), bf16),
            pltpu.VMEM((m_dev, features), bf16),
            pltpu.VMEM((m_dev, 2 * features), bf16),
            pltpu.VMEM((slots, rows, columns), bf16),
            pltpu.SemaphoreType.DMA((slots,)),
            pltpu.SemaphoreType.DMA((2,)),
        ],
        input_output_aliases={} if made is None else {0: 0},
        compiler_params=pltpu.CompilerParams(vmem_limit_bytes=60 << 20),
        cost_estimate=pl.CostEstimate(
            flops=4 * m_dev * count * size * features,
            bytes_accessed=2 * m_dev * count * size,
            transcendentals=m_dev * count * size,
        ),
    )(*extra, points, centers)


def resident_kernel(points_ref, centers_ref, out_ref, points_buf, centers_buf, wide, sems):
    loads = [
        pltpu.make_async_copy(centers_ref, centers_buf, sems.at[0]),
        pltpu.make_async_copy(points_ref, points_buf, sems.at[1]),
    ]
    for copy in loads:
        copy.start()
    for copy in loads:
        copy.wait()
    wide[...] = widened(centers_buf[...], 0)
    for i in range(points_buf.shape[0] // CHUNK):
        rows = slice(i * CHUNK, (i + 1) * CHUNK)
        fill(0, wide, points_buf[rows], out_ref.at[:, rows])


def resident_part(first, count, points, centers, limit):
    m_dev, features = centers.shape

    def kernel(points_ref, *refs):
        resident_kernel(points_ref.at[pl.ds(first * CHUNK, count * CHUNK)], *refs)

    return pl.pallas_call(
        kernel,
        out_shape=jax.ShapeDtypeStruct((m_dev, count * CHUNK), bf16),
        in_specs=[ANY, ANY],
        out_specs=VMEM,
        scratch_shapes=[
            pltpu.VMEM((count * CHUNK, features), bf16),
            pltpu.VMEM((m_dev, features), bf16),
            pltpu.VMEM((m_dev, 2 * features), bf16),
            pltpu.SemaphoreType.DMA((2,)),
        ],
        compiler_params=pltpu.CompilerParams(vmem_limit_bytes=limit << 20),
        cost_estimate=pl.CostEstimate(
            flops=4 * m_dev * count * CHUNK * features,
            bytes_accessed=2 * m_dev * count * CHUNK,
            transcendentals=m_dev * count * CHUNK,
        ),
    )(points, centers)


def head_kernel(flags_ref, centers_ref, dir_ref, out_ref, rows_ref, vals_ref, sems):
    panel, features = rows_ref.shape
    outputs = vals_ref.shape[0]
    first = pltpu.make_async_copy(centers_ref.at[pl.ds(0, panel)], rows_ref, sems.at[0])
    second = pltpu.make_async_copy(dir_ref.at[:, pl.ds(0, panel)], vals_ref, sems.at[1])
    first.start()
    second.start()
    first.wait()
    second.wait()
    root = flags_ref[0] == 0
    core = flags_ref[1] % 2
    half = out_ref.shape[0]

    def piece(row):
        if row < panel:
            return rows_ref[row : row + 16]
        b, r = divmod(row - panel, outputs)
        return vals_ref[r : r + 16, b * features : (b + 1) * features].astype(bf16)

    for row in range(0, half, 16):
        x = jnp.where(core == 0, piece(row).astype(f32), piece(row + half).astype(f32))
        out_ref[row : row + 16] = jnp.where(root, x, 0.0).astype(bf16)


def head_payload(flags, centers, direction, panel):
    outputs, features = direction.shape[0], centers.shape[1]
    rows = panel + outputs * panel // features
    return pl.pallas_call(
        head_kernel,
        out_shape=jax.ShapeDtypeStruct((rows // 2, features), bf16),
        in_specs=[SMEM, ANY, ANY],
        out_specs=VMEM,
        scratch_shapes=[
            pltpu.VMEM((panel, features), bf16),
            pltpu.VMEM((outputs, panel), f32),
            pltpu.SemaphoreType.DMA((2,)),
        ],
        compiler_params=pltpu.CompilerParams(vmem_limit_bytes=60 << 20),
        name="head",
    )(flags, centers, direction)


def pieces(x, count):
    parts = []
    for i in range(count):
        part = x.astype(bf16)
        parts.append(part)
        if i + 1 < count:
            x = x - part.astype(f32)
    return parts


def partial_sums(ref, outputs, rows=slice(None)):
    totals = None
    for i in range(ref.shape[0]):
        x = ref[i, rows].astype(f32)
        x = (x[:outputs] + x[outputs : 2 * outputs], x[2 * outputs :])
        totals = x if totals is None else (totals[0] + x[0], totals[1] + x[1])
    return totals


def sum_kernel(x_ref, out_ref):
    rows = out_ref.shape[1]
    outputs = rows // 3
    for k in range(out_ref.shape[0]):
        high, low = partial_sums(x_ref, outputs, slice(k * rows, (k + 1) * rows))
        out_ref[k] = jnp.concatenate([*pieces(high, 2), low.astype(bf16)], axis=0)


def summed(x, rows, per=2):
    ways, lanes = x.shape[0], x.shape[2]
    count = x.shape[1] // rows
    return pl.pallas_call(
        sum_kernel,
        out_shape=jax.ShapeDtypeStruct((count, rows, lanes), bf16),
        grid=(count // per,),
        in_specs=[pl.BlockSpec((ways, per * rows, lanes), lambda i: (0, i, 0))],
        out_specs=pl.BlockSpec((per, rows, lanes), lambda i: (i, 0, 0)),
        compiler_params=pltpu.CompilerParams(vmem_limit_bytes=LIMIT),
        name="summed",
    )(x)


def scalar_rows(x):
    rows = jnp.concatenate([p.astype(f32) for p in pieces(x, 3)], axis=0)
    return jnp.concatenate([rows, jnp.zeros((EXTRA - 3, x.shape[1]), f32)], axis=0).astype(bf16)


def owned_kernel(scale, image_scale, count, x_ref, z_ref, res_ref, out_ref):
    outputs = z_ref.shape[0]
    high, low = partial_sums(x_ref, outputs)
    w = (high * scale).astype(bf16)
    mine = jnp.sum(w.astype(f32) * (high + low), axis=1, keepdims=True) * image_scale
    z_squares = jnp.sum(z_ref[...] * z_ref[...], axis=1, keepdims=True)
    mine = mine + (RIDGE_TERM / count) * z_squares
    squares = jnp.sum(res_ref[...] * res_ref[...], axis=1, keepdims=True) * (1.0 / count)
    lane = lax.broadcasted_iota(jnp.int32, w.shape, 1)
    row = lax.broadcasted_iota(jnp.int32, w.shape, 0)
    scalars = jnp.where(lane == row, mine, jnp.where(lane == row + outputs, squares, 0.0))
    scalars = scalar_rows(jnp.sum(scalars, axis=0, keepdims=True))
    for i in range(out_ref.shape[0]):
        out_ref[i, :outputs] = w
        out_ref[i, outputs:] = scalars


def owned_copies(x, z, residual, scale, image_scale, count, ways):
    outputs, lanes = z.shape[0], x.shape[2]
    return pl.pallas_call(
        functools.partial(owned_kernel, scale, image_scale, count),
        out_shape=jax.ShapeDtypeStruct((ways, outputs + EXTRA, lanes), bf16),
        in_specs=[VMEM] * 3,
        out_specs=VMEM,
        compiler_params=pltpu.CompilerParams(vmem_limit_bytes=LIMIT),
        name="owned",
    )(x, z, residual)


def scalar_sum(ref, first):
    total = ref[0, first : first + EXTRA].astype(f32)
    for i in range(1, ref.shape[0]):
        total = total + ref[i, first : first + EXTRA].astype(f32)
    return jnp.sum(total, axis=0, keepdims=True)


def relay_kernel(x_ref, out_ref):
    ways, rows, _ = x_ref.shape
    outputs = rows - EXTRA
    scalars = scalar_rows(scalar_sum(x_ref, outputs))
    for i in range(out_ref.shape[0]):
        for k in range(ways):
            out_ref[i, k * outputs : (k + 1) * outputs] = x_ref[k, :outputs]
        out_ref[i, ways * outputs :] = scalars


def relay_copies(x, ways):
    count, rows, lanes = x.shape
    return pl.pallas_call(
        relay_kernel,
        out_shape=jax.ShapeDtypeStruct((ways, count * (rows - EXTRA) + EXTRA, lanes), bf16),
        in_specs=[VMEM],
        out_specs=VMEM,
        compiler_params=pltpu.CompilerParams(vmem_limit_bytes=LIMIT),
        name="relay",
    )(x)


def chunk_copy(source, buffer, sems, i):
    return pltpu.make_async_copy(source.at[i], buffer.at[i], sems.at[i])


def panel_kernel(
    parts, flags_ref, centers_ref, head_ref, head_other_ref, mine_ref, other_ref, pair_ref, dir_ref,
    *refs
):
    blocks, refs = refs[:parts], refs[parts:]
    z_ref, rows_ref, parts_out = refs[:3]
    head, pinv, zz, parts_buf, out_sems = refs[3:]
    share = mine_ref.shape[0]
    panel = pinv.shape[0]
    outputs = dir_ref.shape[0]
    features = centers_ref.shape[1]
    at = flags_ref[1]
    core = at % 2
    far = (2 - (at - core)) * share
    pinv[pl.ds(pl.multiple_of(at * share, share), share)] = mine_ref[...]
    pinv[pl.ds(pl.multiple_of((at + 1 - 2 * core) * share, share), share)] = other_ref[...]
    pinv[pl.ds(pl.multiple_of(far + core * share, share), share)] = pair_ref[:share]
    pinv[pl.ds(pl.multiple_of(far + (1 - core) * share, share), share)] = pair_ref[share:]
    half = head_other_ref.shape[0]
    head[pl.ds(pl.multiple_of(core * half, half), half)] = head_ref[...]
    head[pl.ds(pl.multiple_of(half - core * half, half), half)] = head_other_ref[...]
    vals = jnp.concatenate(
        [head[panel + b * outputs : panel + (b + 1) * outputs] for b in range(panel // features)],
        axis=1,
    )
    z1 = lax.dot_general(vals, pinv[...], LAST, preferred_element_type=f32).astype(bf16)
    q = jnp.dot(z1, pinv[...], preferred_element_type=f32).astype(bf16)
    heads = widened(head[:panel], 1)
    tile = panel
    for i in range(centers_ref.shape[0] // tile):
        rows = slice(i * tile, (i + 1) * tile)
        kp = similar(widened(centers_ref[rows], 0), heads, features)
        rows_ref[rows] = lax.dot_general(
            kp, mine_ref[...], LAST, preferred_element_type=f32
        ).astype(bf16)
        z = dir_ref[:, rows] - lax.dot_general(q, kp, LAST, preferred_element_type=f32)
        if i == 0:
            z = jnp.where(flags_ref[0] == 0, z1.astype(f32), z)
        z_ref[:, rows] = z
        high = z.astype(bf16)
        zz[:outputs, rows] = high
        zz[outputs:, rows] = (z - high.astype(f32)).astype(bf16)
    puts = []
    done = 0
    for block in blocks:
        for i in range(block.shape[1] // CHUNK):
            chunk = block[:, i * CHUNK : (i + 1) * CHUNK]
            u = jnp.dot(zz[...], chunk, preferred_element_type=f32)
            for b in range(CHUNK // 128):
                part = u[:, b * 128 : (b + 1) * 128]
                parts_buf[done + b] = jnp.concatenate(
                    [*pieces(part[:outputs], 2), part[outputs:].astype(bf16)], axis=0
                )
            span = pl.ds(done, CHUNK // 128)
            puts.append(
                pltpu.make_async_copy(
                    parts_buf.at[span], parts_out.at[span], out_sems.at[len(puts)]
                )
            )
            puts[-1].start()
            done += CHUNK // 128
    for put in puts:
        put.wait()


def panel_step(flags, centers, head, head_other, mine, other, pair, direction, blocks):
    outputs, m_dev = direction.shape
    share, panel = mine.shape
    features = centers.shape[1]
    count = sum(block.shape[1] for block in blocks)
    values = jax.ShapeDtypeStruct((count // 128, 3 * outputs, 128), bf16)
    return pl.pallas_call(
        functools.partial(panel_kernel, len(blocks)),
        out_shape=(
            jax.ShapeDtypeStruct((outputs, m_dev), f32),
            jax.ShapeDtypeStruct((m_dev, share), bf16),
            values,
        ),
        in_specs=[SMEM] + [VMEM] * (7 + len(blocks)),
        out_specs=(VMEM, VMEM, ANY),
        scratch_shapes=[
            pltpu.VMEM((2 * head_other.shape[0], features), bf16),
            pltpu.VMEM((panel, panel), bf16),
            pltpu.VMEM((2 * outputs, m_dev), bf16),
            pltpu.VMEM(values.shape, bf16),
            pltpu.SemaphoreType.DMA((count // CHUNK,)),
        ],
        compiler_params=pltpu.CompilerParams(vmem_limit_bytes=16 << 20),
        cost_estimate=pl.CostEstimate(
            flops=2 * 256 * m_dev * count,
            bytes_accessed=2 * m_dev * count,
            transcendentals=m_dev * panel,
        ),
        name="panel",
    )(flags, centers, head, head_other, mine, other, pair, direction, *blocks)


def image_kernel(
    flags_ref, w_ref, centers_ref, points_ref, source_ref, keep_ref, send_ref,
    blocks, made, wide, total, points_buf, sems, points_sem,
):
    stored = sems.shape[0]
    local = pltpu.make_async_copy(
        points_ref.at[pl.ds(stored * CHUNK, points_buf.shape[0])], points_buf, points_sem
    )
    local.start()
    for i in range(stored):
        chunk_copy(source_ref, blocks, sems, i).start()
    wide[...] = widened(centers_ref[...], 1)
    total[...] = jnp.zeros_like(total)
    local.wait()
    count = points_ref.shape[0] // CHUNK
    width = CHUNK // 128
    outputs, m_dev = total.shape

    def use(i, block):
        w = jnp.concatenate(
            [w_ref[i, b * outputs : (b + 1) * outputs] for b in range(width)], axis=1
        )
        total[...] += jnp.dot(w, block, preferred_element_type=f32)

    def local_step(i, carry):
        rows = pl.ds(pl.multiple_of((i - stored) * CHUNK, CHUNK), CHUNK)
        fill(1, wide, points_buf[rows], made)
        use(i, made[...])
        return carry

    def stored_step(i, carry):
        chunk_copy(source_ref, blocks, sems, i).wait()
        use(i, blocks[i])
        return carry

    lax.fori_loop(stored, count, local_step, 0)
    lax.fori_loop(0, stored, stored_step, 0)
    half = keep_ref.shape[0]
    mine = pl.multiple_of((flags_ref[1] % 2) * half, half)
    keep_ref[:, :m_dev] = total[pl.ds(mine, half)]
    send_ref[:, :m_dev] = total[pl.ds(half - mine, half)]
    scalars = jnp.broadcast_to(scalar_sum(w_ref, width * outputs), (half, 128))
    keep_ref[:, m_dev:] = scalars
    send_ref[:, m_dev:] = scalars


def image(flags, outputs, w, centers, points, block):
    m_dev, features = centers.shape
    count = points.shape[0] // CHUNK
    stored = block.shape[0]
    shape = jax.ShapeDtypeStruct((outputs // 2, m_dev + 128), f32)
    return pl.pallas_call(
        image_kernel,
        out_shape=(shape, shape),
        in_specs=[SMEM, VMEM, VMEM, ANY, ANY],
        out_specs=(VMEM, VMEM),
        scratch_shapes=[
            pltpu.VMEM(block.shape, bf16),
            pltpu.VMEM((CHUNK, m_dev), bf16),
            pltpu.VMEM((m_dev, 2 * features), bf16),
            pltpu.VMEM((outputs, m_dev), f32),
            pltpu.VMEM(((count - stored) * CHUNK, features), bf16),
            pltpu.SemaphoreType.DMA((stored,)),
            pltpu.SemaphoreType.DMA,
        ],
        compiler_params=pltpu.CompilerParams(vmem_limit_bytes=44 << 20),
        cost_estimate=pl.CostEstimate(
            flops=2 * 256 * points.shape[0] * m_dev,
            bytes_accessed=2 * points.shape[0] * m_dev,
            transcendentals=0,
        ),
        name="image",
    )(flags, w, centers, points, block)


def exchange(x, axis):
    return lax.all_to_all(x, axis, 0, 0, tiled=True)


def tree_pairs(sizes):
    n_far, n_near = sizes
    stages, holders, stride = [], [0], n_near
    while stride > 1:
        stride //= 2
        stages.append([(i, i + stride) for i in holders])
        holders = holders + [i + stride for i in holders]
    stride = n_far
    while stride > 1:
        stride //= 2
        stages.append([(i, i + stride * n_near) for i in holders])
        holders = holders + [i + stride * n_near for i in holders]
    return stages


def tree_stage(x, pairs):
    return x + lax.ppermute(x, CTR, pairs)


def swap(x, bit):
    n = lax.axis_size("pts")
    return lax.ppermute(x, "pts", [(i, i ^ bit) for i in range(n)])


def final_kernel(scale, flags_ref, keep_ref, other_ref, z_ref, res_ref, op_ref, new_ref):
    outputs, m_dev = z_ref.shape
    half = keep_ref.shape[0]
    sums = keep_ref[0:1, m_dev:]
    lane = lax.broadcasted_iota(jnp.int32, (outputs, sums.shape[1]), 1)
    row = lax.broadcasted_iota(jnp.int32, (outputs, sums.shape[1]), 0)
    curvature = jnp.sum(jnp.where(lane == row, sums, 0.0), axis=1, keepdims=True)
    squares = jnp.sum(jnp.where(lane == row + outputs, sums, 0.0), axis=1, keepdims=True)
    op_ref[...] = RIDGE_TERM * z_ref[...]
    mine = pl.multiple_of((flags_ref[1] % 2) * half, half)
    op_ref[pl.ds(mine, half)] += keep_ref[:, :m_dev] * scale
    op_ref[pl.ds(half - mine, half)] += other_ref[:, :m_dev] * scale
    new_ref[...] = res_ref[...] - (squares / curvature) * op_ref[...]


def final_step(flags, keep, other, z, residual, scale):
    shape = jax.ShapeDtypeStruct(z.shape, f32)
    return pl.pallas_call(
        functools.partial(final_kernel, scale),
        out_shape=(shape, shape),
        in_specs=[SMEM] + [VMEM] * 4,
        out_specs=(VMEM, VMEM),
        compiler_params=pltpu.CompilerParams(vmem_limit_bytes=LIMIT),
        name="final",
    )(flags, keep, other, z, residual)


def step(points, centers, panel_inverse, direction, residual):
    n_ctr = lax.axis_size(CTR)
    n_near = lax.axis_size(NEAR)
    n_far = lax.axis_size(FAR)
    n_pts = lax.axis_size("pts")
    flags = jnp.stack([lax.axis_index(CTR), lax.axis_index("pts")])
    m_dev, _ = centers.shape
    npg = points.shape[0]
    panel = panel_inverse.shape[1]
    outputs = direction.shape[0]
    w_scale = 1.0 / (2.0 * math.sqrt(m_dev * n_ctr))
    image_scale = 1.0 / (2.0 * math.sqrt(npg * n_pts))

    head = head_payload(flags, centers, direction, panel)
    by_center = []
    first = 0
    for count in (2, 2, 2, 2):
        by_center.append(resident_part(first, count, points, centers, 12))
        first += count
    for links in tree_pairs((n_far, n_near)):
        head = tree_stage(head, links)
    other = swap(panel_inverse, 1)
    pair = swap(jnp.concatenate([panel_inverse, other], axis=0), 2)
    z, panel_rows, parts = panel_step(
        flags, centers, head, swap(head, 1),
        panel_inverse, other, pair, direction, by_center,
    )

    rows = 3 * outputs
    parts = exchange(parts.reshape(n_near, n_far * rows, 128), NEAR)
    parts = exchange(summed(parts, rows), FAR)
    block = None
    for first, count in ((0, 5), (5, 1)):
        block = block_part(1, CHUNK, 6, first, count, points, centers, block)
    w = owned_copies(parts, z, residual, w_scale, image_scale, n_pts, n_far)
    w = exchange(w, FAR)
    w = exchange(relay_copies(w, n_near), NEAR)

    keep, send = image(flags, outputs, w, centers, points, block)
    keep = keep + swap(send, 1)
    keep = keep + swap(keep, 2)
    operator_image, new_residual = final_step(flags, keep, swap(keep, 1), z, residual, image_scale)
    return (panel_rows, operator_image, new_residual)


def solution(mesh):
    split = Mesh(
        mesh.devices.reshape(mesh.shape["pts"], 8, 2, 4), ("pts", "ctr_0", "ctr_1", "ctr_2")
    )
    placed = (P("pts", None), P(CTR, None), P("pts", None), P(None, CTR), P(None, CTR))
    return jax.shard_map(
        step,
        mesh=split,
        in_specs=placed,
        out_specs=(P(CTR, "pts"), P(None, CTR), P(None, CTR)),
        check_vma=False,
    )
```

```python
import functools
import math

import jax
import jax.numpy as jnp
from jax import lax
from jax.experimental import pallas as pl
from jax.experimental.pallas import tpu as pltpu
from jax.sharding import Mesh
from jax.sharding import PartitionSpec as P


CTR = ("ctr_0", "ctr_1", "ctr_2")
NEAR = ("ctr_1", "ctr_2")
FAR = "ctr_0"
RIDGE_TERM = 0.002

bf16, f32 = jnp.bfloat16, jnp.float32
LAST = (((1,), (1,)), ((), ()))
VMEM = pl.BlockSpec(memory_space=pltpu.VMEM)
SMEM = pl.BlockSpec(memory_space=pltpu.SMEM)
ANY = pl.BlockSpec(memory_space=pl.ANY)
LIMIT = 12 << 20
CHUNK = 1024
WIDTH = 256
EXTRA = 16


def widened(x, side):
    xf = x.astype(f32)
    n = jnp.sum(xf * xf, axis=1, keepdims=True)
    high = n.astype(bf16).astype(f32)
    rest = n - high
    mid = rest.astype(bf16).astype(f32)
    low = rest - mid
    lane = lax.broadcasted_iota(jnp.int32, x.shape, 1)
    if side == 0:
        extra = jnp.where(lane < 6, 1.0, 0.0)
        extra = jnp.where(lane == 0, high, extra)
        extra = jnp.where(lane == 1, mid, extra)
        extra = jnp.where(lane == 2, low, extra)
        return jnp.concatenate([x, extra.astype(bf16)], axis=1)
    extra = jnp.where(lane < 3, -1.0, 0.0)
    extra = jnp.where(lane == 3, -high, extra)
    extra = jnp.where(lane == 4, -mid, extra)
    extra = jnp.where(lane == 5, -low, extra)
    return jnp.concatenate([(xf * 2.0).astype(bf16), extra.astype(bf16)], axis=1)


def similar(a, b, features):
    t = lax.dot_general(a, b, LAST, preferred_element_type=f32)
    return jnp.exp2(t * (math.log2(math.e) / (2 * features))).astype(bf16)


def fill(side, wide, points, out):
    features = points.shape[1]
    extended = widened(points, 1 - side)
    columns = extended if side == 0 else wide
    for j in range(columns.shape[0] // WIDTH):
        cut = slice(j * WIDTH, (j + 1) * WIDTH)
        rows = wide[...] if side == 0 else extended
        out[:, cut] = similar(rows, columns[cut], features)


def block_kernel(side, size, first, count, *refs):
    points_ref, centers_ref = refs[-9:-7]
    out_ref, points_buf, centers_buf, wide, buffers, sems, in_sems = refs[-7:]
    slots = buffers.shape[0]
    loads = [
        pltpu.make_async_copy(centers_ref, centers_buf, in_sems.at[0]),
        pltpu.make_async_copy(
            points_ref.at[pl.ds(first * size, count * size)], points_buf, in_sems.at[1]
        ),
    ]
    for copy in loads:
        copy.start()
    loads[0].wait()
    wide[...] = widened(centers_buf[...], side)
    loads[1].wait()

    def put(i):
        slot = lax.rem(i, slots)
        return pltpu.make_async_copy(buffers.at[slot], out_ref.at[first + i], sems.at[slot])

    def step(i, carry):
        if count > slots:

            @pl.when(i >= slots)
            def _():
                put(i - slots).wait()

        rows = pl.ds(pl.multiple_of(i * size, size), size)
        fill(side, wide, points_buf[rows], buffers.at[lax.rem(i, slots)])
        put(i).start()
        return carry

    lax.fori_loop(0, count, step, 0)
    for i in range(max(count - slots, 0), count):
        put(jnp.int32(i)).wait()


def block_part(side, size, chunks, first, count, points, centers, made=None, tie=None):
    m_dev, features = centers.shape
    rows, columns = (m_dev, size) if side == 0 else (size, m_dev)
    slots = min(count, 2)
    extra = [x for x in (made, tie) if x is not None]
    return pl.pallas_call(
        functools.partial(block_kernel, side, size, first, count),
        out_shape=jax.ShapeDtypeStruct((chunks, rows, columns), bf16),
        in_specs=[ANY] * (len(extra) + 2),
        out_specs=ANY,
        scratch_shapes=[
            pltpu.VMEM((count * size, features), bf16),
            pltpu.VMEM((m_dev, features), bf16),
            pltpu.VMEM((m_dev, 2 * features), bf16),
            pltpu.VMEM((slots, rows, columns), bf16),
            pltpu.SemaphoreType.DMA((slots,)),
            pltpu.SemaphoreType.DMA((2,)),
        ],
        input_output_aliases={} if made is None else {0: 0},
        compiler_params=pltpu.CompilerParams(vmem_limit_bytes=60 << 20),
        cost_estimate=pl.CostEstimate(
            flops=4 * m_dev * count * size * features,
            bytes_accessed=2 * m_dev * count * size,
            transcendentals=m_dev * count * size,
        ),
    )(*extra, points, centers)


def resident_kernel(points_ref, centers_ref, out_ref, points_buf, centers_buf, wide, sems):
    loads = [
        pltpu.make_async_copy(centers_ref, centers_buf, sems.at[0]),
        pltpu.make_async_copy(points_ref, points_buf, sems.at[1]),
    ]
    for copy in loads:
        copy.start()
    for copy in loads:
        copy.wait()
    wide[...] = widened(centers_buf[...], 0)
    for i in range(points_buf.shape[0] // CHUNK):
        rows = slice(i * CHUNK, (i + 1) * CHUNK)
        fill(0, wide, points_buf[rows], out_ref.at[:, rows])


def resident_part(first, count, points, centers, limit):
    m_dev, features = centers.shape

    def kernel(points_ref, *refs):
        resident_kernel(points_ref.at[pl.ds(first * CHUNK, count * CHUNK)], *refs)

    return pl.pallas_call(
        kernel,
        out_shape=jax.ShapeDtypeStruct((m_dev, count * CHUNK), bf16),
        in_specs=[ANY, ANY],
        out_specs=VMEM,
        scratch_shapes=[
            pltpu.VMEM((count * CHUNK, features), bf16),
            pltpu.VMEM((m_dev, features), bf16),
            pltpu.VMEM((m_dev, 2 * features), bf16),
            pltpu.SemaphoreType.DMA((2,)),
        ],
        compiler_params=pltpu.CompilerParams(vmem_limit_bytes=limit << 20),
        cost_estimate=pl.CostEstimate(
            flops=4 * m_dev * count * CHUNK * features,
            bytes_accessed=2 * m_dev * count * CHUNK,
            transcendentals=m_dev * count * CHUNK,
        ),
    )(points, centers)


def head_kernel(flags_ref, centers_ref, dir_ref, out_ref, rows_ref, vals_ref, sems):
    panel, features = rows_ref.shape
    outputs = vals_ref.shape[0]
    first = pltpu.make_async_copy(centers_ref.at[pl.ds(0, panel)], rows_ref, sems.at[0])
    second = pltpu.make_async_copy(dir_ref.at[:, pl.ds(0, panel)], vals_ref, sems.at[1])
    first.start()
    second.start()
    first.wait()
    second.wait()
    root = flags_ref[0] == 0
    core = flags_ref[1] % 2
    half = out_ref.shape[0]

    def piece(row):
        if row < panel:
            return rows_ref[row : row + 16]
        b, r = divmod(row - panel, outputs)
        return vals_ref[r : r + 16, b * features : (b + 1) * features].astype(bf16)

    for row in range(0, half, 16):
        x = jnp.where(core == 0, piece(row).astype(f32), piece(row + half).astype(f32))
        out_ref[row : row + 16] = jnp.where(root, x, 0.0).astype(bf16)


def head_payload(flags, centers, direction, panel):
    outputs, features = direction.shape[0], centers.shape[1]
    rows = panel + outputs * panel // features
    return pl.pallas_call(
        head_kernel,
        out_shape=jax.ShapeDtypeStruct((rows // 2, features), bf16),
        in_specs=[SMEM, ANY, ANY],
        out_specs=VMEM,
        scratch_shapes=[
            pltpu.VMEM((panel, features), bf16),
            pltpu.VMEM((outputs, panel), f32),
            pltpu.SemaphoreType.DMA((2,)),
        ],
        compiler_params=pltpu.CompilerParams(vmem_limit_bytes=60 << 20),
        name="head",
    )(flags, centers, direction)


def pieces(x, count):
    parts = []
    for i in range(count):
        part = x.astype(bf16)
        parts.append(part)
        if i + 1 < count:
            x = x - part.astype(f32)
    return parts


def partial_sums(ref, outputs, rows=slice(None)):
    totals = None
    for i in range(ref.shape[0]):
        x = ref[i, rows].astype(f32)
        x = (x[:outputs] + x[outputs : 2 * outputs], x[2 * outputs :])
        totals = x if totals is None else (totals[0] + x[0], totals[1] + x[1])
    return totals


def sum_kernel(x_ref, out_ref):
    rows = out_ref.shape[1]
    outputs = rows // 3
    for k in range(out_ref.shape[0]):
        high, low = partial_sums(x_ref, outputs, slice(k * rows, (k + 1) * rows))
        out_ref[k] = jnp.concatenate([*pieces(high, 2), low.astype(bf16)], axis=0)


def summed(x, rows, per=2):
    ways, lanes = x.shape[0], x.shape[2]
    count = x.shape[1] // rows
    return pl.pallas_call(
        sum_kernel,
        out_shape=jax.ShapeDtypeStruct((count, rows, lanes), bf16),
        grid=(count // per,),
        in_specs=[pl.BlockSpec((ways, per * rows, lanes), lambda i: (0, i, 0))],
        out_specs=pl.BlockSpec((per, rows, lanes), lambda i: (i, 0, 0)),
        compiler_params=pltpu.CompilerParams(vmem_limit_bytes=LIMIT),
        name="summed",
    )(x)


def scalar_rows(x):
    rows = jnp.concatenate([p.astype(f32) for p in pieces(x, 3)], axis=0)
    return jnp.concatenate([rows, jnp.zeros((EXTRA - 3, x.shape[1]), f32)], axis=0).astype(bf16)


def owned_kernel(scale, image_scale, count, x_ref, z_ref, res_ref, out_ref):
    outputs = z_ref.shape[0]
    high, low = partial_sums(x_ref, outputs)
    w = (high * scale).astype(bf16)
    mine = jnp.sum(w.astype(f32) * (high + low), axis=1, keepdims=True) * image_scale
    z_squares = jnp.sum(z_ref[...] * z_ref[...], axis=1, keepdims=True)
    mine = mine + (RIDGE_TERM / count) * z_squares
    squares = jnp.sum(res_ref[...] * res_ref[...], axis=1, keepdims=True) * (1.0 / count)
    lane = lax.broadcasted_iota(jnp.int32, w.shape, 1)
    row = lax.broadcasted_iota(jnp.int32, w.shape, 0)
    scalars = jnp.where(lane == row, mine, jnp.where(lane == row + outputs, squares, 0.0))
    scalars = scalar_rows(jnp.sum(scalars, axis=0, keepdims=True))
    for i in range(out_ref.shape[0]):
        out_ref[i, :outputs] = w
        out_ref[i, outputs:] = scalars


def owned_copies(x, z, residual, scale, image_scale, count, ways):
    outputs, lanes = z.shape[0], x.shape[2]
    return pl.pallas_call(
        functools.partial(owned_kernel, scale, image_scale, count),
        out_shape=jax.ShapeDtypeStruct((ways, outputs + EXTRA, lanes), bf16),
        in_specs=[VMEM] * 3,
        out_specs=VMEM,
        compiler_params=pltpu.CompilerParams(vmem_limit_bytes=LIMIT),
        name="owned",
    )(x, z, residual)


def scalar_sum(ref, first):
    total = ref[0, first : first + EXTRA].astype(f32)
    for i in range(1, ref.shape[0]):
        total = total + ref[i, first : first + EXTRA].astype(f32)
    return jnp.sum(total, axis=0, keepdims=True)


def relay_kernel(x_ref, out_ref):
    ways, rows, _ = x_ref.shape
    outputs = rows - EXTRA
    scalars = scalar_rows(scalar_sum(x_ref, outputs))
    for i in range(out_ref.shape[0]):
        for k in range(ways):
            out_ref[i, k * outputs : (k + 1) * outputs] = x_ref[k, :outputs]
        out_ref[i, ways * outputs :] = scalars


def relay_copies(x, ways):
    count, rows, lanes = x.shape
    return pl.pallas_call(
        relay_kernel,
        out_shape=jax.ShapeDtypeStruct((ways, count * (rows - EXTRA) + EXTRA, lanes), bf16),
        in_specs=[VMEM],
        out_specs=VMEM,
        compiler_params=pltpu.CompilerParams(vmem_limit_bytes=LIMIT),
        name="relay",
    )(x)


def chunk_copy(source, buffer, sems, i):
    return pltpu.make_async_copy(source.at[i], buffer.at[i], sems.at[i])


def panel_kernel(
    parts, flags_ref, centers_ref, head_ref, head_other_ref, mine_ref, other_ref, pair_ref, dir_ref,
    *refs
):
    blocks, refs = refs[:parts], refs[parts:]
    z_ref, rows_ref, parts_out = refs[:3]
    head, pinv, zz, parts_buf, out_sems = refs[3:]
    share = mine_ref.shape[0]
    panel = pinv.shape[0]
    outputs = dir_ref.shape[0]
    features = centers_ref.shape[1]
    at = flags_ref[1]
    core = at % 2
    far = (2 - (at - core)) * share
    pinv[pl.ds(pl.multiple_of(at * share, share), share)] = mine_ref[...]
    pinv[pl.ds(pl.multiple_of((at + 1 - 2 * core) * share, share), share)] = other_ref[...]
    pinv[pl.ds(pl.multiple_of(far + core * share, share), share)] = pair_ref[:share]
    pinv[pl.ds(pl.multiple_of(far + (1 - core) * share, share), share)] = pair_ref[share:]
    half = head_other_ref.shape[0]
    head[pl.ds(pl.multiple_of(core * half, half), half)] = head_ref[...]
    head[pl.ds(pl.multiple_of(half - core * half, half), half)] = head_other_ref[...]
    vals = jnp.concatenate(
        [head[panel + b * outputs : panel + (b + 1) * outputs] for b in range(panel // features)],
        axis=1,
    )
    z1 = lax.dot_general(vals, pinv[...], LAST, preferred_element_type=f32).astype(bf16)
    q = jnp.dot(z1, pinv[...], preferred_element_type=f32).astype(bf16)
    heads = widened(head[:panel], 1)
    tile = panel
    for i in range(centers_ref.shape[0] // tile):
        rows = slice(i * tile, (i + 1) * tile)
        kp = similar(widened(centers_ref[rows], 0), heads, features)
        rows_ref[rows] = lax.dot_general(
            kp, mine_ref[...], LAST, preferred_element_type=f32
        ).astype(bf16)
        z = dir_ref[:, rows] - lax.dot_general(q, kp, LAST, preferred_element_type=f32)
        if i == 0:
            z = jnp.where(flags_ref[0] == 0, z1.astype(f32), z)
        z_ref[:, rows] = z
        high = z.astype(bf16)
        zz[:outputs, rows] = high
        zz[outputs:, rows] = (z - high.astype(f32)).astype(bf16)
    puts = []
    done = 0
    for block in blocks:
        for i in range(block.shape[1] // CHUNK):
            chunk = block[:, i * CHUNK : (i + 1) * CHUNK]
            u = jnp.dot(zz[...], chunk, preferred_element_type=f32)
            for b in range(CHUNK // 128):
                part = u[:, b * 128 : (b + 1) * 128]
                parts_buf[done + b] = jnp.concatenate(
                    [*pieces(part[:outputs], 2), part[outputs:].astype(bf16)], axis=0
                )
            span = pl.ds(done, CHUNK // 128)
            puts.append(
                pltpu.make_async_copy(
                    parts_buf.at[span], parts_out.at[span], out_sems.at[len(puts)]
                )
            )
            puts[-1].start()
            done += CHUNK // 128
    for put in puts:
        put.wait()


def panel_step(flags, centers, head, head_other, mine, other, pair, direction, blocks):
    outputs, m_dev = direction.shape
    share, panel = mine.shape
    features = centers.shape[1]
    count = sum(block.shape[1] for block in blocks)
    values = jax.ShapeDtypeStruct((count // 128, 3 * outputs, 128), bf16)
    return pl.pallas_call(
        functools.partial(panel_kernel, len(blocks)),
        out_shape=(
            jax.ShapeDtypeStruct((outputs, m_dev), f32),
            jax.ShapeDtypeStruct((m_dev, share), bf16),
            values,
        ),
        in_specs=[SMEM] + [VMEM] * (7 + len(blocks)),
        out_specs=(VMEM, VMEM, ANY),
        scratch_shapes=[
            pltpu.VMEM((2 * head_other.shape[0], features), bf16),
            pltpu.VMEM((panel, panel), bf16),
            pltpu.VMEM((2 * outputs, m_dev), bf16),
            pltpu.VMEM(values.shape, bf16),
            pltpu.SemaphoreType.DMA((count // CHUNK,)),
        ],
        compiler_params=pltpu.CompilerParams(vmem_limit_bytes=16 << 20),
        cost_estimate=pl.CostEstimate(
            flops=2 * 256 * m_dev * count,
            bytes_accessed=2 * m_dev * count,
            transcendentals=m_dev * panel,
        ),
        name="panel",
    )(flags, centers, head, head_other, mine, other, pair, direction, *blocks)


def image_kernel(
    flags_ref, w_ref, centers_ref, points_ref, source_ref, keep_ref, send_ref,
    blocks, made, wide, total, points_buf, sems, points_sem,
):
    stored = sems.shape[0]
    local = pltpu.make_async_copy(
        points_ref.at[pl.ds(stored * CHUNK, points_buf.shape[0])], points_buf, points_sem
    )
    local.start()
    for i in range(stored):
        chunk_copy(source_ref, blocks, sems, i).start()
    wide[...] = widened(centers_ref[...], 1)
    total[...] = jnp.zeros_like(total)
    local.wait()
    count = points_ref.shape[0] // CHUNK
    width = CHUNK // 128
    outputs, m_dev = total.shape

    def use(i, block):
        w = jnp.concatenate(
            [w_ref[i, b * outputs : (b + 1) * outputs] for b in range(width)], axis=1
        )
        total[...] += jnp.dot(w, block, preferred_element_type=f32)

    def local_step(i, carry):
        rows = pl.ds(pl.multiple_of((i - stored) * CHUNK, CHUNK), CHUNK)
        fill(1, wide, points_buf[rows], made)
        use(i, made[...])
        return carry

    def stored_step(i, carry):
        chunk_copy(source_ref, blocks, sems, i).wait()
        use(i, blocks[i])
        return carry

    lax.fori_loop(stored, count, local_step, 0)
    lax.fori_loop(0, stored, stored_step, 0)
    half = keep_ref.shape[0]
    mine = pl.multiple_of((flags_ref[1] % 2) * half, half)
    keep_ref[:, :m_dev] = total[pl.ds(mine, half)]
    send_ref[:, :m_dev] = total[pl.ds(half - mine, half)]
    scalars = jnp.broadcast_to(scalar_sum(w_ref, width * outputs), (half, 128))
    keep_ref[:, m_dev:] = scalars
    send_ref[:, m_dev:] = scalars


def image(flags, outputs, w, centers, points, block):
    m_dev, features = centers.shape
    count = points.shape[0] // CHUNK
    stored = block.shape[0]
    shape = jax.ShapeDtypeStruct((outputs // 2, m_dev + 128), f32)
    return pl.pallas_call(
        image_kernel,
        out_shape=(shape, shape),
        in_specs=[SMEM, VMEM, VMEM, ANY, ANY],
        out_specs=(VMEM, VMEM),
        scratch_shapes=[
            pltpu.VMEM(block.shape, bf16),
            pltpu.VMEM((CHUNK, m_dev), bf16),
            pltpu.VMEM((m_dev, 2 * features), bf16),
            pltpu.VMEM((outputs, m_dev), f32),
            pltpu.VMEM(((count - stored) * CHUNK, features), bf16),
            pltpu.SemaphoreType.DMA((stored,)),
            pltpu.SemaphoreType.DMA,
        ],
        compiler_params=pltpu.CompilerParams(vmem_limit_bytes=44 << 20),
        cost_estimate=pl.CostEstimate(
            flops=2 * 256 * points.shape[0] * m_dev,
            bytes_accessed=2 * points.shape[0] * m_dev,
            transcendentals=0,
        ),
        name="image",
    )(flags, w, centers, points, block)


def exchange(x, axis):
    return lax.all_to_all(x, axis, 0, 0, tiled=True)


def tree_pairs(sizes):
    n_far, n_near = sizes
    stages, holders, stride = [], [0], n_near
    while stride > 1:
        stride //= 2
        stages.append([(i, i + stride) for i in holders])
        holders = holders + [i + stride for i in holders]
    stride = n_far
    while stride > 1:
        stride //= 2
        stages.append([(i, i + stride * n_near) for i in holders])
        holders = holders + [i + stride * n_near for i in holders]
    return stages


def tree_stage(x, pairs):
    return x + lax.ppermute(x, CTR, pairs)


def swap(x, bit):
    n = lax.axis_size("pts")
    return lax.ppermute(x, "pts", [(i, i ^ bit) for i in range(n)])


def final_kernel(scale, flags_ref, keep_ref, other_ref, z_ref, res_ref, op_ref, new_ref):
    outputs, m_dev = z_ref.shape
    half = keep_ref.shape[0]
    sums = keep_ref[0:1, m_dev:]
    lane = lax.broadcasted_iota(jnp.int32, (outputs, sums.shape[1]), 1)
    row = lax.broadcasted_iota(jnp.int32, (outputs, sums.shape[1]), 0)
    curvature = jnp.sum(jnp.where(lane == row, sums, 0.0), axis=1, keepdims=True)
    squares = jnp.sum(jnp.where(lane == row + outputs, sums, 0.0), axis=1, keepdims=True)
    op_ref[...] = RIDGE_TERM * z_ref[...]
    mine = pl.multiple_of((flags_ref[1] % 2) * half, half)
    op_ref[pl.ds(mine, half)] += keep_ref[:, :m_dev] * scale
    op_ref[pl.ds(half - mine, half)] += other_ref[:, :m_dev] * scale
    new_ref[...] = res_ref[...] - (squares / curvature) * op_ref[...]


def final_step(flags, keep, other, z, residual, scale):
    shape = jax.ShapeDtypeStruct(z.shape, f32)
    return pl.pallas_call(
        functools.partial(final_kernel, scale),
        out_shape=(shape, shape),
        in_specs=[SMEM] + [VMEM] * 4,
        out_specs=(VMEM, VMEM),
        compiler_params=pltpu.CompilerParams(vmem_limit_bytes=LIMIT),
        name="final",
    )(flags, keep, other, z, residual)


def step(points, centers, panel_inverse, direction, residual):
    n_ctr = lax.axis_size(CTR)
    n_near = lax.axis_size(NEAR)
    n_far = lax.axis_size(FAR)
    n_pts = lax.axis_size("pts")
    flags = jnp.stack([lax.axis_index(CTR), lax.axis_index("pts")])
    m_dev, _ = centers.shape
    npg = points.shape[0]
    panel = panel_inverse.shape[1]
    outputs = direction.shape[0]
    w_scale = 1.0 / (2.0 * math.sqrt(m_dev * n_ctr))
    image_scale = 1.0 / (2.0 * math.sqrt(npg * n_pts))

    head = head_payload(flags, centers, direction, panel)
    by_center = []
    first = 0
    for count in (2, 3, 3):
        by_center.append(resident_part(first, count, points, centers, 12))
        first += count
    for links in tree_pairs((n_far, n_near)):
        head = tree_stage(head, links)
    other = swap(panel_inverse, 1)
    pair = swap(jnp.concatenate([panel_inverse, other], axis=0), 2)
    z, panel_rows, parts = panel_step(
        flags, centers, head, swap(head, 1),
        panel_inverse, other, pair, direction, by_center,
    )

    rows = 3 * outputs
    parts = exchange(parts.reshape(n_near, n_far * rows, 128), NEAR)
    parts = exchange(summed(parts, rows), FAR)
    block = block_part(1, CHUNK, 6, 0, 6, points, centers)
    w = owned_copies(parts, z, residual, w_scale, image_scale, n_pts, n_far)
    w = exchange(w, FAR)
    w = exchange(relay_copies(w, n_near), NEAR)

    keep, send = image(flags, outputs, w, centers, points, block)
    keep = keep + swap(send, 1)
    keep = keep + swap(keep, 2)
    operator_image, new_residual = final_step(flags, keep, swap(keep, 1), z, residual, image_scale)
    return (panel_rows, operator_image, new_residual)


def solution(mesh):
    split = Mesh(
        mesh.devices.reshape(mesh.shape["pts"], 8, 2, 4), ("pts", "ctr_0", "ctr_1", "ctr_2")
    )
    placed = (P("pts", None), P(CTR, None), P("pts", None), P(None, CTR), P(None, CTR))
    return jax.shard_map(
        step,
        mesh=split,
        in_specs=placed,
        out_specs=(P(CTR, "pts"), P(None, CTR), P(None, CTR)),
        check_vma=False,
    )
```

```python
import functools
import math

import jax
import jax.numpy as jnp
from jax import lax
from jax.experimental import pallas as pl
from jax.experimental.pallas import tpu as pltpu
from jax.sharding import Mesh
from jax.sharding import PartitionSpec as P


CTR = ("ctr_0", "ctr_1", "ctr_2")
NEAR = ("ctr_1", "ctr_2")
FAR = "ctr_0"
RIDGE_TERM = 0.002

bf16, f32 = jnp.bfloat16, jnp.float32
LAST = (((1,), (1,)), ((), ()))
VMEM = pl.BlockSpec(memory_space=pltpu.VMEM)
SMEM = pl.BlockSpec(memory_space=pltpu.SMEM)
ANY = pl.BlockSpec(memory_space=pl.ANY)
LIMIT = 12 << 20
CHUNK = 1024
WIDTH = 256
EXTRA = 16


def widened(x, side):
    xf = x.astype(f32)
    n = jnp.sum(xf * xf, axis=1, keepdims=True)
    high = n.astype(bf16).astype(f32)
    rest = n - high
    mid = rest.astype(bf16).astype(f32)
    low = rest - mid
    lane = lax.broadcasted_iota(jnp.int32, x.shape, 1)
    if side == 0:
        extra = jnp.where(lane < 6, 1.0, 0.0)
        extra = jnp.where(lane == 0, high, extra)
        extra = jnp.where(lane == 1, mid, extra)
        extra = jnp.where(lane == 2, low, extra)
        return jnp.concatenate([x, extra.astype(bf16)], axis=1)
    extra = jnp.where(lane < 3, -1.0, 0.0)
    extra = jnp.where(lane == 3, -high, extra)
    extra = jnp.where(lane == 4, -mid, extra)
    extra = jnp.where(lane == 5, -low, extra)
    return jnp.concatenate([(xf * 2.0).astype(bf16), extra.astype(bf16)], axis=1)


def similar(a, b, features):
    t = lax.dot_general(a, b, LAST, preferred_element_type=f32)
    return jnp.exp2(t * (math.log2(math.e) / (2 * features))).astype(bf16)


def fill(side, wide, points, out):
    features = points.shape[1]
    extended = widened(points, 1 - side)
    columns = extended if side == 0 else wide
    for j in range(columns.shape[0] // WIDTH):
        cut = slice(j * WIDTH, (j + 1) * WIDTH)
        rows = wide[...] if side == 0 else extended
        out[:, cut] = similar(rows, columns[cut], features)


def block_kernel(side, size, first, count, *refs):
    points_ref, centers_ref = refs[-9:-7]
    out_ref, points_buf, centers_buf, wide, buffers, sems, in_sems = refs[-7:]
    slots = buffers.shape[0]
    loads = [
        pltpu.make_async_copy(centers_ref, centers_buf, in_sems.at[0]),
        pltpu.make_async_copy(
            points_ref.at[pl.ds(first * size, count * size)], points_buf, in_sems.at[1]
        ),
    ]
    for copy in loads:
        copy.start()
    loads[0].wait()
    wide[...] = widened(centers_buf[...], side)
    loads[1].wait()

    def put(i):
        slot = lax.rem(i, slots)
        return pltpu.make_async_copy(buffers.at[slot], out_ref.at[first + i], sems.at[slot])

    def step(i, carry):
        if count > slots:

            @pl.when(i >= slots)
            def _():
                put(i - slots).wait()

        rows = pl.ds(pl.multiple_of(i * size, size), size)
        fill(side, wide, points_buf[rows], buffers.at[lax.rem(i, slots)])
        put(i).start()
        return carry

    lax.fori_loop(0, count, step, 0)
    for i in range(max(count - slots, 0), count):
        put(jnp.int32(i)).wait()


def block_part(side, size, chunks, first, count, points, centers, made=None, tie=None):
    m_dev, features = centers.shape
    rows, columns = (m_dev, size) if side == 0 else (size, m_dev)
    slots = min(count, 2)
    extra = [x for x in (made, tie) if x is not None]
    return pl.pallas_call(
        functools.partial(block_kernel, side, size, first, count),
        out_shape=jax.ShapeDtypeStruct((chunks, rows, columns), bf16),
        in_specs=[ANY] * (len(extra) + 2),
        out_specs=ANY,
        scratch_shapes=[
            pltpu.VMEM((count * size, features), bf16),
            pltpu.VMEM((m_dev, features), bf16),
            pltpu.VMEM((m_dev, 2 * features), bf16),
            pltpu.VMEM((slots, rows, columns), bf16),
            pltpu.SemaphoreType.DMA((slots,)),
            pltpu.SemaphoreType.DMA((2,)),
        ],
        input_output_aliases={} if made is None else {0: 0},
        compiler_params=pltpu.CompilerParams(vmem_limit_bytes=60 << 20),
        cost_estimate=pl.CostEstimate(
            flops=4 * m_dev * count * size * features,
            bytes_accessed=2 * m_dev * count * size,
            transcendentals=m_dev * count * size,
        ),
    )(*extra, points, centers)


def wide_kernel(points_ref, centers_ref, out_ref):
    out_ref[...] = widened(centers_ref[...], 0)


def wide_centers(points, centers):
    m_dev, features = centers.shape
    return pl.pallas_call(
        wide_kernel,
        out_shape=jax.ShapeDtypeStruct((m_dev, 2 * features), bf16),
        in_specs=[VMEM, VMEM],
        out_specs=VMEM,
        compiler_params=pltpu.CompilerParams(vmem_limit_bytes=LIMIT),
        name="wide",
    )(points, centers)


def resident_kernel(first, points_ref, wide_ref, out_ref):
    for i in range(out_ref.shape[1] // CHUNK):
        rows = slice((first + i) * CHUNK, (first + i + 1) * CHUNK)
        fill(0, wide_ref, points_ref[rows], out_ref.at[:, i * CHUNK : (i + 1) * CHUNK])


def resident_part(first, count, points, wide):
    m_dev, features = wide.shape
    return pl.pallas_call(
        functools.partial(resident_kernel, first),
        out_shape=jax.ShapeDtypeStruct((m_dev, count * CHUNK), bf16),
        in_specs=[VMEM, VMEM],
        out_specs=VMEM,
        compiler_params=pltpu.CompilerParams(vmem_limit_bytes=LIMIT),
        cost_estimate=pl.CostEstimate(
            flops=2 * m_dev * count * CHUNK * features,
            bytes_accessed=2 * m_dev * count * CHUNK,
            transcendentals=m_dev * count * CHUNK,
        ),
    )(points, wide)


def head_kernel(flags_ref, centers_ref, dir_ref, out_ref, rows_ref, vals_ref, sems):
    panel, features = rows_ref.shape
    outputs = vals_ref.shape[0]
    first = pltpu.make_async_copy(centers_ref.at[pl.ds(0, panel)], rows_ref, sems.at[0])
    second = pltpu.make_async_copy(dir_ref.at[:, pl.ds(0, panel)], vals_ref, sems.at[1])
    first.start()
    second.start()
    first.wait()
    second.wait()
    root = flags_ref[0] == 0
    core = flags_ref[1] % 2
    half = out_ref.shape[0]

    def piece(row):
        if row < panel:
            return rows_ref[row : row + 16]
        b, r = divmod(row - panel, outputs)
        return vals_ref[r : r + 16, b * features : (b + 1) * features].astype(bf16)

    for row in range(0, half, 16):
        x = jnp.where(core == 0, piece(row).astype(f32), piece(row + half).astype(f32))
        out_ref[row : row + 16] = jnp.where(root, x, 0.0).astype(bf16)


def head_payload(flags, centers, direction, panel):
    outputs, features = direction.shape[0], centers.shape[1]
    rows = panel + outputs * panel // features
    return pl.pallas_call(
        head_kernel,
        out_shape=jax.ShapeDtypeStruct((rows // 2, features), bf16),
        in_specs=[SMEM, ANY, ANY],
        out_specs=VMEM,
        scratch_shapes=[
            pltpu.VMEM((panel, features), bf16),
            pltpu.VMEM((outputs, panel), f32),
            pltpu.SemaphoreType.DMA((2,)),
        ],
        compiler_params=pltpu.CompilerParams(vmem_limit_bytes=60 << 20),
        name="head",
    )(flags, centers, direction)


def pieces(x, count):
    parts = []
    for i in range(count):
        part = x.astype(bf16)
        parts.append(part)
        if i + 1 < count:
            x = x - part.astype(f32)
    return parts


def partial_sums(ref, outputs, rows=slice(None)):
    totals = None
    for i in range(ref.shape[0]):
        x = ref[i, rows].astype(f32)
        x = (x[:outputs] + x[outputs : 2 * outputs], x[2 * outputs :])
        totals = x if totals is None else (totals[0] + x[0], totals[1] + x[1])
    return totals


def sum_kernel(x_ref, out_ref):
    rows = out_ref.shape[1]
    outputs = rows // 3
    for k in range(out_ref.shape[0]):
        high, low = partial_sums(x_ref, outputs, slice(k * rows, (k + 1) * rows))
        out_ref[k] = jnp.concatenate([*pieces(high, 2), low.astype(bf16)], axis=0)


def summed(x, rows, per=2):
    ways, lanes = x.shape[0], x.shape[2]
    count = x.shape[1] // rows
    return pl.pallas_call(
        sum_kernel,
        out_shape=jax.ShapeDtypeStruct((count, rows, lanes), bf16),
        grid=(count // per,),
        in_specs=[pl.BlockSpec((ways, per * rows, lanes), lambda i: (0, i, 0))],
        out_specs=pl.BlockSpec((per, rows, lanes), lambda i: (i, 0, 0)),
        compiler_params=pltpu.CompilerParams(vmem_limit_bytes=LIMIT),
        name="summed",
    )(x)


def scalar_rows(x):
    rows = jnp.concatenate([p.astype(f32) for p in pieces(x, 3)], axis=0)
    return jnp.concatenate([rows, jnp.zeros((EXTRA - 3, x.shape[1]), f32)], axis=0).astype(bf16)


def owned_kernel(scale, image_scale, count, x_ref, z_ref, res_ref, out_ref):
    outputs = z_ref.shape[0]
    high, low = partial_sums(x_ref, outputs)
    w = (high * scale).astype(bf16)
    mine = jnp.sum(w.astype(f32) * (high + low), axis=1, keepdims=True) * image_scale
    z_squares = jnp.sum(z_ref[...] * z_ref[...], axis=1, keepdims=True)
    mine = mine + (RIDGE_TERM / count) * z_squares
    squares = jnp.sum(res_ref[...] * res_ref[...], axis=1, keepdims=True) * (1.0 / count)
    lane = lax.broadcasted_iota(jnp.int32, w.shape, 1)
    row = lax.broadcasted_iota(jnp.int32, w.shape, 0)
    scalars = jnp.where(lane == row, mine, jnp.where(lane == row + outputs, squares, 0.0))
    scalars = scalar_rows(jnp.sum(scalars, axis=0, keepdims=True))
    for i in range(out_ref.shape[0]):
        out_ref[i, :outputs] = w
        out_ref[i, outputs:] = scalars


def owned_copies(x, z, residual, scale, image_scale, count, ways):
    outputs, lanes = z.shape[0], x.shape[2]
    return pl.pallas_call(
        functools.partial(owned_kernel, scale, image_scale, count),
        out_shape=jax.ShapeDtypeStruct((ways, outputs + EXTRA, lanes), bf16),
        in_specs=[VMEM] * 3,
        out_specs=VMEM,
        compiler_params=pltpu.CompilerParams(vmem_limit_bytes=LIMIT),
        name="owned",
    )(x, z, residual)


def scalar_sum(ref, first):
    total = ref[0, first : first + EXTRA].astype(f32)
    for i in range(1, ref.shape[0]):
        total = total + ref[i, first : first + EXTRA].astype(f32)
    return jnp.sum(total, axis=0, keepdims=True)


def relay_kernel(x_ref, out_ref):
    ways, rows, _ = x_ref.shape
    outputs = rows - EXTRA
    scalars = scalar_rows(scalar_sum(x_ref, outputs))
    for i in range(out_ref.shape[0]):
        for k in range(ways):
            out_ref[i, k * outputs : (k + 1) * outputs] = x_ref[k, :outputs]
        out_ref[i, ways * outputs :] = scalars


def relay_copies(x, ways):
    count, rows, lanes = x.shape
    return pl.pallas_call(
        relay_kernel,
        out_shape=jax.ShapeDtypeStruct((ways, count * (rows - EXTRA) + EXTRA, lanes), bf16),
        in_specs=[VMEM],
        out_specs=VMEM,
        compiler_params=pltpu.CompilerParams(vmem_limit_bytes=LIMIT),
        name="relay",
    )(x)


def chunk_copy(source, buffer, sems, i):
    return pltpu.make_async_copy(source.at[i], buffer.at[i], sems.at[i])


def panel_kernel(
    parts, flags_ref, centers_ref, head_ref, head_other_ref, mine_ref, other_ref, pair_ref, dir_ref,
    *refs
):
    blocks, refs = refs[:parts], refs[parts:]
    z_ref, rows_ref, parts_out = refs[:3]
    head, pinv, zz, parts_buf, out_sems = refs[3:]
    share = mine_ref.shape[0]
    panel = pinv.shape[0]
    outputs = dir_ref.shape[0]
    features = centers_ref.shape[1]
    at = flags_ref[1]
    core = at % 2
    far = (2 - (at - core)) * share
    pinv[pl.ds(pl.multiple_of(at * share, share), share)] = mine_ref[...]
    pinv[pl.ds(pl.multiple_of((at + 1 - 2 * core) * share, share), share)] = other_ref[...]
    pinv[pl.ds(pl.multiple_of(far + core * share, share), share)] = pair_ref[:share]
    pinv[pl.ds(pl.multiple_of(far + (1 - core) * share, share), share)] = pair_ref[share:]
    half = head_other_ref.shape[0]
    head[pl.ds(pl.multiple_of(core * half, half), half)] = head_ref[...]
    head[pl.ds(pl.multiple_of(half - core * half, half), half)] = head_other_ref[...]
    vals = jnp.concatenate(
        [head[panel + b * outputs : panel + (b + 1) * outputs] for b in range(panel // features)],
        axis=1,
    )
    z1 = lax.dot_general(vals, pinv[...], LAST, preferred_element_type=f32).astype(bf16)
    q = jnp.dot(z1, pinv[...], preferred_element_type=f32).astype(bf16)
    heads = widened(head[:panel], 1)
    tile = panel
    for i in range(centers_ref.shape[0] // tile):
        rows = slice(i * tile, (i + 1) * tile)
        kp = similar(widened(centers_ref[rows], 0), heads, features)
        rows_ref[rows] = lax.dot_general(
            kp, mine_ref[...], LAST, preferred_element_type=f32
        ).astype(bf16)
        z = dir_ref[:, rows] - lax.dot_general(q, kp, LAST, preferred_element_type=f32)
        if i == 0:
            z = jnp.where(flags_ref[0] == 0, z1.astype(f32), z)
        z_ref[:, rows] = z
        high = z.astype(bf16)
        zz[:outputs, rows] = high
        zz[outputs:, rows] = (z - high.astype(f32)).astype(bf16)
    puts = []
    done = 0
    for block in blocks:
        for i in range(block.shape[1] // CHUNK):
            chunk = block[:, i * CHUNK : (i + 1) * CHUNK]
            u = jnp.dot(zz[...], chunk, preferred_element_type=f32)
            for b in range(CHUNK // 128):
                part = u[:, b * 128 : (b + 1) * 128]
                parts_buf[done + b] = jnp.concatenate(
                    [*pieces(part[:outputs], 2), part[outputs:].astype(bf16)], axis=0
                )
            span = pl.ds(done, CHUNK // 128)
            puts.append(
                pltpu.make_async_copy(
                    parts_buf.at[span], parts_out.at[span], out_sems.at[len(puts)]
                )
            )
            puts[-1].start()
            done += CHUNK // 128
    for put in puts:
        put.wait()


def panel_step(flags, centers, head, head_other, mine, other, pair, direction, blocks):
    outputs, m_dev = direction.shape
    share, panel = mine.shape
    features = centers.shape[1]
    count = sum(block.shape[1] for block in blocks)
    values = jax.ShapeDtypeStruct((count // 128, 3 * outputs, 128), bf16)
    return pl.pallas_call(
        functools.partial(panel_kernel, len(blocks)),
        out_shape=(
            jax.ShapeDtypeStruct((outputs, m_dev), f32),
            jax.ShapeDtypeStruct((m_dev, share), bf16),
            values,
        ),
        in_specs=[SMEM] + [VMEM] * (7 + len(blocks)),
        out_specs=(VMEM, VMEM, ANY),
        scratch_shapes=[
            pltpu.VMEM((2 * head_other.shape[0], features), bf16),
            pltpu.VMEM((panel, panel), bf16),
            pltpu.VMEM((2 * outputs, m_dev), bf16),
            pltpu.VMEM(values.shape, bf16),
            pltpu.SemaphoreType.DMA((count // CHUNK,)),
        ],
        compiler_params=pltpu.CompilerParams(vmem_limit_bytes=16 << 20),
        cost_estimate=pl.CostEstimate(
            flops=2 * 256 * m_dev * count,
            bytes_accessed=2 * m_dev * count,
            transcendentals=m_dev * panel,
        ),
        name="panel",
    )(flags, centers, head, head_other, mine, other, pair, direction, *blocks)


def image_kernel(
    flags_ref, w_ref, centers_ref, points_ref, source_ref, keep_ref, send_ref,
    blocks, made, wide, total, points_buf, sems, points_sem,
):
    stored = sems.shape[0]
    local = pltpu.make_async_copy(
        points_ref.at[pl.ds(stored * CHUNK, points_buf.shape[0])], points_buf, points_sem
    )
    local.start()
    for i in range(stored):
        chunk_copy(source_ref, blocks, sems, i).start()
    wide[...] = widened(centers_ref[...], 1)
    total[...] = jnp.zeros_like(total)
    local.wait()
    count = points_ref.shape[0] // CHUNK
    width = CHUNK // 128
    outputs, m_dev = total.shape

    def use(i, block):
        w = jnp.concatenate(
            [w_ref[i, b * outputs : (b + 1) * outputs] for b in range(width)], axis=1
        )
        total[...] += jnp.dot(w, block, preferred_element_type=f32)

    def local_step(i, carry):
        rows = pl.ds(pl.multiple_of((i - stored) * CHUNK, CHUNK), CHUNK)
        fill(1, wide, points_buf[rows], made)
        use(i, made[...])
        return carry

    def stored_step(i, carry):
        chunk_copy(source_ref, blocks, sems, i).wait()
        use(i, blocks[i])
        return carry

    lax.fori_loop(stored, count, local_step, 0)
    lax.fori_loop(0, stored, stored_step, 0)
    half = keep_ref.shape[0]
    mine = pl.multiple_of((flags_ref[1] % 2) * half, half)
    keep_ref[:, :m_dev] = total[pl.ds(mine, half)]
    send_ref[:, :m_dev] = total[pl.ds(half - mine, half)]
    scalars = jnp.broadcast_to(scalar_sum(w_ref, width * outputs), (half, 128))
    keep_ref[:, m_dev:] = scalars
    send_ref[:, m_dev:] = scalars


def image(flags, outputs, w, centers, points, block):
    m_dev, features = centers.shape
    count = points.shape[0] // CHUNK
    stored = block.shape[0]
    shape = jax.ShapeDtypeStruct((outputs // 2, m_dev + 128), f32)
    return pl.pallas_call(
        image_kernel,
        out_shape=(shape, shape),
        in_specs=[SMEM, VMEM, VMEM, ANY, ANY],
        out_specs=(VMEM, VMEM),
        scratch_shapes=[
            pltpu.VMEM(block.shape, bf16),
            pltpu.VMEM((CHUNK, m_dev), bf16),
            pltpu.VMEM((m_dev, 2 * features), bf16),
            pltpu.VMEM((outputs, m_dev), f32),
            pltpu.VMEM(((count - stored) * CHUNK, features), bf16),
            pltpu.SemaphoreType.DMA((stored,)),
            pltpu.SemaphoreType.DMA,
        ],
        compiler_params=pltpu.CompilerParams(vmem_limit_bytes=44 << 20),
        cost_estimate=pl.CostEstimate(
            flops=2 * 256 * points.shape[0] * m_dev,
            bytes_accessed=2 * points.shape[0] * m_dev,
            transcendentals=0,
        ),
        name="image",
    )(flags, w, centers, points, block)


def exchange(x, axis):
    return lax.all_to_all(x, axis, 0, 0, tiled=True)


def tree_pairs(sizes):
    n_far, n_near = sizes
    stages, holders, stride = [], [0], n_near
    while stride > 1:
        stride //= 2
        stages.append([(i, i + stride) for i in holders])
        holders = holders + [i + stride for i in holders]
    stride = n_far
    while stride > 1:
        stride //= 2
        stages.append([(i, i + stride * n_near) for i in holders])
        holders = holders + [i + stride * n_near for i in holders]
    return stages


def tree_stage(x, pairs):
    return x + lax.ppermute(x, CTR, pairs)


def swap(x, bit):
    n = lax.axis_size("pts")
    return lax.ppermute(x, "pts", [(i, i ^ bit) for i in range(n)])


def final_kernel(scale, flags_ref, keep_ref, other_ref, z_ref, res_ref, op_ref, new_ref):
    outputs, m_dev = z_ref.shape
    half = keep_ref.shape[0]
    sums = keep_ref[0:1, m_dev:]
    lane = lax.broadcasted_iota(jnp.int32, (outputs, sums.shape[1]), 1)
    row = lax.broadcasted_iota(jnp.int32, (outputs, sums.shape[1]), 0)
    curvature = jnp.sum(jnp.where(lane == row, sums, 0.0), axis=1, keepdims=True)
    squares = jnp.sum(jnp.where(lane == row + outputs, sums, 0.0), axis=1, keepdims=True)
    op_ref[...] = RIDGE_TERM * z_ref[...]
    mine = pl.multiple_of((flags_ref[1] % 2) * half, half)
    op_ref[pl.ds(mine, half)] += keep_ref[:, :m_dev] * scale
    op_ref[pl.ds(half - mine, half)] += other_ref[:, :m_dev] * scale
    new_ref[...] = res_ref[...] - (squares / curvature) * op_ref[...]


def final_step(flags, keep, other, z, residual, scale):
    shape = jax.ShapeDtypeStruct(z.shape, f32)
    return pl.pallas_call(
        functools.partial(final_kernel, scale),
        out_shape=(shape, shape),
        in_specs=[SMEM] + [VMEM] * 4,
        out_specs=(VMEM, VMEM),
        compiler_params=pltpu.CompilerParams(vmem_limit_bytes=LIMIT),
        name="final",
    )(flags, keep, other, z, residual)


def step(points, centers, panel_inverse, direction, residual):
    n_ctr = lax.axis_size(CTR)
    n_near = lax.axis_size(NEAR)
    n_far = lax.axis_size(FAR)
    n_pts = lax.axis_size("pts")
    flags = jnp.stack([lax.axis_index(CTR), lax.axis_index("pts")])
    m_dev, _ = centers.shape
    npg = points.shape[0]
    panel = panel_inverse.shape[1]
    outputs = direction.shape[0]
    w_scale = 1.0 / (2.0 * math.sqrt(m_dev * n_ctr))
    image_scale = 1.0 / (2.0 * math.sqrt(npg * n_pts))

    head = head_payload(flags, centers, direction, panel)
    wide = wide_centers(points, centers)
    by_center = []
    first = 0
    for count in (2, 3, 3):
        by_center.append(resident_part(first, count, points, wide))
        first += count
    for links in tree_pairs((n_far, n_near)):
        head = tree_stage(head, links)
    other = swap(panel_inverse, 1)
    pair = swap(jnp.concatenate([panel_inverse, other], axis=0), 2)
    z, panel_rows, parts = panel_step(
        flags, centers, head, swap(head, 1),
        panel_inverse, other, pair, direction, by_center,
    )

    rows = 3 * outputs
    parts = exchange(parts.reshape(n_near, n_far * rows, 128), NEAR)
    parts = exchange(summed(parts, rows), FAR)
    block = block_part(1, CHUNK, 6, 0, 6, points, centers)
    w = owned_copies(parts, z, residual, w_scale, image_scale, n_pts, n_far)
    w = exchange(w, FAR)
    w = exchange(relay_copies(w, n_near), NEAR)

    keep, send = image(flags, outputs, w, centers, points, block)
    keep = keep + swap(send, 1)
    keep = keep + swap(keep, 2)
    operator_image, new_residual = final_step(flags, keep, swap(keep, 1), z, residual, image_scale)
    return (panel_rows, operator_image, new_residual)


def solution(mesh):
    split = Mesh(
        mesh.devices.reshape(mesh.shape["pts"], 8, 2, 4), ("pts", "ctr_0", "ctr_1", "ctr_2")
    )
    placed = (P("pts", None), P(CTR, None), P("pts", None), P(None, CTR), P(None, CTR))
    return jax.shard_map(
        step,
        mesh=split,
        in_specs=placed,
        out_specs=(P(CTR, "pts"), P(None, CTR), P(None, CTR)),
        check_vma=False,
    )
```
